128 devices in a mesh: pair: 4 (over z), bulk: 32 (over x, y, core).
Axes of the slice: x: 4, y: 4, z: 4, core: 2. Of those that a mesh axis runs over, the one named last changes fastest.
Arguments:
- wavefield_now: float32 [512, 96, 128], P(('pair', 'bulk')), may hold values from -6 to 6
- wavefield_vel: float32 [512, 96, 128], P(('pair', 'bulk')), may hold values from -6 to 6
- speed_sq: float32 [128, 24, 32], P(('pair', 'bulk')), may hold values from 0.5 to 2
- source_field: float32 [512, 96, 128], P(('pair', 'bulk')), may hold values from -300 to 300
- wavelet: float32 [6], replicated, may hold values from -4 to 4
- slot_elem: int32 [16384], P(('pair', 'bulk')), may hold values from 0 to 767
- slot_station: int32 [16384], replicated, may hold values from 0 to 8192, as said below
- slot_weight: float32 [125, 16384], P(None, ('pair', 'bulk')), may hold values from -0.5 to 0.5
- pair_blocks: int32 [128, 2], P(('pair', 'bulk')), may hold values from 0 to 255
Outputs:
- wavefield_end: float32 [512, 96, 128], P(('pair', 'bulk'))
- cross: bfloat16 [128, 2, 256, 1024], P(('pair', 'bulk'))
The draws below stay inside these ranges and needn't reach their ends.
Inputs may be any that keep to these rules, and one draw needn't show every extreme that they name: `slot_station`: every station number 0 .. 8191 appears in exactly one slot; empty slots hold 8192. Within each device block of 128 slots the live slots come first; some device block is full in every draw. `slot_elem`: index of the slot's element within the slot block's elements. `pair_blocks`: block k holds stations k * 32 to k * 32 + 31.
All inputs are finite; a program needn't handle non-finite values.
Results may differ from the reference program's by a relative error of at most 0.0057.
Values may be sent and summed in bfloat16 or wider, within the bound.
No kernel may reach another device: no remote copies, remote signals or barrier semaphores. Data moves between devices by JAX's collectives and lax.ppermute only.
A program may use at most 128 MiB of HBM per device.

```python
import math
import jax
import jax.numpy as jnp
import numpy as np
from jax import lax

EX_DEV = 1
EY = 24
EZ = 32
NT = 6
F = 256
STA_DEV = 64
SB = 32
CAP = 128
NSTA = 8192
NSB = 256
NPAIRS = 128
EXT = 128
NX = 512
NYN = 96
NZN = 128
DEVICES = 128


def draw_slot_station(key, part):
    key_load = jax.random.fold_in(key, 11)
    key_ids = jax.random.fold_in(key, 12)
    kinds = jnp.arange(DEVICES, dtype=jnp.int32) % 4
    loads = jnp.where(kinds == 0, CAP, jnp.where(kinds == 1, STA_DEV, STA_DEV // 2)).astype(jnp.int32)
    loads = loads[jax.random.permutation(key_load, DEVICES)]
    live_slot = (jnp.arange(CAP, dtype=jnp.int32)[None, :] < loads[:, None]).reshape(-1)
    slot_rank = jnp.cumsum(live_slot.astype(jnp.int32)) - 1
    stations = jax.random.permutation(key_ids, NSTA).astype(jnp.int32)
    return jnp.where(live_slot, stations[jnp.clip(slot_rank, 0, NSTA - 1)], NSTA).astype(jnp.int32)


def set_ends(drawn, key, least, high):
    place = [jax.random.randint(jax.random.fold_in(key, axis), (), 0, length) for axis, length in enumerate(drawn.shape)]
    widest = drawn.shape.index(max(drawn.shape))
    beside = place[:widest] + [(place[widest] + 1) % drawn.shape[widest]] + place[widest + 1:]
    return drawn.at[tuple(place)].set(least).at[tuple(beside)].set(high)


def level_of(rng, extent, cuts, least, largest):
    level, own = 1.0, jax.random.fold_in(rng, 6)
    for dim, blocks in cuts:
        heights = jnp.exp(jax.random.uniform(jax.random.fold_in(own, dim), (blocks,), jnp.float32, least / len(cuts), largest / len(cuts)))
        level = level * jnp.repeat(heights, extent[dim] // blocks).reshape([-1 if axis == dim else 1 for axis in range(len(extent))])
    return level


def bell_draw(own_key, shape, deviation, reach, shards=(), held_as=jnp.bfloat16):
    gain = level_of(own_key, shape, shards, -0.22, 0.18) if shards else 1.0
    values = jax.random.normal(own_key, shape, jnp.float32) * deviation * gain
    return jnp.minimum(jnp.maximum(values, -reach), reach).astype(held_as)


def setup_inputs(seed: int = 0) -> dict:
    streams_of = jax.random.split(jax.random.key(seed), 10)
    return {
        "wavefield_now": bell_draw(streams_of[0], (NX, NYN, NZN), 1.0, 6.0, ((0, 128),), jnp.float32),
        "wavefield_vel": bell_draw(streams_of[1], (NX, NYN, NZN), 1.0, 6.0, ((0, 128),), jnp.float32),
        "speed_sq": jnp.clip(jnp.exp(math.log(2.0) - 1.3862944 * jax.random.uniform(streams_of[2], (EXT, EY, EZ), jnp.float32) ** level_of(streams_of[2], (EXT, EY, EZ), ((0, 128),), -0.2, 0.2)), 0.5, 2.0),
        "source_field": bell_draw(streams_of[3], (NX, NYN, NZN), 50.0, 300.0, ((0, 128),), jnp.float32),
        "wavelet": bell_draw(streams_of[4], (NT,), 1.0, 4.0, (), jnp.float32),
        "slot_elem": set_ends(jax.random.randint(streams_of[5], (CAP * DEVICES,), 0, EX_DEV * EY * EZ), jax.random.fold_in(streams_of[5], 1), 0, (EX_DEV * EY * EZ) - 1).astype(jnp.int32),
        "slot_station": draw_slot_station(jax.random.fold_in(streams_of[9], 71), 0),
        "slot_weight": bell_draw(streams_of[7], (125, CAP * DEVICES), 125 ** -0.5, 0.5, ((1, 128),), jnp.float32),
        "pair_blocks": set_ends(jax.random.randint(streams_of[8], (NPAIRS, 2), 0, NSB), jax.random.fold_in(streams_of[8], 1), 0, NSB - 1).astype(jnp.int32),
    }


STEP_DT = 0.04

def gll_tables():
    points = np.array([-1.0, -math.sqrt(3.0 / 7.0), 0.0, math.sqrt(3.0 / 7.0), 1.0])
    quadrature = np.array([0.1, 49.0 / 90.0, 32.0 / 45.0, 49.0 / 90.0, 0.1])
    factor = np.array([np.prod([points[row_at] - points[col_at] for col_at in range(5) if col_at != row_at]) for row_at in range(5)])
    derivative = np.zeros((5, 5))
    for row_at in range(5):
        for col_at in range(5):
            if row_at != col_at:
                derivative[row_at, col_at] = factor[row_at] / (factor[col_at] * (points[row_at] - points[col_at]))
        derivative[row_at, row_at] = -np.sum(derivative[row_at])
    return (jnp.asarray(derivative, jnp.float32), jnp.asarray(quadrature, jnp.float32))

def periodic_weights(length):
    position = jnp.arange(length) % 4
    return jnp.where(position == 0, 0.2, jnp.where(position == 2, 32.0 / 45.0, 49.0 / 90.0)).astype(jnp.float32)

def lumped_mass(planes, rows_y, depth_z):
    along_z = jnp.where(jnp.arange(depth_z) == 0, 0.1, periodic_weights(depth_z)).astype(jnp.float32)
    return periodic_weights(planes)[:, None, None] * periodic_weights(rows_y)[None, :, None] * along_z[None, None, :]

def extend(field, next_plane):
    widened = jnp.concatenate([field, next_plane], 0)
    widened = jnp.concatenate([widened, widened[:, :1]], 1)
    bottom = jnp.zeros(widened.shape[:2] + (1,), widened.dtype)
    return jnp.concatenate([widened, bottom], 2)

def split_axis(field, axis_at):
    count = (field.shape[axis_at] - 1) // 4
    shape = field.shape[:axis_at] + (count, 4) + field.shape[axis_at + 1:]
    head = lax.slice_in_dim(field, 0, 4 * count, axis=axis_at).reshape(shape)
    tail = lax.slice_in_dim(field, 4, 4 * count + 1, stride=4, axis=axis_at)
    tail = jnp.expand_dims(tail, axis_at + 1)
    return jnp.concatenate([head, tail], axis_at + 1)

def to_elements(extended):
    split = split_axis(extended, 0)
    split = split_axis(split, 2)
    split = split_axis(split, 4)
    return jnp.transpose(split, (1, 3, 5, 0, 2, 4))

def merge_axis(pieces, axis_at):
    count = pieces.shape[axis_at]
    head = lax.slice_in_dim(pieces, 0, 4, axis=axis_at + 1)
    face = lax.slice_in_dim(pieces, 4, 5, axis=axis_at + 1)
    shape = pieces.shape[:axis_at] + (4 * count,) + pieces.shape[axis_at + 2:]
    zero_shape = list(face.shape)
    zero_shape[axis_at + 1] = 3
    shifted = jnp.concatenate([face, jnp.zeros(tuple(zero_shape), pieces.dtype)], axis_at + 1).reshape(shape)
    config = [(0, 0, 0)] * len(shape)
    config[axis_at] = (0, 1, 0)
    merged = lax.pad(head.reshape(shape), jnp.zeros((), pieces.dtype), config)
    config[axis_at] = (4, -3, 0)
    return merged + lax.pad(shifted, jnp.zeros((), pieces.dtype), config)

def from_elements(pieces):
    arranged = jnp.transpose(pieces, (3, 0, 4, 1, 5, 2))
    merged = merge_axis(arranged, 4)
    merged = merge_axis(merged, 2)
    return merge_axis(merged, 0)

def stiffness(elements, speed_slab, derivative, quadrature):
    highest = lax.Precision.HIGHEST
    flat = elements.reshape(5, 5, 5, -1)
    rates = speed_slab.reshape(-1)
    cube = quadrature[:, None, None] * quadrature[None, :, None] * quadrature[None, None, :]
    scaled = cube[..., None] * rates
    grad_x = jnp.einsum('lm,mbce->lbce', derivative, flat, precision=highest)
    result = jnp.einsum('la,lbce->abce', derivative, scaled * grad_x, precision=highest)
    grad_y = jnp.einsum('lm,amce->alce', derivative, flat, precision=highest)
    result = result + jnp.einsum('lb,alce->abce', derivative, scaled * grad_y, precision=highest)
    grad_z = jnp.einsum('lm,abme->able', derivative, flat, precision=highest)
    result = result + jnp.einsum('lc,able->abce', derivative, scaled * grad_z, precision=highest)
    return result.reshape(elements.shape)

def fold_y_z(forces):
    trimmed = forces[:, :, :-1]
    width_y = trimmed.shape[1] - 1
    return jnp.concatenate([trimmed[:, :1] + trimmed[:, width_y:], trimmed[:, 1:width_y]], 1)

def sample_slots(elements, elem_slab, weight_slab):
    flat = elements.reshape(125, -1)
    picked = jnp.take(flat, elem_slab, axis=1)
    return lax.optimization_barrier(jnp.sum(picked * weight_slab, 0))

def dft_tables(freqs, steps):
    angle = jnp.pi * (jnp.arange(freqs, dtype=jnp.float32) + 0.5) / freqs
    phase = angle[:, None] * jnp.arange(steps, dtype=jnp.float32)[None, :]
    return (jnp.cos(phase), -jnp.sin(phase))

def reference(wavefield_now, wavefield_vel, speed_sq, source_field, wavelet, slot_elem, slot_station, slot_weight, pair_blocks):
    derivative, quadrature = gll_tables()
    planes = 4 * EX_DEV
    mass = lumped_mass(NX, NYN, NZN)
    field_now = wavefield_now
    field_prev = wavefield_now - STEP_DT * wavefield_vel
    speed_slabs = speed_sq.reshape(DEVICES, EX_DEV, EY, EZ)
    elem_slabs = slot_elem.reshape(DEVICES, CAP)
    weight_slabs = slot_weight.reshape(125, DEVICES, CAP).transpose(1, 0, 2)

    def per_slab(inputs):
        slab_field, next_plane, speed_slab, elem_slab, weight_slab = inputs
        elements = to_elements(extend(slab_field, next_plane))
        forces = fold_y_z(from_elements(stiffness(elements, speed_slab, derivative, quadrature)))
        return (forces, sample_slots(elements, elem_slab, weight_slab))
    records = []
    for moment in range(NT):
        slabs = field_now.reshape(DEVICES, planes, NYN, NZN)
        next_planes = jnp.roll(slabs[:, :1], -1, axis=0)
        forces, samples = lax.map(per_slab, (slabs, next_planes, speed_slabs, elem_slabs, weight_slabs))
        back = jnp.roll(forces[:, planes:], 1, axis=0)
        assembled = jnp.concatenate([forces[:, :1] + back, forces[:, 1:planes]], 1).reshape(NX, NYN, NZN)
        accel = wavelet[moment] * source_field - assembled / mass
        field_next = 2.0 * field_now - field_prev + STEP_DT * STEP_DT * accel
        records.append(samples.reshape(-1))
        field_prev = field_now
        field_now = field_next
    samples_all = jnp.stack(records, 0)
    cos_table, sin_table = dft_tables(F, NT)
    highest = lax.Precision.HIGHEST
    real_part = jnp.dot(cos_table, samples_all, precision=highest, preferred_element_type=jnp.float32)
    imag_part = jnp.dot(sin_table, samples_all, precision=highest, preferred_element_type=jnp.float32)
    spectra = jnp.concatenate([real_part, imag_part], 0).astype(jnp.bfloat16)
    slot_count = DEVICES * CAP
    position = jnp.zeros((NSTA + 1,), jnp.int32).at[slot_station].set(jnp.arange(slot_count, dtype=jnp.int32))
    by_station = jnp.take(spectra, position[:NSTA], axis=1).astype(jnp.float32).reshape(2, F, NSB, SB)

    def one_pair(blocks):
        first_block = jnp.take(by_station, blocks[0], axis=2)
        second_block = jnp.take(by_station, blocks[1], axis=2)
        cross_re = (first_block[0][:, :, None] * second_block[0][:, None, :] + first_block[1][:, :, None] * second_block[1][:, None, :]) / NT
        cross_im = (first_block[1][:, :, None] * second_block[0][:, None, :] - first_block[0][:, :, None] * second_block[1][:, None, :]) / NT
        return jnp.stack([cross_re, cross_im], 0).reshape(2, F, SB * SB).astype(jnp.bfloat16)
    cross = lax.map(one_pair, pair_blocks)
    return (field_now, cross)
```

```python
import functools
import math

import jax
import jax.numpy as jnp
import numpy as np
from jax import lax
from jax.experimental import pallas as pl
from jax.experimental.pallas import tpu as pltpu
from jax.sharding import PartitionSpec as P

NT = 6
F = 256
SB = 32
STEP_DT = 0.04
NY = 96
NZ = 128
EY = 24
EZ = 32
CAP = 128
AXES = ("pair", "bulk")
HIGHEST = lax.Precision.HIGHEST
W1 = np.array([0.1, 49.0 / 90.0, 32.0 / 45.0, 49.0 / 90.0, 0.1])


def stiffness_1d():
    points = np.array([-1.0, -math.sqrt(3.0 / 7.0), 0.0, math.sqrt(3.0 / 7.0), 1.0])
    factor = np.array(
        [np.prod([points[i] - points[j] for j in range(5) if j != i]) for i in range(5)]
    )
    d = np.zeros((5, 5))
    for i in range(5):
        for j in range(5):
            if i != j:
                d[i, j] = factor[i] / (factor[j] * (points[i] - points[j]))
        d[i, i] = -np.sum(d[i])
    return d.T @ np.diag(W1) @ d


A = stiffness_1d()
MX = np.array([0.2, W1[1], W1[2], W1[3], 0.2])
AB = A / MX[:, None]
KAPPA = float(sum(AB[4, k] * AB[k, 4] for k in range(4)))


def f32(x):
    return np.asarray(x, np.float32)


def tables():
    my = np.array([MX[y % 4] for y in range(NY)])
    mz = np.array([0.1 if z == 0 else MX[z % 4] for z in range(NZ)])
    mat_z = np.zeros((NZ, 2 * NZ))
    for z in range(NZ):
        e, c = divmod(z, 4)
        for m in range(5):
            if 4 * e + m < NZ:
                mat_z[4 * e + m, z] += A[c, m]
            if c == 0 and e > 0:
                mat_z[4 * (e - 1) + m, NZ + z] += A[4, m]
    mat_y = np.zeros((2 * NY, NY))
    for y in range(NY):
        e, b = divmod(y, 4)
        for m in range(5):
            mat_y[y, (4 * e + m) % NY] += A[b, m]
            if b == 0:
                mat_y[NY + y, (4 * (e - 1) + m) % NY] += A[4, m]
    left = np.zeros((3 * NY, EY))
    for y in range(NY):
        e, b = divmod(y, 4)
        left[y, e] += W1[b]
        left[NY + y, e] += 1.0
        if b == 0:
            left[y, (e - 1) % EY] += W1[4]
            left[2 * NY + y, (e - 1) % EY] += 1.0
    left = left / np.tile(my, 3)[:, None]
    right = np.zeros((EZ, 3 * NZ))
    for z in range(NZ):
        e, c = divmod(z, 4)
        right[e, z] += 1.0
        right[e, 2 * NZ + z] += W1[c]
        if c == 0 and e > 0:
            right[e - 1, NZ + z] += 1.0
            right[e - 1, 2 * NZ + z] += W1[4]
    right = right / np.tile(mz, 3)[None, :] * (STEP_DT * STEP_DT)
    left_pad = np.zeros((3 * NY, 128))
    left_pad[:, :EY] = left
    right_pad = np.zeros((128, 3 * NZ))
    right_pad[:EZ] = right
    return f32(mat_z), f32(mat_y), f32(left_pad[:, :EY]), f32(right_pad)


def dft_table():
    angle = np.pi * (np.arange(F) + 0.5) / F
    phase = angle[:, None] * np.arange(NT)[None, :]
    table = np.zeros((2 * F, 128))
    table[:F, :NT] = np.cos(phase)
    table[F:, :NT] = -np.sin(phase)
    return f32(table)


def dot(a, b):
    return jnp.dot(a, b, precision=HIGHEST, preferred_element_type=jnp.float32)


VMEM = pl.BlockSpec(memory_space=pltpu.VMEM)
SMEM = pl.BlockSpec(memory_space=pltpu.SMEM)


def call(kernel, outs, args, name, smem=0, flops=4_000_000, nbytes=1_000_000):
    return pl.pallas_call(
        kernel,
        out_shape=[jax.ShapeDtypeStruct(s, d) for s, d in outs],
        in_specs=[SMEM] * smem + [VMEM] * (len(args) - smem),
        out_specs=[VMEM] * len(outs),
        compiler_params=pltpu.CompilerParams(vmem_limit_bytes=24 * 1024 * 1024),
        cost_estimate=pl.CostEstimate(flops=flops, bytes_accessed=nbytes, transcendentals=0),
        name=name,
    )(*args)


PLANE = (NY, NZ)
FOUR = (4, NY, NZ)
FIVE = (5, NY, NZ)
FP = jnp.float32


def expand_speed(speed, left, right):
    rows = dot(left, speed)
    by_z = dot(rows[:NY], right)
    by_y = dot(rows[NY:], right[:, 2 * NZ :])
    return by_z[:, :NZ], by_z[:, NZ : 2 * NZ], by_y[:NY], by_y[NY:], by_z[:, 2 * NZ :]


def lateral(plane_z, plane_y, coefs):
    return (
        coefs[0] * plane_z[:, :NZ]
        + coefs[1] * plane_z[:, NZ:]
        + coefs[2] * plane_y[:NY]
        + coefs[3] * plane_y[NY:]
    )


def to_right(sx, u):
    total = float(AB[4, 0]) * u[0]
    for m in range(1, 4):
        total = total + float(AB[4, m]) * u[m]
    return sx * total


def start_kernel(par, now, speed, left, right, coef_ref, first_ref, msg_ref):
    coefs = expand_speed(speed[...], left[...], right[...])
    for i in range(5):
        coef_ref[i] = coefs[i]
    g = to_right(coefs[4], [now[k] for k in range(4)])
    first_ref[...] = g
    msg_ref[:NY] = jnp.where(par[0] == 1, now[0], g)
    msg_ref[NY:] = speed[...]


def base_first_kernel(wave, now, vel, src, coef, mat_z, mat_y, out):
    base_body(0, wave, now, None, vel, src, coef, None, mat_z, mat_y, out)


def base_body(step, wave, now, prev, vel, src, coef, coef0, mat_z, mat_y, out):
    scale = wave[step] * (STEP_DT * STEP_DT)
    sx = coef[4]
    for k in range(4):
        u = now[k]
        pz = dot(u, mat_z[...])
        py = dot(mat_y[...], u)
        if k == 0:
            if coef0 is None:
                force = 0.5 * lateral(pz, py, [coef[i] for i in range(4)])
            else:
                force = lateral(pz, py, [coef0[i] for i in range(4)]) + coef0[4] * u
        else:
            force = lateral(pz, py, [coef[i] for i in range(4)])
        mix = float(AB[k, 0]) * now[0]
        for m in range(1, 4):
            mix = mix + float(AB[k, m]) * now[m]
        force = force + sx * mix
        if prev is None:
            out[k] = u + STEP_DT * vel[k] + (scale * src[k] - force)
        else:
            out[k] = 2.0 * u - prev[k] + (scale * src[k] - force)


def base_kernel(step, wave, now, prev, src, coef, coef0, mat_z, mat_y, out):
    base_body(step, wave, now, prev, None, src, coef, coef0, mat_z, mat_y, out)


def half_left(plane, coefs, mat_z, mat_y):
    pz = dot(plane, mat_z)
    py = dot(mat_y, plane)
    return 0.5 * lateral(pz, py, coefs) + float(AB[4, 4]) * (coefs[4] * plane)


def inner_first_kernel(
    par, base, now, first, recv, speed, coef, left, right, mat_z, mat_y, tent_ref, msg_ref, cleft_ref
):
    odd = par[0] == 1
    coefs = expand_speed(jnp.where(odd, recv[NY:], 0.0), left[...], right[...])
    for i in range(5):
        cleft_ref[i] = coefs[i]
    share = half_left(now[0], coefs, mat_z[...], mat_y[...])
    inner_finish(odd, base, now, first[...], recv[:NY], coef[4], share, tent_ref, msg_ref)
    msg_ref[2 * NY :] = speed[...]


def inner_finish(odd, base, now, g_now, inner, sx, share, tent_ref, msg_ref):
    even_part = jnp.where(odd, 0.0, sx * inner)
    tent = []
    for k in range(4):
        value = base[k] - float(AB[k, 4]) * even_part
        if k == 0:
            value = value - jnp.where(odd, inner, 0.0)
            if share is not None:
                value = value - share
        tent_ref[k] = value
        tent.append(value)
    msg_ref[:NY] = jnp.where(odd, g_now, now[0])
    msg_ref[NY : 2 * NY] = jnp.where(odd, to_right(sx, tent), tent[0])


def inner_kernel(par, base, now, g_now, recv, coef, tent_ref, msg_ref):
    odd = par[0] == 1
    inner_finish(odd, base, now, g_now[...], recv[...], coef[4], None, tent_ref, msg_ref)


def outer_finish(odd, tent, sx, sx_left, recv0, recv1, g_own, u0_own, share, refs):
    u_ref, msg_ref, outer_ref = refs
    odd_part = jnp.where(odd, sx * recv0, 0.0)
    values = []
    for k in range(4):
        value = tent[k] - float(AB[k, 4]) * odd_part
        if k == 0:
            lost = recv0 if share is None else recv0 + share
            value = value - jnp.where(odd, 0.0, lost)
        u_ref[k] = value
        values.append(value)
    msg_ref[...] = jnp.where(odd, values[0], to_right(sx, values))
    mine = g_own if share is None else g_own + share
    outer_ref[...] = recv1 - jnp.where(odd, mine, KAPPA * sx_left * sx_left * u0_own)


def outer_first_kernel(
    par, tent, now, first, recv, inner, coef, cleft, left, right, mat_z, mat_y,
    u_ref, msg_ref, outer_ref, coef0_ref, sxl_ref, last_ref,
):
    odd = par[0] == 1
    theirs = expand_speed(recv[2 * NY :], left[...], right[...])
    coefs = [jnp.where(odd, coef[i], theirs[i]) for i in range(5)]
    recv0 = recv[:NY]
    plane = jnp.where(odd, recv0, now[0])
    share = half_left(plane, coefs, mat_z[...], mat_y[...])
    on_left = [jnp.where(odd, cleft[i], theirs[i]) for i in range(5)]
    for i in range(4):
        coef0_ref[i] = 0.5 * (coef[i] + on_left[i])
    coef0_ref[4] = float(AB[4, 4]) * on_left[4]
    sxl_ref[...] = on_left[4]
    last_ref[...] = jnp.where(odd, recv0, inner[:NY])
    outer_finish(
        odd, tent, coef[4], on_left[4], recv0, recv[NY : 2 * NY], first[...], now[0], share,
        (u_ref, msg_ref, outer_ref),
    )


def outer_kernel(par, tent, now, g_now, recv, inner, coef, sxl, u_ref, msg_ref, outer_ref, last_ref):
    odd = par[0] == 1
    recv0 = recv[:NY]
    last_ref[...] = jnp.where(odd, recv0, inner[...])
    outer_finish(
        odd, tent, coef[4], sxl[...], recv0, recv[NY:], g_now[...], now[0], None,
        (u_ref, msg_ref, outer_ref),
    )


def both_kernel(par, base, inner, outer, coef, u_ref, g_ref, msg_ref, last_ref):
    odd = par[0] == 1
    last = jnp.where(odd, outer[...], inner[...])
    from_left = jnp.where(odd, inner[...], outer[...])
    sx = coef[4]
    pull = sx * last
    values = []
    for k in range(4):
        value = base[k] - float(AB[k, 4]) * pull
        if k == 0:
            value = value - from_left
        u_ref[k] = value
        values.append(value)
    g = to_right(sx, values)
    g_ref[...] = g
    msg_ref[...] = jnp.where(odd, values[0], g)
    last_ref[...] = last


def slots_kernel(elem, weight, pick_ref, spread_ref):
    e = elem[...]
    ey = e // EZ
    ez = e - ey * EZ
    z = lax.broadcasted_iota(jnp.int32, (NZ, CAP), 0)
    for c in range(5):
        hot = (z == 4 * ez + c).astype(FP).astype(jnp.bfloat16)
        for half in range(2):
            pick_ref[half * NZ : (half + 1) * NZ, c * CAP : (c + 1) * CAP] = hot
    y = lax.broadcasted_iota(jnp.int32, (NY, CAP), 0)
    masks = []
    for b in range(5):
        row = 4 * ey + b
        row = jnp.where(row >= NY, row - NY, row)
        masks.append(y == row)
    for a in range(5):
        for c in range(5):
            total = jnp.zeros((NY, CAP), FP)
            for b in range(5):
                at = 25 * a + 5 * b + c
                total = jnp.where(masks[b], weight[at : at + 1, :], total)
            spread_ref[c, a * NY : (a + 1) * NY, :] = total


def sample(u, last, pick, spread):
    acc = jnp.zeros((8, CAP), FP)
    for a in range(5):
        plane = last[...] if a == 4 else u[a]
        high = plane.astype(jnp.bfloat16)
        low = (plane - high.astype(FP)).astype(jnp.bfloat16)
        got = jnp.dot(
            jnp.concatenate([high, low], 1), pick[...], preferred_element_type=jnp.float32
        )
        for c in range(5):
            part = got[:, c * CAP : (c + 1) * CAP] * spread[c, a * NY : (a + 1) * NY, :]
            acc = acc + jnp.sum(part.reshape(NY // 8, 8, CAP), 0)
    return jnp.sum(acc, 0, keepdims=True)


def sample_two_kernel(u0, l0, u1, l1, pick, spread, out):
    out[0:1, :] = sample(u0, l0, pick, spread)
    out[1:2, :] = sample(u1, l1, pick, spread)


def sample_one_kernel(u0, l0, pick, spread, out):
    out[...] = sample(u0, l0, pick, spread)


def stations_kernel(blocks, stations, row_ref, lane_ref):
    lanes = []
    for j in range(2 * SB):
        wanted = blocks[0, j // SB] * SB + j % SB
        hit = jnp.zeros((8, CAP), FP)
        for r in range(16):
            hit = hit + jnp.where(stations[8 * r : 8 * r + 8, :] == wanted, 1.0, 0.0)
        lane_ref[j : j + 1, :] = jnp.sum(hit, 0, keepdims=True)
    lane = lane_ref[...]
    ids = stations[...].astype(FP)
    at = lax.dot_general(
        lane, ids, (((1,), (1,)), ((), ())), precision=HIGHEST, preferred_element_type=jnp.float32
    )
    j = lax.broadcasted_iota(jnp.int32, (2 * SB, 128), 0)
    wanted = jnp.where(j < SB, blocks[0, 0] * SB + j, blocks[0, 1] * SB + (j - SB))
    row_ref[...] = jnp.where(jnp.abs(at - wanted.astype(FP)) < 0.5, 1.0, 0.0)


def cross_kernel(gathered, row, lane, table, spread_a, spread_b, out):
    t_of = lax.broadcasted_iota(jnp.int32, (2 * SB, 128), 1)
    samples = jnp.zeros((2 * SB, 128), FP)
    for t in range(NT):
        slab = gathered[pl.ds(t, 128, stride=8), :]
        found = dot(row[...], slab) * lane[...]
        samples = jnp.where(t_of == t, jnp.sum(found, 1, keepdims=True), samples)
    spectra = lax.dot_general(
        table[...], samples, (((1,), (1,)), ((), ())), precision=HIGHEST,
        preferred_element_type=jnp.float32,
    ).astype(jnp.bfloat16)
    second = jnp.dot(spectra, spread_b[...], preferred_element_type=jnp.float32) * (1.0 / NT)
    b_re = second[:F]
    b_im = second[F:]
    for i in range(8):
        cols = slice(128 * i, 128 * (i + 1))
        first = jnp.dot(spectra, spread_a[:, cols], preferred_element_type=jnp.float32)
        a_re = first[:F]
        a_im = first[F:]
        out[0, 0, :, cols] = (a_re * b_re + a_im * b_im).astype(jnp.bfloat16)
        out[0, 1, :, cols] = (a_im * b_re - a_re * b_im).astype(jnp.bfloat16)


def body(
    now, vel, speed_sq, src, wavelet, slot_elem, slot_station, slot_weight, pair_blocks, devices
):
    inner_route = [(i, i ^ 1) for i in range(devices)]
    outer_route = [(i, (i + 1 if i % 2 else i - 1) % devices) for i in range(devices)]

    def swap_inner(x):
        return lax.ppermute(x, AXES, inner_route)

    def swap_outer(x):
        return lax.ppermute(x, AXES, outer_route)

    mat_z, mat_y, left, right = (jnp.asarray(x) for x in tables())
    table = jnp.asarray(dft_table())
    reps = np.zeros((2 * SB, SB * SB))
    for i in range(SB):
        reps[i, i * SB : (i + 1) * SB] = 1.0
    tiles = np.zeros((2 * SB, 128))
    for i in range(128):
        tiles[SB + i % SB, i] = 1.0
    reps = jnp.asarray(reps, jnp.bfloat16)
    tiles = jnp.asarray(tiles, jnp.bfloat16)

    par = (lax.axis_index("bulk") % 2).astype(jnp.int32).reshape(1)
    speed = jnp.pad(speed_sq[0], ((0, 0), (0, 128 - EZ)))

    coef, g0, msg = call(
        start_kernel, [(FIVE, FP), (PLANE, FP), ((NY + EY, NZ), FP)], (par, now, speed, left, right),
        "start", 1,
    )
    inner0 = swap_inner(msg)
    (base,) = call(
        base_first_kernel, [(FOUR, FP)], (wavelet, now, vel, src, coef, mat_z, mat_y), "base0", 1
    )
    tent, msg, cleft = call(
        inner_first_kernel, [(FOUR, FP), ((2 * NY + EY, NZ), FP), (FIVE, FP)],
        (par, base, now, g0, inner0, speed, coef, left, right, mat_z, mat_y), "inner0", 1,
    )
    outer0 = swap_outer(msg)
    pick, spread = call(
        slots_kernel, [((2 * NZ, 5 * CAP), jnp.bfloat16), ((5, 5 * NY, CAP), FP)],
        (slot_elem.reshape(1, CAP), slot_weight), "slots",
    )
    row, lane = call(
        stations_kernel, [((2 * SB, 128), FP), ((2 * SB, CAP), FP)],
        (pair_blocks, slot_station.reshape(128, CAP)), "stations", 1,
    )
    u_a = now
    u_b, msg, outer, coef0, sxl, last_a = call(
        outer_first_kernel,
        [(FOUR, FP), (PLANE, FP), (PLANE, FP), (FIVE, FP), (PLANE, FP), (PLANE, FP)],
        (par, tent, now, g0, outer0, inner0, coef, cleft, left, right, mat_z, mat_y), "outer0", 1,
    )
    rows = []
    step = 1
    while True:
        inner = swap_inner(msg)
        (base,) = call(
            functools.partial(base_kernel, step), [(FOUR, FP)],
            (wavelet, u_b, u_a, src, coef, coef0, mat_z, mat_y), "base", 1,
        )
        u_c, g_c, msg, last_b = call(
            both_kernel, [(FOUR, FP), (PLANE, FP), (PLANE, FP), (PLANE, FP)],
            (par, base, inner, outer, coef), "both", 1,
        )
        if step == NT - 1:
            break
        inner = swap_inner(msg)
        (base,) = call(
            functools.partial(base_kernel, step + 1), [(FOUR, FP)],
            (wavelet, u_c, u_b, src, coef, coef0, mat_z, mat_y), "base", 1,
        )
        tent, msg = call(
            inner_kernel, [(FOUR, FP), ((2 * NY, NZ), FP)],
            (par, base, u_c, g_c, inner, coef), "inner", 1,
        )
        recv = swap_outer(msg)
        (two,) = call(
            sample_two_kernel, [((2, CAP), FP)], (u_a, last_a, u_b, last_b, pick, spread), "sample2"
        )
        rows.append(two)
        u_a = u_c
        u_b, msg, outer, last_a = call(
            outer_kernel, [(FOUR, FP), (PLANE, FP), (PLANE, FP), (PLANE, FP)],
            (par, tent, u_c, g_c, recv, inner, coef, sxl), "outer", 1,
        )
        step += 2
    (one,) = call(sample_one_kernel, [((1, CAP), FP)], (u_a, last_a, pick, spread), "sample")
    rows.append(one)
    (one,) = call(sample_one_kernel, [((1, CAP), FP)], (u_b, last_b, pick, spread), "sample")
    rows.append(one)
    mine = jnp.pad(jnp.concatenate(rows, 0), ((0, 2), (0, 0)))
    gathered = lax.all_to_all(
        jnp.broadcast_to(mine[None], (devices, 8, CAP)), AXES, 0, 0, tiled=True
    )
    (cross,) = call(
        cross_kernel, [((1, 2, F, SB * SB), jnp.bfloat16)],
        (gathered.reshape(8 * devices, CAP), row, lane, table, reps, tiles), "cross",
    )
    return u_c, cross


def solution(mesh):
    split = P(AXES)
    in_specs = (
        P(AXES, None, None), P(AXES, None, None), P(AXES, None, None), P(AXES, None, None),
        P(), split, P(), P(None, AXES), P(AXES, None),
    )
    out_specs = (P(AXES, None, None), P(AXES, None, None, None))
    devices = math.prod(mesh.shape.values())
    run = functools.partial(body, devices=devices)
    return jax.shard_map(run, mesh=mesh, in_specs=in_specs, out_specs=out_specs, check_vma=False)
```

```python
import functools
import math

import jax
import jax.numpy as jnp
import numpy as np
from jax import lax
from jax.experimental import pallas as pl
from jax.experimental.pallas import tpu as pltpu
from jax.sharding import PartitionSpec as P

NT = 6
F = 256
SB = 32
STEP_DT = 0.04
NY = 96
NZ = 128
EY = 24
EZ = 32
CAP = 128
AXES = ("pair", "bulk")
HIGHEST = lax.Precision.HIGHEST
W1 = np.array([0.1, 49.0 / 90.0, 32.0 / 45.0, 49.0 / 90.0, 0.1])


def stiffness_1d():
    points = np.array([-1.0, -math.sqrt(3.0 / 7.0), 0.0, math.sqrt(3.0 / 7.0), 1.0])
    factor = np.array(
        [np.prod([points[i] - points[j] for j in range(5) if j != i]) for i in range(5)]
    )
    d = np.zeros((5, 5))
    for i in range(5):
        for j in range(5):
            if i != j:
                d[i, j] = factor[i] / (factor[j] * (points[i] - points[j]))
        d[i, i] = -np.sum(d[i])
    return d.T @ np.diag(W1) @ d


A = stiffness_1d()
MX = np.array([0.2, W1[1], W1[2], W1[3], 0.2])
AB = A / MX[:, None]
KAPPA = float(sum(AB[4, k] * AB[k, 4] for k in range(4)))


def f32(x):
    return np.asarray(x, np.float32)


def tables():
    my = np.array([MX[y % 4] for y in range(NY)])
    mz = np.array([0.1 if z == 0 else MX[z % 4] for z in range(NZ)])
    mat_z = np.zeros((NZ, 2 * NZ))
    for z in range(NZ):
        e, c = divmod(z, 4)
        for m in range(5):
            if 4 * e + m < NZ:
                mat_z[4 * e + m, z] += A[c, m]
            if c == 0 and e > 0:
                mat_z[4 * (e - 1) + m, NZ + z] += A[4, m]
    left = np.zeros((3 * NY, EY))
    for y in range(NY):
        e, b = divmod(y, 4)
        left[y, e] += W1[b]
        left[NY + y, e] += 1.0
        if b == 0:
            left[y, (e - 1) % EY] += W1[4]
            left[2 * NY + y, (e - 1) % EY] += 1.0
    left = left / np.tile(my, 3)[:, None]
    right = np.zeros((EZ, 3 * NZ))
    for z in range(NZ):
        e, c = divmod(z, 4)
        right[e, z] += 1.0
        right[e, 2 * NZ + z] += W1[c]
        if c == 0 and e > 0:
            right[e - 1, NZ + z] += 1.0
            right[e - 1, 2 * NZ + z] += W1[4]
    right = right / np.tile(mz, 3)[None, :] * (STEP_DT * STEP_DT)
    high = mat_z.astype(jnp.bfloat16).astype(np.float64)
    low = (mat_z - high).astype(jnp.bfloat16)
    stack = np.concatenate([mat_z, mat_z], 0).astype(jnp.bfloat16)
    return np.concatenate([stack, low], 0), f32(left), f32(right)


PART_PAIRS = ((0, 0), (1, 0), (0, 1), (1, 1), (2, 0), (0, 2))


def parts_of(x, count):
    parts = []
    for _ in range(count):
        part = x.astype(jnp.bfloat16)
        parts.append(part)
        x = x - part.astype(x.dtype)
    return parts


def dft_table():
    angle = np.pi * (np.arange(F) + 0.5) / F
    phase = angle[:, None] * np.arange(NT)[None, :]
    parts = parts_of(f32(np.concatenate([np.cos(phase), -np.sin(phase)], 0)), 3)
    table = np.zeros((2 * F, 128), jnp.bfloat16)
    for group, (_, part) in enumerate(PART_PAIRS):
        table[:, 8 * group : 8 * group + NT] = parts[part]
    return table


def dot(a, b):
    return jnp.dot(a, b, precision=HIGHEST, preferred_element_type=jnp.float32)


VMEM = pl.BlockSpec(memory_space=pltpu.VMEM)
SMEM = pl.BlockSpec(memory_space=pltpu.SMEM)
HBM = pl.BlockSpec(memory_space=pltpu.HBM)


def call(kernel, outs, args, name, smem=0, specs=None, out_specs=None, scratch=(), flops=4_000_000):
    return pl.pallas_call(
        kernel,
        out_shape=[jax.ShapeDtypeStruct(s, d) for s, d in outs],
        in_specs=specs or [SMEM] * smem + [VMEM] * (len(args) - smem),
        out_specs=out_specs or [VMEM] * len(outs),
        scratch_shapes=list(scratch),
        compiler_params=pltpu.CompilerParams(vmem_limit_bytes=24 * 1024 * 1024),
        cost_estimate=pl.CostEstimate(flops=flops, bytes_accessed=1_000_000, transcendentals=0),
        name=name,
    )(*args)


def in_hbm(x):
    return pltpu.with_memory_space_constraint(x, pltpu.HBM)


PLANE = (NY, NZ)
FOUR = (4, NY, NZ)
FIVE = (5, NY, NZ)
FP = jnp.float32


def expand_speed(speed, left, right):
    rows = dot(left, speed)
    by_z = dot(rows[:NY], right)
    by_y = dot(rows[NY:], right[:, 2 * NZ :])
    return by_z[:, :NZ], by_z[:, NZ : 2 * NZ], by_y[:NY], by_y[NY:], by_z[:, 2 * NZ :]


def along_z(u, mat_z):
    high, low = parts_of(u, 2)
    return jnp.dot(
        jnp.concatenate([high, low], 1), mat_z[: 2 * NZ], preferred_element_type=jnp.float32
    ) + jnp.dot(high, mat_z[2 * NZ :], preferred_element_type=jnp.float32)


def y_patterns():
    b = lax.broadcasted_iota(jnp.int32, (8, NZ), 0) % 4
    own, before = {}, {}
    for d in range(-4, 5):
        total = jnp.zeros((8, NZ), FP)
        for row in range(4):
            if 0 <= row + d <= 4:
                total = jnp.where(b == row, float(A[row, row + d]), total)
        own[d] = total
        if d <= 0:
            before[d] = jnp.where(b == 0, float(A[4, 4 + d]), 0.0)
    return own, before


def y_coefs(y1, y2, patterns):
    own, before = patterns
    return {d: y1 * own[d] + y2 * before[d] if d in before else y1 * own[d] for d in own}


def wrap_rows(pad, at, plane):
    pad[at, 8 : 8 + NY, :] = plane
    pad[at, 4:8, :] = plane[NY - 4 :]
    pad[at, 8 + NY : 12 + NY, :] = plane[:4]


def along_y(pad, at, row, coefs):
    total = None
    for d, c in coefs.items():
        term = c * pad[at, 8 + row + d : 16 + row + d, :]
        total = term if total is None else total + term
    return total


def to_right(sx, u):
    total = float(AB[4, 0]) * u[0]
    for m in range(1, 4):
        total = total + float(AB[4, m]) * u[m]
    return sx * total


def start_kernel(
    par, now_in, vel_in, src_in, speed_in, left_in, right_in, mat_in,
    now, vel, src, speed, left, right, mat, coef_ref, first_ref, msg_ref, sems,
):
    pairs = (
        (speed_in.at[0], speed), (left_in, left), (right_in, right), (now_in, now), (vel_in, vel),
        (src_in, src), (mat_in, mat),
    )
    copies = [pltpu.make_async_copy(a, b, sems.at[i]) for i, (a, b) in enumerate(pairs)]
    for copy in copies:
        copy.start()
    for copy in copies[:3]:
        copy.wait()
    coefs = expand_speed(speed[...], left[...], right[...])
    for i in range(5):
        coef_ref[i] = coefs[i]
    msg_ref[NY:] = jnp.zeros((EY, NZ), FP)
    msg_ref[NY:, :EZ] = speed[...]
    copies[3].wait()
    g = to_right(coefs[4], [now[k] for k in range(4)])
    first_ref[...] = g
    msg_ref[:NY] = jnp.where(par[0] == 1, now[0], g)
    for copy in copies[4:]:
        copy.wait()


def base_first_kernel(wave, now, vel, src, coef, mat_z, out, pad):
    base_body(0, wave, now, None, vel, src, coef, None, mat_z, out, pad)


def base_body(step, wave, now, prev, vel, src, coef, coef0, mat_z, out, pad):
    scale = wave[step] * (STEP_DT * STEP_DT)
    by_z = along_z(now[...].reshape(4 * NY, NZ), mat_z)
    patterns = y_patterns()
    for k in range(4):
        wrap_rows(pad, k, now[k])
    for row in range(0, NY, 8):
        at = slice(row, row + 8)
        u = [now[k, at, :] for k in range(4)]
        sx = coef[4, at, :]
        own = [coef[i, at, :] for i in range(4)]
        first = own if coef0 is None else [coef0[i, at, :] for i in range(4)]
        cy = y_coefs(own[2], own[3], patterns)
        cy0 = cy if coef0 is None else y_coefs(first[2], first[3], patterns)
        for k in range(4):
            c = own if k else first
            z = by_z[NY * k + row : NY * k + row + 8]
            force = c[0] * z[:, :NZ] + c[1] * z[:, NZ:] + along_y(pad, k, row, cy if k else cy0)
            if k == 0:
                force = 0.5 * force if coef0 is None else force + coef0[4, at, :] * u[0]
            mix = float(AB[k, 0]) * u[0]
            for m in range(1, 4):
                mix = mix + float(AB[k, m]) * u[m]
            force = scale * src[k, at, :] - (force + sx * mix)
            if prev is None:
                out[k, at, :] = u[k] + STEP_DT * vel[k, at, :] + force
            else:
                out[k, at, :] = 2.0 * u[k] - prev[k, at, :] + force


def base_kernel(step, wave, now, prev, src, coef, coef0, mat_z, out, pad):
    base_body(step, wave, now, prev, None, src, coef, coef0, mat_z, out, pad)


def half_left(plane, coefs, mat_z, pad):
    by_z = along_z(plane, mat_z)
    wrap_rows(pad, 0, plane)
    patterns = y_patterns()
    tiles = []
    for row in range(0, NY, 8):
        c = [x[row : row + 8] for x in coefs]
        by_y = along_y(pad, 0, row, y_coefs(c[2], c[3], patterns))
        z = by_z[row : row + 8]
        tiles.append(0.5 * (c[0] * z[:, :NZ] + c[1] * z[:, NZ:] + by_y))
    return jnp.concatenate(tiles, 0) + float(AB[4, 4]) * (coefs[4] * plane)


def inner_first_kernel(
    par, base, now, first, recv, speed, coef, left, right, mat_z, tent_ref, msg_ref, cleft_ref, pad
):
    odd = par[0] == 1
    coefs = expand_speed(jnp.where(odd, recv[NY:, :EZ], 0.0), left[...], right[...])
    for i in range(5):
        cleft_ref[i] = coefs[i]
    share = half_left(now[0], coefs, mat_z, pad)
    inner_finish(odd, base, now, first[...], recv[:NY], coef[4], share, tent_ref, msg_ref)
    msg_ref[2 * NY :] = jnp.zeros((EY, NZ), FP)
    msg_ref[2 * NY :, :EZ] = speed[...]


def inner_finish(odd, base, now, g_now, inner, sx, share, tent_ref, msg_ref):
    even_part = jnp.where(odd, 0.0, sx * inner)
    tent = []
    for k in range(4):
        value = base[k] - float(AB[k, 4]) * even_part
        if k == 0:
            value = value - jnp.where(odd, inner, 0.0)
            if share is not None:
                value = value - share
        tent_ref[k] = value
        tent.append(value)
    msg_ref[:NY] = jnp.where(odd, g_now, now[0])
    msg_ref[NY : 2 * NY] = jnp.where(odd, to_right(sx, tent), tent[0])


def inner_kernel(par, base, now, g_now, recv, coef, tent_ref, msg_ref):
    odd = par[0] == 1
    inner_finish(odd, base, now, g_now[...], recv[...], coef[4], None, tent_ref, msg_ref)


def outer_finish(odd, tent, sx, sx_left, recv0, recv1, g_own, u0_own, share, refs):
    u_ref, msg_ref, outer_ref = refs
    odd_part = jnp.where(odd, sx * recv0, 0.0)
    values = []
    for k in range(4):
        value = tent[k] - float(AB[k, 4]) * odd_part
        if k == 0:
            lost = recv0 if share is None else recv0 + share
            value = value - jnp.where(odd, 0.0, lost)
        u_ref[k] = value
        values.append(value)
    msg_ref[...] = jnp.where(odd, values[0], to_right(sx, values))
    mine = g_own if share is None else g_own + share
    outer_ref[...] = recv1 - jnp.where(odd, mine, KAPPA * sx_left * sx_left * u0_own)


def outer_first_kernel(
    par, tent, now, first, recv, inner, coef, cleft, left, right, mat_z,
    u_ref, msg_ref, outer_ref, coef0_ref, sxl_ref, last_ref, pad,
):
    odd = par[0] == 1
    theirs = expand_speed(recv[2 * NY :, :EZ], left[...], right[...])
    coefs = [jnp.where(odd, coef[i], theirs[i]) for i in range(5)]
    recv0 = recv[:NY]
    plane = jnp.where(odd, recv0, now[0])
    share = half_left(plane, coefs, mat_z, pad)
    on_left = [jnp.where(odd, cleft[i], theirs[i]) for i in range(5)]
    for i in range(4):
        coef0_ref[i] = 0.5 * (coef[i] + on_left[i])
    coef0_ref[4] = float(AB[4, 4]) * on_left[4]
    sxl_ref[...] = on_left[4]
    last_ref[...] = jnp.where(odd, recv0, inner[:NY])
    outer_finish(
        odd, tent, coef[4], on_left[4], recv0, recv[NY : 2 * NY], first[...], now[0], share,
        (u_ref, msg_ref, outer_ref),
    )


def outer_kernel(par, tent, now, g_now, recv, inner, coef, sxl, u_ref, msg_ref, outer_ref, last_ref):
    odd = par[0] == 1
    recv0 = recv[:NY]
    last_ref[...] = jnp.where(odd, recv0, inner[...])
    outer_finish(
        odd, tent, coef[4], sxl[...], recv0, recv[NY:], g_now[...], now[0], None,
        (u_ref, msg_ref, outer_ref),
    )


def both_kernel(par, base, inner, outer, coef, u_ref, g_ref, msg_ref, last_ref):
    odd = par[0] == 1
    last = jnp.where(odd, outer[...], inner[...])
    from_left = jnp.where(odd, inner[...], outer[...])
    sx = coef[4]
    pull = sx * last
    values = []
    for k in range(4):
        value = base[k] - float(AB[k, 4]) * pull
        if k == 0:
            value = value - from_left
        u_ref[k] = value
        values.append(value)
    g = to_right(sx, values)
    g_ref[...] = g
    msg_ref[...] = jnp.where(odd, values[0], g)
    last_ref[...] = last


def last_kernel(par, base, inner, outer, coef, u_ref):
    odd = par[0] == 1
    pull = coef[4] * jnp.where(odd, outer[...], inner[...])
    for k in range(4):
        u_ref[k] = base[k] - float(AB[k, 4]) * pull
    u_ref[0] = u_ref[0] - jnp.where(odd, inner[...], outer[...])


def slots_kernel(elem, weight, pick_ref, spread_ref):
    e = elem[...]
    ey = e // EZ
    ez = e - ey * EZ
    z = lax.broadcasted_iota(jnp.int32, (NZ, CAP), 0)
    for c in range(5):
        hot = (z == 4 * ez + c).astype(FP).astype(jnp.bfloat16)
        for half in range(2):
            pick_ref[half * NZ : (half + 1) * NZ, c * CAP : (c + 1) * CAP] = hot
    y = lax.broadcasted_iota(jnp.int32, (NY, CAP), 0)
    masks = []
    for b in range(5):
        row = 4 * ey + b
        row = jnp.where(row >= NY, row - NY, row)
        masks.append(y == row)
    for a in range(5):
        for c in range(5):
            total = jnp.zeros((NY, CAP), FP)
            for b in range(5):
                at = 25 * a + 5 * b + c
                total = jnp.where(masks[b], weight[at : at + 1, :], total)
            spread_ref[c, a * NY : (a + 1) * NY, :] = total


def sample(u, last, pick, spread):
    acc = jnp.zeros((8, CAP), FP)
    for a in range(5):
        plane = last[...] if a == 4 else u[a]
        high = plane.astype(jnp.bfloat16)
        low = (plane - high.astype(FP)).astype(jnp.bfloat16)
        got = jnp.dot(
            jnp.concatenate([high, low], 1), pick[...], preferred_element_type=jnp.float32
        )
        for c in range(5):
            part = got[:, c * CAP : (c + 1) * CAP] * spread[c, a * NY : (a + 1) * NY, :]
            acc = acc + jnp.sum(part.reshape(NY // 8, 8, CAP), 0)
    return jnp.sum(acc, 0, keepdims=True)


def sample_two_kernel(u0, l0, u1, l1, pick, spread, out):
    out[0:1, :] = sample(u0, l0, pick, spread)
    out[1:2, :] = sample(u1, l1, pick, spread)


def sample_last_kernel(par, inner, outer, u0, l0, u1, pick, spread, r0, r1, out, last):
    last[...] = jnp.where(par[0] == 1, outer[...], inner[...])
    rows = [r0[...], r1[...], sample(u0, l0, pick, spread), sample(u1, last, pick, spread)]
    rows = jnp.concatenate(rows + [jnp.zeros((2, CAP), FP)], 0)
    for i in range(out.shape[0]):
        out[i] = rows


def stations_kernel(blocks, stations, row_ref, lane_ref):
    lanes = []
    for j in range(2 * SB):
        wanted = blocks[0, j // SB] * SB + j % SB
        hit = jnp.zeros((8, CAP), FP)
        for r in range(16):
            hit = hit + jnp.where(stations[8 * r : 8 * r + 8, :] == wanted, 1.0, 0.0)
        lane_ref[j : j + 1, :] = jnp.sum(hit, 0, keepdims=True)
    lane = lane_ref[...]
    ids = stations[...].astype(FP)
    at = lax.dot_general(
        lane, ids, (((1,), (1,)), ((), ())), precision=HIGHEST, preferred_element_type=jnp.float32
    )
    j = lax.broadcasted_iota(jnp.int32, (2 * SB, 128), 0)
    wanted = jnp.where(j < SB, blocks[0, 0] * SB + j, blocks[0, 1] * SB + (j - SB))
    row_ref[...] = jnp.where(jnp.abs(at - wanted.astype(FP)) < 0.5, 1.0, 0.0)


def cross_kernel(gathered, row, lane, table, spread_a, spread_b, out, held, sems):
    slabs = [gathered[pl.ds(t, 128, stride=8), :] for t in range(NT)]
    hot = row[...].astype(jnp.bfloat16)
    found = jnp.dot(
        jnp.concatenate([hot, hot], 1),
        jnp.concatenate(parts_of(jnp.concatenate(slabs, 1), 2), 0),
        preferred_element_type=jnp.float32,
    )
    at = lax.broadcasted_iota(jnp.int32, (2 * SB, 128), 1)
    samples = jnp.zeros((2 * SB, 128), FP)
    for t in range(NT):
        one = jnp.sum(found[:, 128 * t : 128 * (t + 1)] * lane[...], 1, keepdims=True)
        samples = jnp.where(at % 8 == t, one, samples)
    parts = [part.astype(FP) for part in parts_of(samples, 3)]
    mixed = jnp.zeros((2 * SB, 128), FP)
    for group, (part, _) in enumerate(PART_PAIRS):
        mixed = jnp.where(at // 8 == group, parts[part], mixed)
    spectra = lax.dot_general(
        table[...], mixed.astype(jnp.bfloat16), (((1,), (1,)), ((), ())),
        preferred_element_type=jnp.float32,
    ).astype(jnp.bfloat16)
    second = jnp.dot(spectra, spread_b[...], preferred_element_type=jnp.float32) * (1.0 / NT)
    b_re = second[:F]
    b_im = second[F:]
    copies = []
    for i in range(4):
        first = jnp.dot(
            spectra, spread_a[:, 256 * i : 256 * (i + 1)], preferred_element_type=jnp.float32
        )
        for half in range(2):
            cols = slice(256 * i + 128 * half, 256 * i + 128 * (half + 1))
            a_re = first[:F, 128 * half : 128 * (half + 1)]
            a_im = first[F:, 128 * half : 128 * (half + 1)]
            held[0, :, cols] = (a_re * b_re + a_im * b_im).astype(jnp.bfloat16)
            held[1, :, cols] = (a_im * b_re - a_re * b_im).astype(jnp.bfloat16)
        cols = slice(256 * i, 256 * (i + 1))
        copy = pltpu.make_async_copy(held.at[:, :, cols], out.at[0, :, :, cols], sems.at[i])
        copy.start()
        copies.append(copy)
    for copy in copies:
        copy.wait()


def body(
    now, vel, speed_sq, src, wavelet, slot_elem, slot_station, slot_weight, pair_blocks, devices
):
    inner_route = [(i, i ^ 1) for i in range(devices)]
    outer_route = [(i, (i + 1 if i % 2 else i - 1) % devices) for i in range(devices)]

    def swap_inner(x):
        return lax.ppermute(x, AXES, inner_route)

    def swap_outer(x):
        return lax.ppermute(x, AXES, outer_route)

    mat_z, left, right = (jnp.asarray(x) for x in tables())
    table = jnp.asarray(dft_table())
    reps = np.zeros((2 * SB, SB * SB))
    for i in range(SB):
        reps[i, i * SB : (i + 1) * SB] = 1.0
    tiles = np.zeros((2 * SB, 128))
    for i in range(128):
        tiles[SB + i % SB, i] = 1.0
    reps = jnp.asarray(reps, jnp.bfloat16)
    tiles = jnp.asarray(tiles, jnp.bfloat16)
    pads = (pltpu.VMEM((4, NY + 16, NZ), FP),)
    one_pad = (pltpu.VMEM((1, NY + 16, NZ), FP),)

    par = (lax.axis_index("bulk") % 2).astype(jnp.int32).reshape(1)

    now, vel, src, speed, left, right, mat_z, coef, g0, msg = call(
        start_kernel,
        [(FOUR, FP)] * 3
        + [((EY, EZ), FP), (left.shape, FP), (right.shape, FP), (mat_z.shape, jnp.bfloat16)]
        + [(FIVE, FP), (PLANE, FP), ((NY + EY, NZ), FP)],
        (par, *(in_hbm(x) for x in (now, vel, src, speed_sq, left, right, mat_z))), "start",
        specs=[SMEM] + [HBM] * 7, scratch=(pltpu.SemaphoreType.DMA((7,)),),
    )
    inner0 = swap_inner(msg)
    (base,) = call(
        base_first_kernel, [(FOUR, FP)], (wavelet, now, vel, src, coef, mat_z), "base0", 1, scratch=pads
    )
    tent, msg, cleft = call(
        inner_first_kernel, [(FOUR, FP), ((2 * NY + EY, NZ), FP), (FIVE, FP)],
        (par, base, now, g0, inner0, speed, coef, left, right, mat_z), "inner0", 1, scratch=one_pad,
    )
    outer0 = swap_outer(msg)
    pick, spread = call(
        slots_kernel, [((2 * NZ, 5 * CAP), jnp.bfloat16), ((5, 5 * NY, CAP), FP)],
        (slot_elem.reshape(1, CAP), slot_weight), "slots",
    )
    row, lane = call(
        stations_kernel, [((2 * SB, 128), FP), ((2 * SB, CAP), FP)],
        (pair_blocks, slot_station.reshape(128, CAP)), "stations", 1,
    )
    outer0, pick, spread, row, lane = lax.optimization_barrier((outer0, pick, spread, row, lane))
    u_a = now
    u_b, msg, outer, coef0, sxl, last_a = call(
        outer_first_kernel,
        [(FOUR, FP), (PLANE, FP), (PLANE, FP), (FIVE, FP), (PLANE, FP), (PLANE, FP)],
        (par, tent, now, g0, outer0, inner0, coef, cleft, left, right, mat_z), "outer0", 1,
        scratch=one_pad,
    )
    rows = []
    step = 1
    while True:
        inner = swap_inner(msg)
        (base,) = call(
            functools.partial(base_kernel, step), [(FOUR, FP)],
            (wavelet, u_b, u_a, src, coef, coef0, mat_z), "base", 1, scratch=pads,
        )
        if step == NT - 1:
            break
        u_c, g_c, msg, last_b = call(
            both_kernel, [(FOUR, FP), (PLANE, FP), (PLANE, FP), (PLANE, FP)],
            (par, base, inner, outer, coef), "both", 1,
        )
        inner = swap_inner(msg)
        (base,) = call(
            functools.partial(base_kernel, step + 1), [(FOUR, FP)],
            (wavelet, u_c, u_b, src, coef, coef0, mat_z), "base", 1, scratch=pads,
        )
        tent, msg = call(
            inner_kernel, [(FOUR, FP), ((2 * NY, NZ), FP)],
            (par, base, u_c, g_c, inner, coef), "inner", 1,
        )
        recv = swap_outer(msg)
        (two,) = call(
            sample_two_kernel, [((2, CAP), FP)], (u_a, last_a, u_b, last_b, pick, spread), "sample2"
        )
        recv, two = lax.optimization_barrier((recv, two))
        rows.append(two)
        u_a = u_c
        u_b, msg, outer, last_a = call(
            outer_kernel, [(FOUR, FP), (PLANE, FP), (PLANE, FP), (PLANE, FP)],
            (par, tent, u_c, g_c, recv, inner, coef, sxl), "outer", 1,
        )
        step += 2
    (mine,) = call(
        sample_last_kernel, [((devices, 8, CAP), FP)],
        (par, inner, outer, u_a, last_a, u_b, pick, spread, *rows), "sample3", 1,
        scratch=(pltpu.VMEM(PLANE, FP),),
    )
    gathered = lax.all_to_all(mine, AXES, 0, 0, tiled=True)
    (end,) = call(last_kernel, [(FOUR, FP)], (par, base, inner, outer, coef), "last", 1)
    (cross,) = call(
        cross_kernel, [((1, 2, F, SB * SB), jnp.bfloat16)],
        (gathered.reshape(8 * devices, CAP), row, lane, table, reps, tiles), "cross",
        out_specs=[HBM],
        scratch=(pltpu.VMEM((2, F, SB * SB), jnp.bfloat16), pltpu.SemaphoreType.DMA((4,))),
    )
    return end, cross


def solution(mesh):
    split = P(AXES)
    in_specs = (
        P(AXES, None, None), P(AXES, None, None), P(AXES, None, None), P(AXES, None, None),
        P(), split, P(), P(None, AXES), P(AXES, None),
    )
    out_specs = (P(AXES, None, None), P(AXES, None, None, None))
    devices = math.prod(mesh.shape.values())
    run = functools.partial(body, devices=devices)
    return jax.shard_map(run, mesh=mesh, in_specs=in_specs, out_specs=out_specs, check_vma=False)
```

```python
import functools
import math

import jax
import jax.numpy as jnp
import numpy as np
from jax import lax
from jax.experimental import pallas as pl
from jax.experimental.pallas import tpu as pltpu
from jax.sharding import PartitionSpec as P

NT = 6
F = 256
SB = 32
STEP_DT = 0.04
NY = 96
NZ = 128
EY = 24
EZ = 32
CAP = 128
AXES = ("pair", "bulk")
HIGHEST = lax.Precision.HIGHEST
W1 = np.array([0.1, 49.0 / 90.0, 32.0 / 45.0, 49.0 / 90.0, 0.1])


def stiffness_1d():
    points = np.array([-1.0, -math.sqrt(3.0 / 7.0), 0.0, math.sqrt(3.0 / 7.0), 1.0])
    factor = np.array(
        [np.prod([points[i] - points[j] for j in range(5) if j != i]) for i in range(5)]
    )
    d = np.zeros((5, 5))
    for i in range(5):
        for j in range(5):
            if i != j:
                d[i, j] = factor[i] / (factor[j] * (points[i] - points[j]))
        d[i, i] = -np.sum(d[i])
    return d.T @ np.diag(W1) @ d


A = stiffness_1d()
MX = np.array([0.2, W1[1], W1[2], W1[3], 0.2])
AB = A / MX[:, None]
KAPPA = float(sum(AB[4, k] * AB[k, 4] for k in range(4)))


def f32(x):
    return np.asarray(x, np.float32)


def tables():
    my = np.array([MX[y % 4] for y in range(NY)])
    mz = np.array([0.1 if z == 0 else MX[z % 4] for z in range(NZ)])
    mat_z = np.zeros((NZ, 2 * NZ))
    for z in range(NZ):
        e, c = divmod(z, 4)
        for m in range(5):
            if 4 * e + m < NZ:
                mat_z[4 * e + m, z] += A[c, m]
            if c == 0 and e > 0:
                mat_z[4 * (e - 1) + m, NZ + z] += A[4, m]
    left = np.zeros((3 * NY, EY))
    for y in range(NY):
        e, b = divmod(y, 4)
        left[y, e] += W1[b]
        left[NY + y, e] += 1.0
        if b == 0:
            left[y, (e - 1) % EY] += W1[4]
            left[2 * NY + y, (e - 1) % EY] += 1.0
    left = left / np.tile(my, 3)[:, None]
    right = np.zeros((EZ, 3 * NZ))
    for z in range(NZ):
        e, c = divmod(z, 4)
        right[e, z] += 1.0
        right[e, 2 * NZ + z] += W1[c]
        if c == 0 and e > 0:
            right[e - 1, NZ + z] += 1.0
            right[e - 1, 2 * NZ + z] += W1[4]
    right = right / np.tile(mz, 3)[None, :] * (STEP_DT * STEP_DT)
    high = mat_z.astype(jnp.bfloat16).astype(np.float64)
    low = (mat_z - high).astype(jnp.bfloat16)
    stack = np.concatenate([mat_z, mat_z], 0).astype(jnp.bfloat16)
    return np.concatenate([stack, low], 0), f32(left), f32(right)


PART_PAIRS = ((0, 0), (1, 0), (0, 1), (1, 1), (2, 0), (0, 2))


def parts_of(x, count):
    parts = []
    for _ in range(count):
        part = x.astype(jnp.bfloat16)
        parts.append(part)
        x = x - part.astype(x.dtype)
    return parts


def dft_table():
    angle = np.pi * (np.arange(F) + 0.5) / F
    phase = angle[:, None] * np.arange(NT)[None, :]
    parts = parts_of(f32(np.concatenate([np.cos(phase), -np.sin(phase)], 0)), 3)
    table = np.zeros((2 * F, 128), jnp.bfloat16)
    for group, (_, part) in enumerate(PART_PAIRS):
        table[:, 8 * group : 8 * group + NT] = parts[part]
    return table


def dot(a, b):
    return jnp.dot(a, b, precision=HIGHEST, preferred_element_type=jnp.float32)


VMEM = pl.BlockSpec(memory_space=pltpu.VMEM)
SMEM = pl.BlockSpec(memory_space=pltpu.SMEM)
HBM = pl.BlockSpec(memory_space=pltpu.HBM)


def call(kernel, outs, args, name, smem=0, specs=None, out_specs=None, scratch=(), flops=4_000_000):
    return pl.pallas_call(
        kernel,
        out_shape=[jax.ShapeDtypeStruct(s, d) for s, d in outs],
        in_specs=specs or [SMEM] * smem + [VMEM] * (len(args) - smem),
        out_specs=out_specs or [VMEM] * len(outs),
        scratch_shapes=list(scratch),
        compiler_params=pltpu.CompilerParams(vmem_limit_bytes=24 * 1024 * 1024),
        cost_estimate=pl.CostEstimate(flops=flops, bytes_accessed=1_000_000, transcendentals=0),
        name=name,
    )(*args)


def in_hbm(x):
    return pltpu.with_memory_space_constraint(x, pltpu.HBM)


PACK = 32
ROWS = 9
PLANE = (NY, NZ)
FOUR = (4, NY, NZ)
FIVE = (5, NY, NZ)
FP = jnp.float32


def expand_speed(speed, left, right):
    rows = dot(left, speed)
    by_z = dot(rows[:NY], right)
    by_y = dot(rows[NY:], right[:, 2 * NZ :])
    return by_z[:, :NZ], by_z[:, NZ : 2 * NZ], by_y[:NY], by_y[NY:], by_z[:, 2 * NZ :]


def along_z(u, mat_z):
    high, low = parts_of(u, 2)
    return jnp.dot(
        jnp.concatenate([high, low], 1), mat_z[: 2 * NZ], preferred_element_type=jnp.float32
    ) + jnp.dot(high, mat_z[2 * NZ :], preferred_element_type=jnp.float32)


def y_patterns():
    b = lax.broadcasted_iota(jnp.int32, (8, NZ), 0) % 4
    own, before = {}, {}
    for d in range(-4, 5):
        total = jnp.zeros((8, NZ), FP)
        for row in range(4):
            if 0 <= row + d <= 4:
                total = jnp.where(b == row, float(A[row, row + d]), total)
        own[d] = total
        if d <= 0:
            before[d] = jnp.where(b == 0, float(A[4, 4 + d]), 0.0)
    return own, before


def y_coefs(y1, y2, patterns):
    own, before = patterns
    return {d: y1 * own[d] + y2 * before[d] if d in before else y1 * own[d] for d in own}


def wrap_rows(pad, at, plane):
    pad[at, 8 : 8 + NY, :] = plane
    pad[at, 4:8, :] = plane[NY - 4 :]
    pad[at, 8 + NY : 12 + NY, :] = plane[:4]


def along_y(pad, at, row, coefs):
    total = None
    for d, c in coefs.items():
        term = c * pad[at, 8 + row + d : 16 + row + d, :]
        total = term if total is None else total + term
    return total


def to_right(sx, u):
    total = float(AB[4, 0]) * u[0]
    for m in range(1, 4):
        total = total + float(AB[4, m]) * u[m]
    return sx * total


def start_kernel(
    par, now_in, vel_in, src_in, speed_in, left_in, right_in, mat_in, elem_in, weight_in,
    now, vel, src, speed, left, right, mat, elem, weight, coef_ref, first_ref, msg_ref, sems,
):
    pairs = (
        (speed_in.at[0], speed), (left_in, left), (right_in, right), (now_in, now), (vel_in, vel),
        (elem_in, elem), (weight_in, weight), (src_in, src), (mat_in, mat),
    )
    copies = [pltpu.make_async_copy(a, b, sems.at[i]) for i, (a, b) in enumerate(pairs)]
    for copy in copies:
        copy.start()
    for copy in copies[:3]:
        copy.wait()
    coefs = expand_speed(speed[...], left[...], right[...])
    for i in range(5):
        coef_ref[i] = coefs[i]
    msg_ref[NY:] = jnp.zeros((EY + PACK, NZ), FP)
    msg_ref[NY : NY + EY, :EZ] = speed[...]
    copies[3].wait()
    g = to_right(coefs[4], [now[k] for k in range(4)])
    first_ref[...] = g
    msg_ref[:NY] = jnp.where(par[0] == 1, now[0], g)
    for copy in copies[4:]:
        copy.wait()
    msg_ref[NY + EY : NY + EY + 25] = weight[100:125]
    msg_ref[NY + EY + PACK - 1 :] = elem[...].astype(FP)


def base_first_kernel(wave, now, vel, src, coef, mat_z, out, pad):
    base_body(0, wave, now, None, vel, src, coef, None, mat_z, out, pad)


def base_body(step, wave, now, prev, vel, src, coef, coef0, mat_z, out, pad):
    scale = wave[step] * (STEP_DT * STEP_DT)
    by_z = along_z(now[...].reshape(4 * NY, NZ), mat_z)
    patterns = y_patterns()
    for k in range(4):
        wrap_rows(pad, k, now[k])
    for row in range(0, NY, 8):
        at = slice(row, row + 8)
        u = [now[k, at, :] for k in range(4)]
        sx = coef[4, at, :]
        own = [coef[i, at, :] for i in range(4)]
        first = own if coef0 is None else [coef0[i, at, :] for i in range(4)]
        cy = y_coefs(own[2], own[3], patterns)
        cy0 = cy if coef0 is None else y_coefs(first[2], first[3], patterns)
        for k in range(4):
            c = own if k else first
            z = by_z[NY * k + row : NY * k + row + 8]
            force = c[0] * z[:, :NZ] + c[1] * z[:, NZ:] + along_y(pad, k, row, cy if k else cy0)
            if k == 0:
                force = 0.5 * force if coef0 is None else force + coef0[4, at, :] * u[0]
            mix = float(AB[k, 0]) * u[0]
            for m in range(1, 4):
                mix = mix + float(AB[k, m]) * u[m]
            force = scale * src[k, at, :] - (force + sx * mix)
            if prev is None:
                out[k, at, :] = u[k] + STEP_DT * vel[k, at, :] + force
            else:
                out[k, at, :] = 2.0 * u[k] - prev[k, at, :] + force


def base_kernel(step, wave, now, prev, src, coef, coef0, mat_z, out, pad):
    base_body(step, wave, now, prev, None, src, coef, coef0, mat_z, out, pad)


def half_left(plane, coefs, mat_z, pad):
    by_z = along_z(plane, mat_z)
    wrap_rows(pad, 0, plane)
    patterns = y_patterns()
    tiles = []
    for row in range(0, NY, 8):
        c = [x[row : row + 8] for x in coefs]
        by_y = along_y(pad, 0, row, y_coefs(c[2], c[3], patterns))
        z = by_z[row : row + 8]
        tiles.append(0.5 * (c[0] * z[:, :NZ] + c[1] * z[:, NZ:] + by_y))
    return jnp.concatenate(tiles, 0) + float(AB[4, 4]) * (coefs[4] * plane)


def inner_first_kernel(
    par, base, now, first, recv, speed, elem, weight, coef, left, right, mat_z,
    tent_ref, msg_ref, cleft_ref, pad,
):
    odd = par[0] == 1
    coefs = expand_speed(jnp.where(odd, recv[NY : NY + EY, :EZ], 0.0), left[...], right[...])
    for i in range(5):
        cleft_ref[i] = coefs[i]
    share = half_left(now[0], coefs, mat_z, pad)
    inner_finish(odd, base, now, first[...], recv[:NY], coef[4], share, tent_ref, msg_ref)
    at = 2 * NY
    msg_ref[at:] = jnp.zeros((EY + 3 * PACK, NZ), FP)
    msg_ref[at : at + EY, :EZ] = speed[...]
    at += EY
    msg_ref[at : at + 25] = jnp.where(odd, weight[100:125], weight[:25])
    msg_ref[at + PACK - 1 : at + PACK] = elem[...].astype(FP)
    at += PACK
    pulled = -float(AB[0, 4]) * weight[:25]
    for k in range(1, 4):
        pulled = pulled - float(AB[k, 4]) * weight[25 * k : 25 * k + 25]
    msg_ref[at : at + 25] = pulled
    at += PACK
    msg_ref[at:] = recv[NY + EY :]


def inner_finish(odd, base, now, g_now, inner, sx, share, tent_ref, msg_ref):
    even_part = jnp.where(odd, 0.0, sx * inner)
    tent = []
    for k in range(4):
        value = base[k] - float(AB[k, 4]) * even_part
        if k == 0:
            value = value - jnp.where(odd, inner, 0.0)
            if share is not None:
                value = value - share
        tent_ref[k] = value
        tent.append(value)
    msg_ref[:NY] = jnp.where(odd, g_now, now[0])
    msg_ref[NY : 2 * NY] = jnp.where(odd, to_right(sx, tent), tent[0])


def inner_kernel(par, base, now, g_now, recv, coef, tent_ref, msg_ref):
    odd = par[0] == 1
    inner_finish(odd, base, now, g_now[...], recv[...], coef[4], None, tent_ref, msg_ref)


def outer_finish(odd, tent, sx, sx_left, recv0, recv1, g_own, u0_own, share, refs):
    u_ref, msg_ref, outer_ref = refs
    odd_part = jnp.where(odd, sx * recv0, 0.0)
    values = []
    for k in range(4):
        value = tent[k] - float(AB[k, 4]) * odd_part
        if k == 0:
            lost = recv0 if share is None else recv0 + share
            value = value - jnp.where(odd, 0.0, lost)
        u_ref[k] = value
        values.append(value)
    msg_ref[...] = jnp.where(odd, values[0], to_right(sx, values))
    mine = g_own if share is None else g_own + share
    outer_ref[...] = recv1 - jnp.where(odd, mine, KAPPA * sx_left * sx_left * u0_own)


def outer_first_kernel(
    par, tent, now, first, recv, inner, coef, cleft, left, right, mat_z,
    u_ref, msg_ref, outer_ref, coef0_ref, sxl_ref, last_ref, pad,
):
    odd = par[0] == 1
    theirs = expand_speed(recv[2 * NY : 2 * NY + EY, :EZ], left[...], right[...])
    coefs = [jnp.where(odd, coef[i], theirs[i]) for i in range(5)]
    recv0 = recv[:NY]
    plane = jnp.where(odd, recv0, now[0])
    share = half_left(plane, coefs, mat_z, pad)
    on_left = [jnp.where(odd, cleft[i], theirs[i]) for i in range(5)]
    for i in range(4):
        coef0_ref[i] = 0.5 * (coef[i] + on_left[i])
    coef0_ref[4] = float(AB[4, 4]) * on_left[4]
    sxl_ref[...] = on_left[4]
    last_ref[...] = jnp.where(odd, recv0, inner[:NY])
    outer_finish(
        odd, tent, coef[4], on_left[4], recv0, recv[NY : 2 * NY], first[...], now[0], share,
        (u_ref, msg_ref, outer_ref),
    )


def outer_kernel(par, tent, now, g_now, recv, inner, coef, sxl, u_ref, msg_ref, outer_ref, last_ref):
    odd = par[0] == 1
    recv0 = recv[:NY]
    last_ref[...] = jnp.where(odd, recv0, inner[...])
    outer_finish(
        odd, tent, coef[4], sxl[...], recv0, recv[NY:], g_now[...], now[0], None,
        (u_ref, msg_ref, outer_ref),
    )


def both_kernel(par, base, inner, outer, coef, u_ref, g_ref, msg_ref, last_ref):
    odd = par[0] == 1
    last = jnp.where(odd, outer[...], inner[...])
    from_left = jnp.where(odd, inner[...], outer[...])
    sx = coef[4]
    pull = sx * last
    values = []
    for k in range(4):
        value = base[k] - float(AB[k, 4]) * pull
        if k == 0:
            value = value - from_left
        u_ref[k] = value
        values.append(value)
    g = to_right(sx, values)
    g_ref[...] = g
    msg_ref[...] = jnp.where(odd, values[0], g)
    last_ref[...] = last


def last_kernel(par, base, inner, outer, coef, u_ref):
    odd = par[0] == 1
    pull = coef[4] * jnp.where(odd, outer[...], inner[...])
    for k in range(4):
        u_ref[k] = base[k] - float(AB[k, 4]) * pull
    u_ref[0] = u_ref[0] - jnp.where(odd, inner[...], outer[...])


def pick_nodes(ez, pick_ref):
    z = lax.broadcasted_iota(jnp.int32, (NZ, CAP), 0)
    for c in range(5):
        hot = (z == 4 * ez + c).astype(FP).astype(jnp.bfloat16)
        for half in range(2):
            pick_ref[half * NZ : (half + 1) * NZ, c * CAP : (c + 1) * CAP] = hot


def y_masks(ey):
    y = lax.broadcasted_iota(jnp.int32, (NY, CAP), 0)
    masks = []
    for b in range(5):
        row = 4 * ey + b
        masks.append(y == jnp.where(row >= NY, row - NY, row))
    return masks


def spread_nodes(masks, weight, c):
    total = jnp.zeros((NY, CAP), FP)
    for b in range(5):
        total = jnp.where(masks[b], weight[5 * b + c : 5 * b + c + 1, :], total)
    return total


def slots_kernel(elem, weight, pick_ref, spread_ref):
    ey = elem[...] // EZ
    pick_nodes(elem[...] - ey * EZ, pick_ref)
    masks = y_masks(ey)
    for a in range(5):
        plane = weight[25 * a : 25 * a + 25, :]
        for c in range(5):
            spread_ref[c, a * NY : (a + 1) * NY, :] = spread_nodes(masks, plane, c)


def others_kernel(par, inner, outer, pick_l_ref, pick_2_ref, spread_ref):
    odd = par[0] == 1
    at = 2 * NY + EY
    from_inner = inner[NY + EY :]
    from_outer = outer[at : at + PACK]
    relayed = outer[at + 2 * PACK :]
    on_left = jnp.where(odd, from_inner, from_outer)
    second = jnp.where(odd, from_outer, relayed)
    pulled = jnp.where(odd, 0.0, outer[at + PACK : at + 2 * PACK])
    for group, (package, pick_ref) in enumerate(((on_left, pick_l_ref), (second, pick_2_ref))):
        elem = package[PACK - 1 :].astype(jnp.int32)
        ey = elem // EZ
        pick_nodes(elem - ey * EZ, pick_ref)
        masks = y_masks(ey)
        for c in range(5):
            spread_ref[2 * group, c] = spread_nodes(masks, package, c)
            if group == 0:
                spread_ref[1, c] = spread_nodes(masks, pulled, c)


def picked(planes, pick):
    high, low = parts_of(jnp.concatenate(planes, 0), 2)
    return jnp.dot(
        jnp.concatenate([high, low], 1), pick[...], preferred_element_type=jnp.float32
    )


def weighted(got, spread):
    total = None
    for c in range(5):
        term = got[:, c * CAP : (c + 1) * CAP] * spread(c)
        total = term if total is None else total + term
    return jnp.sum(jnp.sum(total.reshape(-1, 8, CAP), 0), 0, keepdims=True)


def sample(planes, pick, spread):
    rows = NY * len(planes)
    return weighted(picked(planes, pick), lambda c: spread[c, :rows, :])


def all_planes(u, last):
    return [u[0], u[1], u[2], u[3], last]


def sample_two_kernel(u0, l0, u1, l1, pick, spread, out):
    out[0:1, :] = sample(all_planes(u0, l0[...]), pick, spread)
    out[1:2, :] = sample(all_planes(u1, l1[...]), pick, spread)


def sample_last_kernel(
    par, u2, l2, u3, l3, u4, inner, tent, g, sxl, pick, spread, pick_l, pick_2, spread_o, first, out
):
    odd = par[0] == 1
    own_g = jnp.where(odd, -g[...], 0.0)
    face = u4[0]
    x = sxl[...] * face
    left = picked([tent[0], x, face], pick_l)
    rows = [
        first[...],
        sample(all_planes(u2, l2[...]), pick, spread),
        sample(all_planes(u3, l3[...]), pick, spread),
        sample(all_planes(u4, jnp.where(odd, 0.0, inner[...])), pick, spread),
        sample(all_planes(tent, own_g), pick, spread),
        weighted(left[:NY], lambda c: spread_o[0, c])
        + weighted(left[NY : 2 * NY], lambda c: spread_o[1, c]),
        weighted(
            picked([jnp.where(odd, -g[...], -float(AB[0, 4]) * x)], pick_2), lambda c: spread_o[2, c]
        ),
        jnp.where(odd, 0.0, weighted(left[2 * NY :], lambda c: spread_o[0, c])),
    ]
    rows = jnp.concatenate(rows, 0)
    for i in range(out.shape[0] // ROWS):
        out[ROWS * i : ROWS * (i + 1), :] = rows


def stations_kernel(blocks, stations, row_ref, lane_ref):
    lanes = []
    for j in range(2 * SB):
        wanted = blocks[0, j // SB] * SB + j % SB
        hit = jnp.zeros((8, CAP), FP)
        for r in range(16):
            hit = hit + jnp.where(stations[8 * r : 8 * r + 8, :] == wanted, 1.0, 0.0)
        lane_ref[j : j + 1, :] = jnp.sum(hit, 0, keepdims=True)
    lane = lane_ref[...]
    ids = stations[...].astype(FP)
    at = lax.dot_general(
        lane, ids, (((1,), (1,)), ((), ())), precision=HIGHEST, preferred_element_type=jnp.float32
    )
    j = lax.broadcasted_iota(jnp.int32, (2 * SB, 128), 0)
    wanted = jnp.where(j < SB, blocks[0, 0] * SB + j, blocks[0, 1] * SB + (j - SB))
    row = jnp.where(jnp.abs(at - wanted.astype(FP)) < 0.5, 1.0, 0.0)
    device = lax.broadcasted_iota(jnp.int32, (2 * SB, 128), 1)
    even = jnp.where(device % 2 == 0, row, 0.0)
    row_ref[0] = row
    row_ref[1] = pltpu.roll(row, 1, 1)
    row_ref[2] = pltpu.roll(even, 2, 1) + pltpu.roll(even, 127, 1)


def cross_kernel(gathered, row, lane, table, spread_a, spread_b, out, held, sems):
    slabs = [gathered[pl.ds(t, 128, stride=ROWS), :] for t in range(ROWS)]

    def select(which, slabs):
        hot = row[which].astype(jnp.bfloat16)
        parts = jnp.concatenate(parts_of(jnp.concatenate(slabs, 1), 2), 0)
        return jnp.dot(
            jnp.concatenate([hot, hot], 1), parts, preferred_element_type=jnp.float32
        )

    found = select(0, slabs[:6])
    more = select(1, [slabs[8], slabs[6]])
    last = select(2, [slabs[7]])
    found = [found[:, 128 * t : 128 * (t + 1)] for t in range(NT)]
    found[4] = found[4] + more[:, :128]
    found[5] = found[5] + more[:, 128:] + last
    at = lax.broadcasted_iota(jnp.int32, (2 * SB, 128), 1)
    samples = jnp.zeros((2 * SB, 128), FP)
    for t in range(NT):
        one = jnp.sum(found[t] * lane[...], 1, keepdims=True)
        samples = jnp.where(at % 8 == t, one, samples)
    parts = [part.astype(FP) for part in parts_of(samples, 3)]
    mixed = jnp.zeros((2 * SB, 128), FP)
    for group, (part, _) in enumerate(PART_PAIRS):
        mixed = jnp.where(at // 8 == group, parts[part], mixed)
    spectra = lax.dot_general(
        table[...], mixed.astype(jnp.bfloat16), (((1,), (1,)), ((), ())),
        preferred_element_type=jnp.float32,
    ).astype(jnp.bfloat16)
    second = jnp.dot(spectra, spread_b[...], preferred_element_type=jnp.float32) * (1.0 / NT)
    b_re = second[:F]
    b_im = second[F:]
    copies = []
    for i in range(4):
        first = jnp.dot(
            spectra, spread_a[:, 256 * i : 256 * (i + 1)], preferred_element_type=jnp.float32
        )
        for half in range(2):
            cols = slice(256 * i + 128 * half, 256 * i + 128 * (half + 1))
            a_re = first[:F, 128 * half : 128 * (half + 1)]
            a_im = first[F:, 128 * half : 128 * (half + 1)]
            held[0, :, cols] = (a_re * b_re + a_im * b_im).astype(jnp.bfloat16)
            held[1, :, cols] = (a_im * b_re - a_re * b_im).astype(jnp.bfloat16)
        cols = slice(256 * i, 256 * (i + 1))
        copy = pltpu.make_async_copy(held.at[:, :, cols], out.at[0, :, :, cols], sems.at[i])
        copy.start()
        copies.append(copy)
    for copy in copies:
        copy.wait()


def body(
    now, vel, speed_sq, src, wavelet, slot_elem, slot_station, slot_weight, pair_blocks, devices
):
    inner_route = [(i, i ^ 1) for i in range(devices)]
    outer_route = [(i, (i + 1 if i % 2 else i - 1) % devices) for i in range(devices)]

    def swap_inner(x):
        return lax.ppermute(x, AXES, inner_route)

    def swap_outer(x):
        return lax.ppermute(x, AXES, outer_route)

    mat_z, left, right = (jnp.asarray(x) for x in tables())
    table = jnp.asarray(dft_table())
    reps = np.zeros((2 * SB, SB * SB))
    for i in range(SB):
        reps[i, i * SB : (i + 1) * SB] = 1.0
    tiles = np.zeros((2 * SB, 128))
    for i in range(128):
        tiles[SB + i % SB, i] = 1.0
    reps = jnp.asarray(reps, jnp.bfloat16)
    tiles = jnp.asarray(tiles, jnp.bfloat16)
    pads = (pltpu.VMEM((4, NY + 16, NZ), FP),)
    one_pad = (pltpu.VMEM((1, NY + 16, NZ), FP),)

    par = (lax.axis_index("bulk") % 2).astype(jnp.int32).reshape(1)

    inputs = (now, vel, src, speed_sq, left, right, mat_z, slot_elem.reshape(1, CAP), slot_weight)
    now, vel, src, speed, left, right, mat_z, elem, weight, coef, g0, msg = call(
        start_kernel,
        [(FOUR, FP)] * 3
        + [((EY, EZ), FP), (left.shape, FP), (right.shape, FP), (mat_z.shape, jnp.bfloat16)]
        + [((1, CAP), jnp.int32), ((125, CAP), FP)]
        + [(FIVE, FP), (PLANE, FP), ((NY + EY + PACK, NZ), FP)],
        (par, *(in_hbm(x) for x in inputs)), "start",
        specs=[SMEM] + [HBM] * 9, scratch=(pltpu.SemaphoreType.DMA((9,)),),
    )
    inner0 = swap_inner(msg)
    (base,) = call(
        base_first_kernel, [(FOUR, FP)], (wavelet, now, vel, src, coef, mat_z), "base0", 1, scratch=pads
    )
    tent, msg, cleft = call(
        inner_first_kernel, [(FOUR, FP), ((2 * NY + EY + 3 * PACK, NZ), FP), (FIVE, FP)],
        (par, base, now, g0, inner0, speed, elem, weight, coef, left, right, mat_z), "inner0", 1,
        scratch=one_pad,
    )
    outer0 = swap_outer(msg)
    pick_shape = ((2 * NZ, 5 * CAP), jnp.bfloat16)
    pick, spread = call(slots_kernel, [pick_shape, ((5, 5 * NY, CAP), FP)], (elem, weight), "slots")
    row, lane = call(
        stations_kernel, [((3, 2 * SB, 128), FP), ((2 * SB, CAP), FP)],
        (pair_blocks, slot_station.reshape(128, CAP)), "stations", 1,
    )
    outer0, pick, spread, row, lane = lax.optimization_barrier((outer0, pick, spread, row, lane))
    u1, msg, outer, coef0, sxl, last0 = call(
        outer_first_kernel,
        [(FOUR, FP), (PLANE, FP), (PLANE, FP), (FIVE, FP), (PLANE, FP), (PLANE, FP)],
        (par, tent, now, g0, outer0, inner0, coef, cleft, left, right, mat_z), "outer0", 1,
        scratch=one_pad,
    )

    def base_of(step, u, before):
        return call(
            functools.partial(base_kernel, step), [(FOUR, FP)],
            (wavelet, u, before, src, coef, coef0, mat_z), "base", 1, scratch=pads,
        )[0]

    def two_steps(step, u_b, u_a, msg, outer):
        inner = swap_inner(msg)
        base = base_of(step, u_b, u_a)
        u_c, g, msg, last = call(
            both_kernel, [(FOUR, FP), (PLANE, FP), (PLANE, FP), (PLANE, FP)],
            (par, base, inner, outer, coef), "both", 1,
        )
        inner = swap_inner(msg)
        base = base_of(step + 1, u_c, u_b)
        tent, msg = call(
            inner_kernel, [(FOUR, FP), ((2 * NY, NZ), FP)],
            (par, base, u_c, g, inner, coef), "inner", 1,
        )
        return u_c, g, last, inner, tent, msg

    def complete(tent, u, g, recv, inner):
        return call(
            outer_kernel, [(FOUR, FP), (PLANE, FP), (PLANE, FP), (PLANE, FP)],
            (par, tent, u, g, recv, inner, coef, sxl), "outer", 1,
        )

    u2, g2, last1, inner2, tent, msg = two_steps(1, u1, now, msg, outer)
    recv = swap_outer(msg)
    (rows,) = call(
        sample_two_kernel, [((2, CAP), FP)], (now, last0, u1, last1, pick, spread), "sample2"
    )
    others = call(
        others_kernel, [pick_shape, pick_shape, ((3, 5, NY, CAP), FP)], (par, inner0, outer0), "others", 1
    )
    recv, rows, *others = lax.optimization_barrier((recv, rows, *others))
    u3, msg, outer, last2 = complete(tent, u2, g2, recv, inner2)
    u4, g4, last3, inner4, tent, msg = two_steps(3, u3, u2, msg, outer)
    (mine,) = call(
        sample_last_kernel, [((devices * ROWS, CAP), FP)],
        (par, u2, last2, u3, last3, u4, inner4, tent, g4, sxl, pick, spread, *others, rows), "sample4", 1,
    )
    gathered = lax.all_to_all(mine.reshape(devices, 1, ROWS * CAP), AXES, 0, 0, tiled=True)
    recv = swap_outer(msg)
    u5, msg, outer, _ = complete(tent, u4, g4, recv, inner4)
    inner = swap_inner(msg)
    (end,) = call(
        last_kernel, [(FOUR, FP)], (par, base_of(5, u5, u4), inner, outer, coef), "last", 1
    )
    (cross,) = call(
        cross_kernel, [((1, 2, F, SB * SB), jnp.bfloat16)],
        (gathered.reshape(devices * ROWS, CAP), row, lane, table, reps, tiles), "cross",
        out_specs=[HBM],
        scratch=(pltpu.VMEM((2, F, SB * SB), jnp.bfloat16), pltpu.SemaphoreType.DMA((4,))),
    )
    return end, cross


def solution(mesh):
    split = P(AXES)
    in_specs = (
        P(AXES, None, None), P(AXES, None, None), P(AXES, None, None), P(AXES, None, None),
        P(), split, P(), P(None, AXES), P(AXES, None),
    )
    out_specs = (P(AXES, None, None), P(AXES, None, None, None))
    devices = math.prod(mesh.shape.values())
    run = functools.partial(body, devices=devices)
    return jax.shard_map(run, mesh=mesh, in_specs=in_specs, out_specs=out_specs, check_vma=False)
```

```python
import functools
import math

import jax
import jax.numpy as jnp
import numpy as np
from jax import lax
from jax.experimental import pallas as pl
from jax.experimental.pallas import tpu as pltpu
from jax.sharding import PartitionSpec as P

NT = 6
F = 256
SB = 32
STEP_DT = 0.04
NY = 96
NZ = 128
EY = 24
EZ = 32
CAP = 128
AXES = ("pair", "chip", "core")
HIGHEST = lax.Precision.HIGHEST
W1 = np.array([0.1, 49.0 / 90.0, 32.0 / 45.0, 49.0 / 90.0, 0.1])


def stiffness_1d():
    points = np.array([-1.0, -math.sqrt(3.0 / 7.0), 0.0, math.sqrt(3.0 / 7.0), 1.0])
    factor = np.array(
        [np.prod([points[i] - points[j] for j in range(5) if j != i]) for i in range(5)]
    )
    d = np.zeros((5, 5))
    for i in range(5):
        for j in range(5):
            if i != j:
                d[i, j] = factor[i] / (factor[j] * (points[i] - points[j]))
        d[i, i] = -np.sum(d[i])
    return d.T @ np.diag(W1) @ d


A = stiffness_1d()
MX = np.array([0.2, W1[1], W1[2], W1[3], 0.2])
AB = A / MX[:, None]
KAPPA = float(sum(AB[4, k] * AB[k, 4] for k in range(4)))


def f32(x):
    return np.asarray(x, np.float32)


def tables():
    my = np.array([MX[y % 4] for y in range(NY)])
    mz = np.array([0.1 if z == 0 else MX[z % 4] for z in range(NZ)])
    mat_z = np.zeros((NZ, 2 * NZ))
    for z in range(NZ):
        e, c = divmod(z, 4)
        for m in range(5):
            if 4 * e + m < NZ:
                mat_z[4 * e + m, z] += A[c, m]
            if c == 0 and e > 0:
                mat_z[4 * (e - 1) + m, NZ + z] += A[4, m]
    left = np.zeros((3 * NY, EY))
    for y in range(NY):
        e, b = divmod(y, 4)
        left[y, e] += W1[b]
        left[NY + y, e] += 1.0
        if b == 0:
            left[y, (e - 1) % EY] += W1[4]
            left[2 * NY + y, (e - 1) % EY] += 1.0
    left[:NY] /= my[:, None]
    right = np.zeros((EZ, 3 * NZ))
    for z in range(NZ):
        e, c = divmod(z, 4)
        right[e, z] += 1.0
        right[e, 2 * NZ + z] += W1[c]
        if c == 0 and e > 0:
            right[e - 1, NZ + z] += 1.0
            right[e - 1, 2 * NZ + z] += W1[4]
    right[:, 2 * NZ :] /= mz[None, :]
    over_z = np.broadcast_to(1.0 / mz, (8, NZ)) * (STEP_DT * STEP_DT)
    over_y = np.broadcast_to(1.0 / my[:8, None], (8, NZ)) * (STEP_DT * STEP_DT)
    left = np.tile(left, (1, 3)).astype(jnp.bfloat16)
    right = np.tile(right, (3, 1)).astype(jnp.bfloat16)
    high = mat_z.astype(jnp.bfloat16).astype(np.float64)
    low = (mat_z - high).astype(jnp.bfloat16)
    stack = np.concatenate([mat_z, mat_z], 0).astype(jnp.bfloat16)
    return np.concatenate([stack, low], 0), left, right, f32(np.concatenate([over_y, over_z], 0))


PART_PAIRS = ((0, 0), (1, 0), (0, 1), (1, 1), (2, 0), (0, 2))


def parts_of(x, count):
    parts = []
    for _ in range(count):
        part = x.astype(jnp.bfloat16)
        parts.append(part)
        x = x - part.astype(x.dtype)
    return parts


def dft_table():
    angle = np.pi * (np.arange(F) + 0.5) / F
    phase = angle[:, None] * np.arange(NT)[None, :]
    parts = parts_of(f32(np.concatenate([np.cos(phase), -np.sin(phase)], 0)), 3)
    table = np.zeros((2 * F, 128), jnp.bfloat16)
    for group, (_, part) in enumerate(PART_PAIRS):
        table[:, 8 * group : 8 * group + NT] = parts[part]
    return table


def dot(a, b):
    return jnp.dot(a, b, precision=HIGHEST, preferred_element_type=jnp.float32)


VMEM = pl.BlockSpec(memory_space=pltpu.VMEM)
SMEM = pl.BlockSpec(memory_space=pltpu.SMEM)
HBM = pl.BlockSpec(memory_space=pltpu.HBM)


def call(kernel, outs, args, name, smem=0, specs=None, out_specs=None, scratch=(), flops=4_000_000):
    return pl.pallas_call(
        kernel,
        out_shape=[jax.ShapeDtypeStruct(s, d) for s, d in outs],
        in_specs=specs or [SMEM] * smem + [VMEM] * (len(args) - smem),
        out_specs=out_specs or [VMEM] * len(outs),
        scratch_shapes=list(scratch),
        compiler_params=pltpu.CompilerParams(vmem_limit_bytes=24 * 1024 * 1024),
        cost_estimate=pl.CostEstimate(flops=flops, bytes_accessed=1_000_000, transcendentals=0),
        name=name,
    )(*args)


def in_hbm(x):
    return pltpu.with_memory_space_constraint(x, pltpu.HBM)


PACK = 32
ROWS = 9
PLANE = (NY, NZ)
FOUR = (4, NY, NZ)
FIVE = (5, NY, NZ)
FP = jnp.float32


def expand_speed(speed, left, right, over):
    parts = jnp.concatenate(parts_of(speed, 3), 0)
    rows = jnp.dot(left, parts, preferred_element_type=jnp.float32)
    parts = jnp.concatenate(parts_of(rows, 3), 1)
    by_z = jnp.dot(parts[:NY], right, preferred_element_type=jnp.float32)
    by_y = jnp.dot(parts[NY:], right[:, 2 * NZ :], preferred_element_type=jnp.float32)
    over_y = jnp.concatenate([over[:8]] * (NY // 8), 0)
    over_z = over[8:9]
    return (
        by_z[:, :NZ] * over_z, by_z[:, NZ : 2 * NZ] * over_z, by_y[:NY] * over_y, by_y[NY:] * over_y,
        by_z[:, 2 * NZ :] * (STEP_DT * STEP_DT),
    )


def along_z(u, mat_z):
    high, low = parts_of(u, 2)
    return jnp.dot(
        jnp.concatenate([high, low], 1), mat_z[: 2 * NZ], preferred_element_type=jnp.float32
    ) + jnp.dot(high, mat_z[2 * NZ :], preferred_element_type=jnp.float32)


def y_patterns():
    b = lax.broadcasted_iota(jnp.int32, (8, NZ), 0) % 4
    own, before = {}, {}
    for d in range(-4, 5):
        total = jnp.zeros((8, NZ), FP)
        for row in range(4):
            if 0 <= row + d <= 4:
                total = jnp.where(b == row, float(A[row, row + d]), total)
        own[d] = total
        if d <= 0:
            before[d] = jnp.where(b == 0, float(A[4, 4 + d]), 0.0)
    return own, before


def y_coefs(y1, y2, patterns):
    own, before = patterns
    return {d: y1 * own[d] + y2 * before[d] if d in before else y1 * own[d] for d in own}


def wrap_rows(pad, at, plane):
    pad[at, 8 : 8 + NY, :] = plane
    pad[at, 4:8, :] = plane[NY - 4 :]
    pad[at, 8 + NY : 12 + NY, :] = plane[:4]


def along_y(pad, at, row, coefs):
    total = None
    for d, c in coefs.items():
        term = c * pad[at, 8 + row + d : 16 + row + d, :]
        total = term if total is None else total + term
    return total


def to_right(sx, u):
    total = float(AB[4, 0]) * u[0]
    for m in range(1, 4):
        total = total + float(AB[4, m]) * u[m]
    return sx * total


def start_kernel(
    par, now_in, vel_in, src_in, speed_in, left_in, right_in, over_in, mat_in, elem_in, weight_in, wave_in,
    now, vel, src, speed, left, right, over, mat, elem, weight, wave, coef_ref, first_ref, msg_ref, sems,
):
    pairs = (
        (speed_in.at[0], speed), (left_in, left), (right_in, right), (over_in, over), (now_in, now),
        (elem_in, elem), (weight_in, weight), (vel_in, vel), (src_in, src), (mat_in, mat),
        (wave_in, wave),
    )
    copies = [pltpu.make_async_copy(a, b, sems.at[i]) for i, (a, b) in enumerate(pairs)]
    for copy in copies:
        copy.start()
    for copy in copies[:4]:
        copy.wait()
    coefs = expand_speed(speed[...], left[...], right[...], over[...])
    for i in range(5):
        coef_ref[i] = coefs[i]
    msg_ref[NY:] = jnp.zeros((EY + PACK, NZ), FP)
    msg_ref[NY : NY + EY, :EZ] = speed[...]
    copies[4].wait()
    g = to_right(coefs[4], [now[k] for k in range(4)])
    first_ref[...] = g
    msg_ref[:NY] = jnp.where(par[0] == 1, now[0], g)
    for copy in copies[5:]:
        copy.wait()
    msg_ref[NY + EY : NY + EY + 25] = weight[100:125]
    msg_ref[NY + EY + PACK - 1 :] = elem[...].astype(FP)


def base_first_kernel(wave, now, vel, src, coef, mat_z, out, pad):
    base_body(0, wave, now, None, vel, src, coef, None, mat_z, out, pad)


def base_body(step, wave, now, prev, vel, src, coef, coef0, mat_z, out, pad):
    scale = jnp.broadcast_to(wave[:, step : step + 1] * (STEP_DT * STEP_DT), (8, NZ))
    by_z = along_z(now[...].reshape(4 * NY, NZ), mat_z)
    patterns = y_patterns()
    for k in range(4):
        wrap_rows(pad, k, now[k])
    for row in range(0, NY, 8):
        at = slice(row, row + 8)
        u = [now[k, at, :] for k in range(4)]
        sx = coef[4, at, :]
        own = [coef[i, at, :] for i in range(4)]
        first = own if coef0 is None else [coef0[i, at, :] for i in range(4)]
        cy = y_coefs(own[2], own[3], patterns)
        cy0 = cy if coef0 is None else y_coefs(first[2], first[3], patterns)
        for k in range(4):
            c = own if k else first
            z = by_z[NY * k + row : NY * k + row + 8]
            force = c[0] * z[:, :NZ] + c[1] * z[:, NZ:] + along_y(pad, k, row, cy if k else cy0)
            if k == 0:
                force = 0.5 * force if coef0 is None else force + coef0[4, at, :] * u[0]
            mix = float(AB[k, 0]) * u[0]
            for m in range(1, 4):
                mix = mix + float(AB[k, m]) * u[m]
            force = scale * src[k, at, :] - (force + sx * mix)
            if prev is None:
                out[k, at, :] = u[k] + STEP_DT * vel[k, at, :] + force
            else:
                out[k, at, :] = 2.0 * u[k] - prev[k, at, :] + force


def base_kernel(step, wave, now, prev, src, coef, coef0, mat_z, out, pad):
    base_body(step, wave, now, prev, None, src, coef, coef0, mat_z, out, pad)


def half_left(plane, coefs, mat_z, pad):
    by_z = along_z(plane, mat_z)
    wrap_rows(pad, 0, plane)
    patterns = y_patterns()
    tiles = []
    for row in range(0, NY, 8):
        c = [x[row : row + 8] for x in coefs]
        by_y = along_y(pad, 0, row, y_coefs(c[2], c[3], patterns))
        z = by_z[row : row + 8]
        tiles.append(0.5 * (c[0] * z[:, :NZ] + c[1] * z[:, NZ:] + by_y))
    return jnp.concatenate(tiles, 0) + float(AB[4, 4]) * (coefs[4] * plane)


def inner_first_kernel(
    par, base, now, first, recv, speed, elem, weight, coef, left, right, over, mat_z,
    tent_ref, msg_ref, cleft_ref, pad,
):
    odd = par[0] == 1
    coefs = expand_speed(jnp.where(odd, recv[NY : NY + EY, :EZ], 0.0), left[...], right[...], over[...])
    for i in range(5):
        cleft_ref[i] = coefs[i]
    share = half_left(now[0], coefs, mat_z, pad)
    inner_finish(odd, base, now, first[...], recv[:NY], coef[4], share, tent_ref, msg_ref)
    at = 2 * NY
    msg_ref[at:] = jnp.zeros((EY + 3 * PACK, NZ), FP)
    msg_ref[at : at + EY, :EZ] = speed[...]
    at += EY
    msg_ref[at : at + 25] = jnp.where(odd, weight[100:125], weight[:25])
    msg_ref[at + PACK - 1 : at + PACK] = elem[...].astype(FP)
    at += PACK
    pulled = -float(AB[0, 4]) * weight[:25]
    for k in range(1, 4):
        pulled = pulled - float(AB[k, 4]) * weight[25 * k : 25 * k + 25]
    msg_ref[at : at + 25] = pulled
    at += PACK
    msg_ref[at:] = recv[NY + EY :]


def inner_finish(odd, base, now, g_now, inner, sx, share, tent_ref, msg_ref):
    even_part = jnp.where(odd, 0.0, sx * inner)
    tent = []
    for k in range(4):
        value = base[k] - float(AB[k, 4]) * even_part
        if k == 0:
            value = value - jnp.where(odd, inner, 0.0)
            if share is not None:
                value = value - share
        tent_ref[k] = value
        tent.append(value)
    msg_ref[:NY] = jnp.where(odd, g_now, now[0])
    msg_ref[NY : 2 * NY] = jnp.where(odd, to_right(sx, tent), tent[0])


def inner_kernel(par, base, now, g_now, recv, coef, tent_ref, msg_ref):
    odd = par[0] == 1
    inner_finish(odd, base, now, g_now[...], recv[...], coef[4], None, tent_ref, msg_ref)


def outer_finish(odd, tent, sx, sx_left, recv0, recv1, g_own, u0_own, share, refs):
    u_ref, msg_ref, outer_ref = refs
    odd_part = jnp.where(odd, sx * recv0, 0.0)
    values = []
    for k in range(4):
        value = tent[k] - float(AB[k, 4]) * odd_part
        if k == 0:
            lost = recv0 if share is None else recv0 + share
            value = value - jnp.where(odd, 0.0, lost)
        u_ref[k] = value
        values.append(value)
    msg_ref[...] = jnp.where(odd, values[0], to_right(sx, values))
    mine = g_own if share is None else g_own + share
    outer_ref[...] = recv1 - jnp.where(odd, mine, KAPPA * sx_left * sx_left * u0_own)


def outer_first_kernel(
    par, tent, now, first, recv, inner, coef, cleft, left, right, over, mat_z,
    u_ref, msg_ref, outer_ref, coef0_ref, sxl_ref, last_ref, pad,
):
    odd = par[0] == 1
    theirs = expand_speed(recv[2 * NY : 2 * NY + EY, :EZ], left[...], right[...], over[...])
    coefs = [jnp.where(odd, coef[i], theirs[i]) for i in range(5)]
    recv0 = recv[:NY]
    plane = jnp.where(odd, recv0, now[0])
    share = half_left(plane, coefs, mat_z, pad)
    on_left = [jnp.where(odd, cleft[i], theirs[i]) for i in range(5)]
    for i in range(4):
        coef0_ref[i] = 0.5 * (coef[i] + on_left[i])
    coef0_ref[4] = float(AB[4, 4]) * on_left[4]
    sxl_ref[...] = on_left[4]
    last_ref[...] = jnp.where(odd, recv0, inner[:NY])
    outer_finish(
        odd, tent, coef[4], on_left[4], recv0, recv[NY : 2 * NY], first[...], now[0], share,
        (u_ref, msg_ref, outer_ref),
    )


def outer_kernel(par, tent, now, g_now, recv, inner, coef, sxl, u_ref, msg_ref, outer_ref, last_ref):
    odd = par[0] == 1
    recv0 = recv[:NY]
    last_ref[...] = jnp.where(odd, recv0, inner[...])
    outer_finish(
        odd, tent, coef[4], sxl[...], recv0, recv[NY:], g_now[...], now[0], None,
        (u_ref, msg_ref, outer_ref),
    )


def both_kernel(par, base, inner, outer, coef, u_ref, g_ref, msg_ref, last_ref):
    odd = par[0] == 1
    last = jnp.where(odd, outer[...], inner[...])
    from_left = jnp.where(odd, inner[...], outer[...])
    sx = coef[4]
    pull = sx * last
    values = []
    for k in range(4):
        value = base[k] - float(AB[k, 4]) * pull
        if k == 0:
            value = value - from_left
        u_ref[k] = value
        values.append(value)
    g = to_right(sx, values)
    g_ref[...] = g
    msg_ref[...] = jnp.where(odd, values[0], g)
    last_ref[...] = last


def outer_last_kernel(par, tent, now, g_now, recv, inner, coef, sxl, u_ref, msg_ref, outer_ref):
    outer_finish(
        par[0] == 1, tent, coef[4], sxl[...], recv[:NY], recv[NY:], g_now[...], now[0], None,
        (u_ref, msg_ref, outer_ref),
    )


def pick_nodes(ez, pick_ref):
    z = lax.broadcasted_iota(jnp.int32, (NZ, CAP), 0)
    for c in range(5):
        hot = (z == 4 * ez + c).astype(FP).astype(jnp.bfloat16)
        for half in range(2):
            pick_ref[half * NZ : (half + 1) * NZ, c * CAP : (c + 1) * CAP] = hot


def y_masks(ey):
    y = lax.broadcasted_iota(jnp.int32, (NY, CAP), 0)
    masks = []
    for b in range(5):
        row = 4 * ey + b
        masks.append(y == jnp.where(row >= NY, row - NY, row))
    return masks


def spread_nodes(masks, weight, c):
    total = jnp.zeros((NY, CAP), FP)
    for b in range(5):
        total = jnp.where(masks[b], weight[5 * b + c : 5 * b + c + 1, :], total)
    return total


def slots_kernel(elem, weight, pick_ref, spread_ref):
    ey = elem[...] // EZ
    pick_nodes(elem[...] - ey * EZ, pick_ref)
    masks = y_masks(ey)
    for a in range(5):
        plane = weight[25 * a : 25 * a + 25, :]
        for c in range(5):
            spread_ref[c, a * NY : (a + 1) * NY, :] = spread_nodes(masks, plane, c)


def others_kernel(par, inner, outer, pick_l_ref, pick_2_ref, spread_ref):
    odd = par[0] == 1
    at = 2 * NY + EY
    from_inner = inner[NY + EY :]
    from_outer = outer[at : at + PACK]
    relayed = outer[at + 2 * PACK :]
    on_left = jnp.where(odd, from_inner, from_outer)
    second = jnp.where(odd, from_outer, relayed)
    pulled = jnp.where(odd, 0.0, outer[at + PACK : at + 2 * PACK])
    for group, (package, pick_ref) in enumerate(((on_left, pick_l_ref), (second, pick_2_ref))):
        elem = package[PACK - 1 :].astype(jnp.int32)
        ey = elem // EZ
        pick_nodes(elem - ey * EZ, pick_ref)
        masks = y_masks(ey)
        for c in range(5):
            spread_ref[2 * group, c] = spread_nodes(masks, package, c)
            if group == 0:
                spread_ref[1, c] = spread_nodes(masks, pulled, c)


def picked(planes, pick):
    high, low = parts_of(jnp.concatenate(planes, 0), 2)
    return jnp.dot(
        jnp.concatenate([high, low], 1), pick[...], preferred_element_type=jnp.float32
    )


def weighted(got, spread):
    total = None
    for c in range(5):
        term = got[:, c * CAP : (c + 1) * CAP] * spread(c)
        total = term if total is None else total + term
    return jnp.sum(jnp.sum(total.reshape(-1, 8, CAP), 0), 0, keepdims=True)


def sample(planes, pick, spread):
    rows = NY * len(planes)
    return weighted(picked(planes, pick), lambda c: spread[c, :rows, :])


def all_planes(u, last):
    return [u[0], u[1], u[2], u[3], last]


def sample_first_kernel(u0, l0, u1, l1, u2, pick, spread, out):
    out[0:1, :] = sample(all_planes(u0, l0[...]), pick, spread)
    out[1:2, :] = sample(all_planes(u1, l1[...]), pick, spread)
    out[2:3, :] = sample([u2[k] for k in range(4)], pick, spread)


def sample_second_kernel(first, l2, u3, pick, spread, out):
    got = picked(all_planes(u3, l2[...]), pick)
    rest = 4 * NY
    out[0:2, :] = first[0:2, :]
    out[2:3, :] = first[2:3, :] + weighted(got[rest:], lambda c: spread[c, rest:, :])
    out[3:4, :] = weighted(got[:rest], lambda c: spread[c, :rest, :])


def sample_third_kernel(
    par, before, l3, u4, g, sxl, pick, spread, pick_l, pick_2, spread_o, out
):
    odd = par[0] == 1
    got = picked(all_planes(u4, l3[...]), pick)
    rest = 4 * NY
    face = u4[0]
    x = sxl[...] * face
    left = picked([x, face], pick_l)
    second = picked([jnp.where(odd, -g[...], -float(AB[0, 4]) * x)], pick_2)
    out[0:3, :] = before[0:3, :]
    out[3:4, :] = before[3:4, :] + weighted(got[rest:], lambda c: spread[c, rest:, :])
    out[4:5, :] = weighted(got[:rest], lambda c: spread[c, :rest, :])
    out[5:6, :] = weighted(left[:NY], lambda c: spread_o[1, c])
    out[6:7, :] = weighted(second, lambda c: spread_o[2, c])
    out[7:8, :] = jnp.where(odd, 0.0, weighted(left[NY:], lambda c: spread_o[0, c]))


def sample_last_kernel(
    par, before, inner, tent, g, pick, spread, pick_l, spread_o, out, block, sems
):
    odd = par[0] == 1
    own_g = jnp.where(odd, -g[...], 0.0)
    last = jnp.where(odd, 0.0, inner[...])
    got = picked(all_planes(tent, own_g) + [last], pick)
    face = picked([tent[0]], pick_l)
    rest = 4 * NY
    rows = [
        before[0:4, :],
        before[4:5, :] + weighted(got[5 * NY :], lambda c: spread[c, rest:, :]),
        weighted(got[: 5 * NY], lambda c: spread[c]),
        before[5:6, :] + weighted(face, lambda c: spread_o[0, c]),
        before[6:8, :],
    ]
    rows = jnp.concatenate(rows, 0)
    for i in range(8):
        block[ROWS * i : ROWS * (i + 1), :] = rows
    size = 8 * ROWS
    copies = [
        pltpu.make_async_copy(block, out.at[pl.ds(size * i, size), :], sems.at[i])
        for i in range(out.shape[0] // size)
    ]
    for copy in copies:
        copy.start()
    for copy in copies:
        copy.wait()


def stations_kernel(par, blocks, stations, row_ref, lane_ref):
    odd = par[0] == 1
    for j in range(2 * SB):
        wanted = blocks[0, j // SB] * SB + j % SB
        hit = jnp.zeros((8, CAP), FP)
        for r in range(16):
            hit = hit + jnp.where(stations[8 * r : 8 * r + 8, :] == wanted, 1.0, 0.0)
        lane_ref[j : j + 1, :] = jnp.sum(hit, 0, keepdims=True)
    lane = lane_ref[...]
    ids = stations[...].astype(FP)
    at = lax.dot_general(
        lane, ids, (((1,), (1,)), ((), ())), precision=HIGHEST, preferred_element_type=jnp.float32
    )
    j = lax.broadcasted_iota(jnp.int32, (2 * SB, 128), 0)
    wanted = jnp.where(j < SB, blocks[0, 0] * SB + j, blocks[0, 1] * SB + (j - SB))
    place = lax.broadcasted_iota(jnp.int32, (2 * SB, 128), 1)
    hit = jnp.where(jnp.abs(at - wanted.astype(FP)) < 0.5, place.astype(FP), 0.0)
    device = jnp.sum(hit, 1, keepdims=True).astype(jnp.int32)
    first = jnp.where(odd, 1, 0)

    def one_hot(device):
        device = jnp.bitwise_and(device, 127)
        side = jnp.where(jnp.bitwise_and(device, 1) == first, 0, 64)
        return jnp.where(place == side + jnp.right_shift(device, 1), 1.0, 0.0)

    row_ref[0] = one_hot(device)
    row_ref[1] = one_hot(device + 1)
    even = jnp.where(jnp.bitwise_and(device, 1) == 0, 1.0, 0.0)
    row_ref[2] = even * (one_hot(device + 2) + one_hot(device + 127))


def spectra_kernel(near, far, row, lane, table, out):
    slabs = [
        jnp.concatenate([half[pl.ds(t, 64, stride=ROWS), :] for half in (near, far)], 0)
        for t in range(ROWS)
    ]

    def select(which, slabs):
        hot = row[which].astype(jnp.bfloat16)
        parts = jnp.concatenate(parts_of(jnp.concatenate(slabs, 1), 2), 0)
        return jnp.dot(
            jnp.concatenate([hot, hot], 1), parts, preferred_element_type=jnp.float32
        )

    found = select(0, slabs[:6])
    more = select(1, [slabs[8], slabs[6]])
    last = select(2, [slabs[7]])
    found = [found[:, 128 * t : 128 * (t + 1)] for t in range(NT)]
    found[4] = found[4] + more[:, :128]
    found[5] = found[5] + more[:, 128:] + last
    at = lax.broadcasted_iota(jnp.int32, (2 * SB, 128), 1)
    samples = jnp.zeros((2 * SB, 128), FP)
    for t in range(NT):
        one = jnp.sum(found[t] * lane[...], 1, keepdims=True)
        samples = jnp.where(at % 8 == t, one, samples)
    parts = [part.astype(FP) for part in parts_of(samples, 3)]
    mixed = jnp.zeros((2 * SB, 128), FP)
    for group, (part, _) in enumerate(PART_PAIRS):
        mixed = jnp.where(at // 8 == group, parts[part], mixed)
    out[...] = lax.dot_general(
        table[...], mixed.astype(jnp.bfloat16), (((1,), (1,)), ((), ())),
        preferred_element_type=jnp.float32,
    ).astype(jnp.bfloat16)


def cross_kernel(
    par, base, inner, outer, coef, spectra_in, spread_a, spread_b, end, out, held_end, held, sems
):
    odd = par[0] == 1
    pull = coef[4] * jnp.where(odd, outer[...], inner[...])
    for k in range(4):
        value = base[k] - float(AB[k, 4]) * pull
        held_end[k] = value - jnp.where(odd, inner[...], outer[...]) if k == 0 else value
    copies = [pltpu.make_async_copy(held_end, end, sems.at[4])]
    copies[0].start()
    spectra = spectra_in[...]
    second = jnp.dot(spectra, spread_b[...], preferred_element_type=jnp.float32) * (1.0 / NT)
    b_re = second[:F]
    b_im = second[F:]
    for i in range(4):
        first = jnp.dot(
            spectra, spread_a[:, 256 * i : 256 * (i + 1)], preferred_element_type=jnp.float32
        )
        for half in range(2):
            cols = slice(256 * i + 128 * half, 256 * i + 128 * (half + 1))
            a_re = first[:F, 128 * half : 128 * (half + 1)]
            a_im = first[F:, 128 * half : 128 * (half + 1)]
            held[0, :, cols] = (a_re * b_re + a_im * b_im).astype(jnp.bfloat16)
            held[1, :, cols] = (a_im * b_re - a_re * b_im).astype(jnp.bfloat16)
        cols = slice(256 * i, 256 * (i + 1))
        copy = pltpu.make_async_copy(held.at[:, :, cols], out.at[0, :, :, cols], sems.at[i])
        copy.start()
        copies.append(copy)
    for copy in copies:
        copy.wait()


def body(
    now, vel, speed_sq, src, wavelet, slot_elem, slot_station, slot_weight, pair_blocks, devices
):
    inner_route = [(i, i ^ 1) for i in range(devices)]
    outer_route = [(i, (i + 1 if i % 2 else i - 1) % devices) for i in range(devices)]

    def swap_inner(x):
        return lax.ppermute(x, AXES, inner_route)

    def swap_outer(x):
        return lax.ppermute(x, AXES, outer_route)

    mat_z, left, right, over = (jnp.asarray(x) for x in tables())
    table = jnp.asarray(dft_table())
    reps = np.zeros((2 * SB, SB * SB))
    for i in range(SB):
        reps[i, i * SB : (i + 1) * SB] = 1.0
    tiles = np.zeros((2 * SB, 128))
    for i in range(128):
        tiles[SB + i % SB, i] = 1.0
    reps = jnp.asarray(reps, jnp.bfloat16)
    tiles = jnp.asarray(tiles, jnp.bfloat16)
    pads = (pltpu.VMEM((4, NY + 16, NZ), FP),)
    one_pad = (pltpu.VMEM((1, NY + 16, NZ), FP),)

    par = lax.axis_index("core").astype(jnp.int32).reshape(1)

    inputs = (
        now, vel, src, speed_sq, left, right, over, mat_z, slot_elem.reshape(1, CAP), slot_weight,
        wavelet.reshape(1, NT),
    )
    kept = [jax.ShapeDtypeStruct(x.shape, x.dtype) for x in inputs]
    kept[3] = jax.ShapeDtypeStruct((EY, EZ), FP)
    now, vel, src, speed, left, right, over, mat_z, elem, weight, wavelet, coef, g0, msg = call(
        start_kernel,
        [(x.shape, x.dtype) for x in kept]
        + [(FIVE, FP), (PLANE, FP), ((NY + EY + PACK, NZ), FP)],
        (par, *(in_hbm(x) for x in inputs)), "start",
        specs=[SMEM] + [HBM] * len(inputs), scratch=(pltpu.SemaphoreType.DMA((len(inputs),)),),
    )
    inner0 = swap_inner(msg)
    (base,) = call(
        base_first_kernel, [(FOUR, FP)], (wavelet, now, vel, src, coef, mat_z), "base0", scratch=pads
    )
    tent, msg, cleft = call(
        inner_first_kernel, [(FOUR, FP), ((2 * NY + EY + 3 * PACK, NZ), FP), (FIVE, FP)],
        (par, base, now, g0, inner0, speed, elem, weight, coef, left, right, over, mat_z), "inner0", 1,
        scratch=one_pad,
    )
    outer0 = swap_outer(msg)
    pick_shape = ((2 * NZ, 5 * CAP), jnp.bfloat16)
    pick, spread = call(slots_kernel, [pick_shape, ((5, 5 * NY, CAP), FP)], (elem, weight), "slots")
    row, lane = call(
        stations_kernel, [((3, 2 * SB, 128), FP), ((2 * SB, CAP), FP)],
        (par, pair_blocks, slot_station.reshape(128, CAP)), "stations", 2,
    )
    outer0, pick, spread, row, lane = lax.optimization_barrier((outer0, pick, spread, row, lane))
    u1, msg, outer, coef0, sxl, last0 = call(
        outer_first_kernel,
        [(FOUR, FP), (PLANE, FP), (PLANE, FP), (FIVE, FP), (PLANE, FP), (PLANE, FP)],
        (par, tent, now, g0, outer0, inner0, coef, cleft, left, right, over, mat_z), "outer0", 1,
        scratch=one_pad,
    )

    def base_of(step, u, before):
        return call(
            functools.partial(base_kernel, step), [(FOUR, FP)],
            (wavelet, u, before, src, coef, coef0, mat_z), "base", scratch=pads,
        )[0]

    def two_steps(step, u_b, u_a, msg, outer, fill=(None, None)):
        inner = swap_inner(msg)
        base = base_of(step, u_b, u_a)
        more = None
        if fill[0]:
            inner, base, more = lax.optimization_barrier((inner, base, fill[0]()))
        u_c, g, msg, last = call(
            both_kernel, [(FOUR, FP), (PLANE, FP), (PLANE, FP), (PLANE, FP)],
            (par, base, inner, outer, coef), "both", 1,
        )
        inner = swap_inner(msg)
        base = base_of(step + 1, u_c, u_b)
        if fill[1]:
            inner, base, more = lax.optimization_barrier((inner, base, fill[1](more, u_c, g, last)))
        tent, msg = call(
            inner_kernel, [(FOUR, FP), ((2 * NY, NZ), FP)],
            (par, base, u_c, g, inner, coef), "inner", 1,
        )
        return u_c, g, last, inner, tent, msg, more

    def complete(tent, u, g, recv, inner):
        return call(
            outer_kernel, [(FOUR, FP), (PLANE, FP), (PLANE, FP), (PLANE, FP)],
            (par, tent, u, g, recv, inner, coef, sxl), "outer", 1,
        )

    u2, g2, last1, inner2, tent, msg, _ = two_steps(1, u1, now, msg, outer)
    recv = swap_outer(msg)
    (rows,) = call(
        sample_first_kernel, [((3, CAP), FP)], (now, last0, u1, last1, u2, pick, spread), "sample3"
    )
    others = call(
        others_kernel, [pick_shape, pick_shape, ((3, 5, NY, CAP), FP)], (par, inner0, outer0), "others", 1
    )
    recv, rows, *others = lax.optimization_barrier((recv, rows, *others))
    u3, msg, outer, last2 = complete(tent, u2, g2, recv, inner2)

    def second_rows():
        return call(
            sample_second_kernel, [((4, CAP), FP)], (rows, last2, u3, pick, spread), "sample5"
        )[0]

    def third_rows(before, u, g, last):
        return call(
            sample_third_kernel, [((8, CAP), FP)],
            (par, before, last, u, g, sxl, pick, spread, *others), "sample8", 1,
        )[0]

    u4, g4, _, inner4, tent, msg, rows = two_steps(3, u3, u2, msg, outer, (second_rows, third_rows))
    pick_l, _, spread_o = others
    (mine,) = call(
        sample_last_kernel, [((devices // 2 * ROWS, CAP), FP)],
        (par, rows, inner4, tent, g4, pick, spread, pick_l, spread_o), "sample7", 1,
        out_specs=[HBM],
        scratch=(
            pltpu.VMEM((8 * ROWS, CAP), FP), pltpu.SemaphoreType.DMA((devices // 16,)),
        ),
    )
    near = lax.all_to_all(
        mine.reshape(devices // 2, 1, ROWS * CAP), ("pair", "chip"), 0, 0, tiled=True
    ).reshape(devices // 2 * ROWS, CAP)
    recv = swap_outer(msg)
    recv, near = lax.optimization_barrier((recv, near))
    far = swap_inner(near)
    u5, msg, outer = call(
        outer_last_kernel, [(FOUR, FP), (PLANE, FP), (PLANE, FP)],
        (par, tent, u4, g4, recv, inner4, coef, sxl), "outer", 1,
    )
    inner = swap_inner(msg)
    base = base_of(5, u5, u4)
    (spectra,) = call(
        spectra_kernel, [((2 * F, 2 * SB), jnp.bfloat16)],
        (near, far, row, lane, table), "spectra",
    )
    inner, base, spectra = lax.optimization_barrier((inner, base, spectra))
    end, cross = call(
        cross_kernel, [(FOUR, FP), ((1, 2, F, SB * SB), jnp.bfloat16)],
        (par, base, inner, outer, coef, spectra, reps, tiles), "cross", 1,
        out_specs=[HBM, HBM],
        scratch=(
            pltpu.VMEM(FOUR, FP), pltpu.VMEM((2, F, SB * SB), jnp.bfloat16),
            pltpu.SemaphoreType.DMA((5,)),
        ),
    )
    return end, cross


def solution(mesh):
    split = P(AXES)
    in_specs = (
        P(AXES, None, None), P(AXES, None, None), P(AXES, None, None), P(AXES, None, None),
        P(), split, P(), P(None, AXES), P(AXES, None),
    )
    out_specs = (P(AXES, None, None), P(AXES, None, None, None))
    grid = mesh.devices.reshape(mesh.shape["pair"], -1, 2)
    mesh = jax.sharding.Mesh(grid, AXES)
    devices = grid.size
    run = functools.partial(body, devices=devices)
    return jax.shard_map(run, mesh=mesh, in_specs=in_specs, out_specs=out_specs, check_vma=False)
```

```python
import functools
import math

import jax
import jax.numpy as jnp
import numpy as np
from jax import lax
from jax.experimental import pallas as pl
from jax.experimental.pallas import tpu as pltpu
from jax.sharding import PartitionSpec as P

NT = 6
F = 256
SB = 32
STEP_DT = 0.04
NY = 96
NZ = 128
EY = 24
EZ = 32
CAP = 128
AXES = ("pair", "chip", "core")
HIGHEST = lax.Precision.HIGHEST
W1 = np.array([0.1, 49.0 / 90.0, 32.0 / 45.0, 49.0 / 90.0, 0.1])


def stiffness_1d():
    points = np.array([-1.0, -math.sqrt(3.0 / 7.0), 0.0, math.sqrt(3.0 / 7.0), 1.0])
    factor = np.array(
        [np.prod([points[i] - points[j] for j in range(5) if j != i]) for i in range(5)]
    )
    d = np.zeros((5, 5))
    for i in range(5):
        for j in range(5):
            if i != j:
                d[i, j] = factor[i] / (factor[j] * (points[i] - points[j]))
        d[i, i] = -np.sum(d[i])
    return d.T @ np.diag(W1) @ d


A = stiffness_1d()
MX = np.array([0.2, W1[1], W1[2], W1[3], 0.2])
AB = A / MX[:, None]
KAPPA = float(sum(AB[4, k] * AB[k, 4] for k in range(4)))


def f32(x):
    return np.asarray(x, np.float32)


def tables():
    my = np.array([MX[y % 4] for y in range(NY)])
    mz = np.array([0.1 if z == 0 else MX[z % 4] for z in range(NZ)])
    mat_z = np.zeros((NZ, 2 * NZ))
    for z in range(NZ):
        e, c = divmod(z, 4)
        for m in range(5):
            if 4 * e + m < NZ:
                mat_z[4 * e + m, z] += A[c, m]
            if c == 0 and e > 0:
                mat_z[4 * (e - 1) + m, NZ + z] += A[4, m]
    left = np.zeros((3 * NY, EY))
    for y in range(NY):
        e, b = divmod(y, 4)
        left[y, e] += W1[b]
        left[NY + y, e] += 1.0
        if b == 0:
            left[y, (e - 1) % EY] += W1[4]
            left[2 * NY + y, (e - 1) % EY] += 1.0
    left[:NY] /= my[:, None]
    right = np.zeros((EZ, 3 * NZ))
    for z in range(NZ):
        e, c = divmod(z, 4)
        right[e, z] += 1.0
        right[e, 2 * NZ + z] += W1[c]
        if c == 0 and e > 0:
            right[e - 1, NZ + z] += 1.0
            right[e - 1, 2 * NZ + z] += W1[4]
    right[:, 2 * NZ :] /= mz[None, :]
    over_z = np.broadcast_to(1.0 / mz, (8, NZ)) * (STEP_DT * STEP_DT)
    over_y = np.broadcast_to(1.0 / my[:8, None], (8, NZ)) * (STEP_DT * STEP_DT)
    left = np.tile(left, (1, 3)).astype(jnp.bfloat16)
    right = np.tile(right, (3, 1)).astype(jnp.bfloat16)
    high = mat_z.astype(jnp.bfloat16).astype(np.float64)
    low = (mat_z - high).astype(jnp.bfloat16)
    stack = np.concatenate([mat_z, mat_z], 0).astype(jnp.bfloat16)
    return np.concatenate([stack, low], 0), left, right, f32(np.concatenate([over_y, over_z], 0))


PART_PAIRS = ((0, 0), (1, 0), (0, 1), (1, 1), (2, 0), (0, 2))


def parts_of(x, count):
    parts = []
    for _ in range(count):
        part = x.astype(jnp.bfloat16)
        parts.append(part)
        x = x - part.astype(x.dtype)
    return parts


def dft_table():
    angle = np.pi * (np.arange(F) + 0.5) / F
    phase = angle[:, None] * np.arange(NT)[None, :]
    parts = parts_of(f32(np.concatenate([np.cos(phase), -np.sin(phase)], 0)), 3)
    table = np.zeros((2 * F, 128), jnp.bfloat16)
    for group, (_, part) in enumerate(PART_PAIRS):
        table[:, 8 * group : 8 * group + NT] = parts[part]
    return table


def dot(a, b):
    return jnp.dot(a, b, precision=HIGHEST, preferred_element_type=jnp.float32)


VMEM = pl.BlockSpec(memory_space=pltpu.VMEM)
SMEM = pl.BlockSpec(memory_space=pltpu.SMEM)
HBM = pl.BlockSpec(memory_space=pltpu.HBM)


def call(kernel, outs, args, name, smem=0, specs=None, out_specs=None, scratch=(), flops=4_000_000):
    return pl.pallas_call(
        kernel,
        out_shape=[jax.ShapeDtypeStruct(s, d) for s, d in outs],
        in_specs=specs or [SMEM] * smem + [VMEM] * (len(args) - smem),
        out_specs=out_specs or [VMEM] * len(outs),
        scratch_shapes=list(scratch),
        compiler_params=pltpu.CompilerParams(vmem_limit_bytes=24 * 1024 * 1024),
        cost_estimate=pl.CostEstimate(flops=flops, bytes_accessed=1_000_000, transcendentals=0),
        name=name,
    )(*args)


def in_hbm(x):
    return pltpu.with_memory_space_constraint(x, pltpu.HBM)


PACK = 32
ROWS = 9
PACK_AT = 2 * NY + 2 * EY
PLANE = (NY, NZ)
FOUR = (4, NY, NZ)
FIVE = (5, NY, NZ)
FP = jnp.float32


def expand_speed(parts, left, right, over):
    rows = jnp.dot(left, parts, preferred_element_type=jnp.float32)
    parts = jnp.concatenate(parts_of(rows, 3), 1)
    by_z = jnp.dot(parts[:NY], right, preferred_element_type=jnp.float32)
    by_y = jnp.dot(parts[NY:], right[:, 2 * NZ :], preferred_element_type=jnp.float32)
    over_y = jnp.concatenate([over[:8]] * (NY // 8), 0)
    over_z = over[8:9]
    return (
        by_z[:, :NZ] * over_z, by_z[:, NZ : 2 * NZ] * over_z, by_y[:NY] * over_y, by_y[NY:] * over_y,
        by_z[:, 2 * NZ :] * (STEP_DT * STEP_DT),
    )


def speed_parts(speed, count=3):
    return jnp.concatenate(parts_of(speed, count), 0)


def along_z(u, mat_z):
    high, low = parts_of(u, 2)
    return jnp.dot(
        jnp.concatenate([high, low], 1), mat_z[: 2 * NZ], preferred_element_type=jnp.float32
    ) + jnp.dot(high, mat_z[2 * NZ :], preferred_element_type=jnp.float32)


def y_patterns():
    b = lax.broadcasted_iota(jnp.int32, (8, NZ), 0) % 4
    own, before = {}, {}
    for d in range(-4, 5):
        total = jnp.zeros((8, NZ), FP)
        for row in range(4):
            if 0 <= row + d <= 4:
                total = jnp.where(b == row, float(A[row, row + d]), total)
        own[d] = total
        if d <= 0:
            before[d] = jnp.where(b == 0, float(A[4, 4 + d]), 0.0)
    return own, before


def y_coefs(y1, y2, patterns):
    own, before = patterns
    return {d: y1 * own[d] + y2 * before[d] if d in before else y1 * own[d] for d in own}


def wrap_rows(pad, at, plane):
    pad[at, 8 : 8 + NY, :] = plane
    pad[at, 4:8, :] = plane[NY - 4 :]
    pad[at, 8 + NY : 12 + NY, :] = plane[:4]


def along_y(pad, at, row, coefs):
    total = None
    for d, c in coefs.items():
        term = c * pad[at, 8 + row + d : 16 + row + d, :]
        total = term if total is None else total + term
    return total


def to_right(sx, u):
    total = float(AB[4, 0]) * u[0]
    for m in range(1, 4):
        total = total + float(AB[4, m]) * u[m]
    return sx * total


def start_kernel(
    par, now_in, vel_in, src_in, speed_in, left_in, right_in, over_in, mat_in, elem_in, weight_in, wave_in,
    now, vel, src, speed, left, right, over, mat, elem, weight, wave, msg_ref, sems,
):
    pairs = (
        (now_in, now), (speed_in.at[0], speed), (elem_in, elem), (weight_in, weight), (vel_in, vel),
        (src_in, src), (left_in, left), (right_in, right), (over_in, over), (mat_in, mat), (wave_in, wave),
    )
    copies = [pltpu.make_async_copy(a, b, sems.at[i]) for i, (a, b) in enumerate(pairs)]
    for copy in copies:
        copy.start()
    msg_ref[NY:] = jnp.zeros((EY + PACK, NZ), FP)
    copies[0].wait()
    msg_ref[:NY] = jnp.where(par[0] == 1, now[0], to_right(1.0, [now[k] for k in range(4)]))
    for copy in copies[1:4]:
        copy.wait()
    msg_ref[NY : NY + EY, :EZ] = speed[...]
    msg_ref[NY + EY : NY + EY + 25] = weight[100:125]
    msg_ref[NY + EY + PACK - 1 :] = elem[...].astype(FP)
    for copy in copies[4:]:
        copy.wait()


def base_first_kernel(
    wave, now, vel, src, speed, left, right, over, mat_z, out, coef_ref, first_ref, pad
):
    coefs = expand_speed(speed_parts(speed[...]), left[...], right[...], over[...])
    for i in range(5):
        coef_ref[i] = coefs[i]
    first_ref[...] = to_right(coefs[4], [now[k] for k in range(4)])
    base_body(0, wave, now, None, vel, src, coef_ref, None, mat_z, out, pad)


def base_body(step, wave, now, prev, vel, src, coef, coef0, mat_z, out, pad):
    scale = jnp.broadcast_to(wave[:, step : step + 1] * (STEP_DT * STEP_DT), (8, NZ))
    by_z = along_z(now[...].reshape(4 * NY, NZ), mat_z)
    patterns = y_patterns()
    for k in range(4):
        wrap_rows(pad, k, now[k])
    for row in range(0, NY, 8):
        at = slice(row, row + 8)
        u = [now[k, at, :] for k in range(4)]
        sx = coef[4, at, :]
        own = [coef[i, at, :] for i in range(4)]
        first = own if coef0 is None else [coef0[i, at, :] for i in range(4)]
        cy = y_coefs(own[2], own[3], patterns)
        cy0 = cy if coef0 is None else y_coefs(first[2], first[3], patterns)
        for k in range(4):
            c = own if k else first
            z = by_z[NY * k + row : NY * k + row + 8]
            force = c[0] * z[:, :NZ] + c[1] * z[:, NZ:] + along_y(pad, k, row, cy if k else cy0)
            if k == 0:
                force = 0.5 * force if coef0 is None else force + coef0[4, at, :] * u[0]
            mix = float(AB[k, 0]) * u[0]
            for m in range(1, 4):
                mix = mix + float(AB[k, m]) * u[m]
            force = scale * src[k, at, :] - (force + sx * mix)
            if prev is None:
                out[k, at, :] = u[k] + STEP_DT * vel[k, at, :] + force
            else:
                out[k, at, :] = 2.0 * u[k] - prev[k, at, :] + force


def base_kernel(step, wave, now, prev, src, coef, coef0, mat_z, out, pad):
    base_body(step, wave, now, prev, None, src, coef, coef0, mat_z, out, pad)


def half_left(plane, coefs, mat_z, pad):
    by_z = along_z(plane, mat_z)
    wrap_rows(pad, 0, plane)
    patterns = y_patterns()
    tiles = []
    for row in range(0, NY, 8):
        c = [x[row : row + 8] for x in coefs]
        by_y = along_y(pad, 0, row, y_coefs(c[2], c[3], patterns))
        z = by_z[row : row + 8]
        tiles.append(0.5 * (c[0] * z[:, :NZ] + c[1] * z[:, NZ:] + by_y))
    return jnp.concatenate(tiles, 0) + float(AB[4, 4]) * (coefs[4] * plane)


def inner_first_kernel(
    par, base, now, first, recv, speed, elem, weight, coef, left, right, over, mat_z,
    tent_ref, msg_ref, cleft_ref, pad,
):
    odd = par[0] == 1
    their_speed = jnp.where(odd, recv[NY : NY + EY, :EZ], 0.0)
    coefs = expand_speed(speed_parts(their_speed), left[...], right[...], over[...])
    for i in range(5):
        cleft_ref[i] = coefs[i]
    share = half_left(now[0], coefs, mat_z, pad)
    inner = jnp.where(odd, coefs[4] * recv[:NY], recv[:NY])
    inner_finish(odd, base, now, first[...], inner, coef[4], share, tent_ref, msg_ref)
    own_speed = jnp.concatenate([speed[...], jnp.zeros((EY, NZ - EZ), FP)], 1)
    msg_ref[2 * NY : PACK_AT] = speed_parts(own_speed, 2)
    pulled = -float(AB[0, 4]) * weight[:25]
    for k in range(1, 4):
        pulled = pulled - float(AB[k, 4]) * weight[25 * k : 25 * k + 25]
    slots = elem[...].astype(FP)
    theirs = recv[NY + EY :]
    packages = (
        (jnp.where(odd, weight[100:125], weight[:25]), slots),
        (pulled, slots),
        (theirs[:25], theirs[PACK - 1 :]),
    )
    for group, (rows, slots) in enumerate(packages):
        eights = jnp.floor(slots * 0.125)
        package = [rows, jnp.zeros((PACK - 27, CAP), FP), eights, slots - 8.0 * eights]
        at = PACK_AT + 2 * PACK * group
        msg_ref[at : at + 2 * PACK] = jnp.concatenate(parts_of(jnp.concatenate(package, 0), 2), 0)


def inner_finish(odd, base, now, g_now, inner, sx, share, tent_ref, msg_ref):
    even_part = jnp.where(odd, 0.0, sx * inner)
    tent = []
    for k in range(4):
        value = base[k] - float(AB[k, 4]) * even_part
        if k == 0:
            value = value - jnp.where(odd, inner, 0.0)
            if share is not None:
                value = value - share
        tent_ref[k] = value
        tent.append(value)
    msg_ref[:NY] = jnp.where(odd, g_now, now[0]).astype(jnp.bfloat16)
    msg_ref[NY : 2 * NY] = jnp.where(odd, to_right(sx, tent), tent[0]).astype(jnp.bfloat16)


def inner_kernel(par, base, now, g_now, recv, coef, tent_ref, msg_ref):
    odd = par[0] == 1
    inner_finish(odd, base, now, g_now[...], recv[...], coef[4], None, tent_ref, msg_ref)


def outer_finish(odd, tent, sx, sx_left, recv0, recv1, g_own, u0_own, share, refs):
    u_ref, msg_ref, outer_ref = refs
    odd_part = jnp.where(odd, sx * recv0, 0.0)
    values = []
    for k in range(4):
        value = tent[k] - float(AB[k, 4]) * odd_part
        if k == 0:
            lost = recv0 if share is None else recv0 + share
            value = value - jnp.where(odd, 0.0, lost)
        u_ref[k] = value
        values.append(value)
    msg_ref[...] = jnp.where(odd, values[0], to_right(sx, values))
    mine = g_own if share is None else g_own + share
    outer_ref[...] = recv1 - jnp.where(odd, mine, KAPPA * sx_left * sx_left * u0_own)


def outer_first_kernel(
    par, tent, now, first, recv, inner, coef, cleft, left, right, over, mat_z,
    u_ref, msg_ref, outer_ref, coef0_ref, sxl_ref, last_ref, pad,
):
    odd = par[0] == 1
    parts = jnp.concatenate([recv[2 * NY : PACK_AT, :EZ], jnp.zeros((EY, EZ), jnp.bfloat16)], 0)
    theirs = expand_speed(parts, left[...], right[...], over[...])
    coefs = [jnp.where(odd, coef[i], theirs[i]) for i in range(5)]
    recv0 = recv[:NY].astype(FP)
    plane = jnp.where(odd, recv0, now[0])
    share = half_left(plane, coefs, mat_z, pad)
    on_left = [jnp.where(odd, cleft[i], theirs[i]) for i in range(5)]
    for i in range(4):
        coef0_ref[i] = 0.5 * (coef[i] + on_left[i])
    coef0_ref[4] = float(AB[4, 4]) * on_left[4]
    sxl_ref[...] = on_left[4]
    last_ref[...] = jnp.where(odd, recv0, inner[:NY])
    outer_finish(
        odd, tent, coef[4], on_left[4], recv0, recv[NY : 2 * NY].astype(FP), first[...], now[0], share,
        (u_ref, msg_ref, outer_ref),
    )


def outer_kernel(par, tent, now, g_now, recv, inner, coef, sxl, u_ref, msg_ref, outer_ref, last_ref):
    odd = par[0] == 1
    recv0 = recv[:NY].astype(FP)
    last_ref[...] = jnp.where(odd, recv0, inner[...])
    outer_finish(
        odd, tent, coef[4], sxl[...], recv0, recv[NY:].astype(FP), g_now[...], now[0], None,
        (u_ref, msg_ref, outer_ref),
    )


def both_kernel(par, base, inner, outer, coef, u_ref, g_ref, msg_ref, last_ref):
    odd = par[0] == 1
    last = jnp.where(odd, outer[...], inner[...])
    from_left = jnp.where(odd, inner[...], outer[...])
    sx = coef[4]
    pull = sx * last
    values = []
    for k in range(4):
        value = base[k] - float(AB[k, 4]) * pull
        if k == 0:
            value = value - from_left
        u_ref[k] = value
        values.append(value)
    g = to_right(sx, values)
    g_ref[...] = g
    msg_ref[...] = jnp.where(odd, values[0], g)
    last_ref[...] = last


def outer_last_kernel(par, tent, now, g_now, recv, inner, coef, sxl, u_ref, msg_ref, outer_ref):
    outer_finish(
        par[0] == 1, tent, coef[4], sxl[...], recv[:NY].astype(FP), recv[NY:].astype(FP), g_now[...],
        now[0], None,
        (u_ref, msg_ref, outer_ref),
    )


def pick_nodes(ez, pick_ref):
    z = lax.broadcasted_iota(jnp.int32, (NZ, CAP), 0)
    for c in range(5):
        hot = (z == 4 * ez + c).astype(FP).astype(jnp.bfloat16)
        for half in range(2):
            pick_ref[half * NZ : (half + 1) * NZ, c * CAP : (c + 1) * CAP] = hot


def y_masks(ey):
    y = lax.broadcasted_iota(jnp.int32, (NY, CAP), 0)
    masks = []
    for b in range(5):
        row = 4 * ey + b
        masks.append(y == jnp.where(row >= NY, row - NY, row))
    return masks


def spread_nodes(masks, weight, c):
    total = jnp.zeros((NY, CAP), FP)
    for b in range(5):
        total = jnp.where(masks[b], weight[5 * b + c : 5 * b + c + 1, :], total)
    return total


def slots_kernel(elem, weight, pick_ref, spread_ref):
    ey = elem[...] // EZ
    pick_nodes(elem[...] - ey * EZ, pick_ref)
    masks = y_masks(ey)
    for a in range(5):
        plane = weight[25 * a : 25 * a + 25, :]
        for c in range(5):
            spread_ref[c, a * NY : (a + 1) * NY, :] = spread_nodes(masks, plane, c)


def others_kernel(par, inner, outer, pick_l_ref, pick_2_ref, spread_ref):
    odd = par[0] == 1
    from_inner = inner[NY + EY :]
    halves = [
        outer[PACK_AT + PACK * i : PACK_AT + PACK * (i + 1)].astype(FP) for i in range(6)
    ]
    from_outer, pulled, relayed = (halves[2 * i] + halves[2 * i + 1] for i in range(3))
    pulled = jnp.where(odd, 0.0, pulled)

    def number(package):
        return 8.0 * package[PACK - 2 : PACK - 1] + package[PACK - 1 :]

    groups = (
        (
            jnp.where(odd, from_inner[:25], from_outer[:25]),
            jnp.where(odd, from_inner[PACK - 1 :], number(from_outer)),
            pick_l_ref,
        ),
        (
            jnp.where(odd, from_outer[:25], relayed[:25]),
            jnp.where(odd, number(from_outer), number(relayed)),
            pick_2_ref,
        ),
    )
    for group, (rows, elem, pick_ref) in enumerate(groups):
        elem = elem.astype(jnp.int32)
        ey = elem // EZ
        pick_nodes(elem - ey * EZ, pick_ref)
        masks = y_masks(ey)
        for c in range(5):
            spread_ref[2 * group, c] = spread_nodes(masks, rows, c)
            if group == 0:
                spread_ref[1, c] = spread_nodes(masks, pulled, c)


def picked(planes, pick):
    high, low = parts_of(jnp.concatenate(planes, 0), 2)
    return jnp.dot(
        jnp.concatenate([high, low], 1), pick[...], preferred_element_type=jnp.float32
    )


def weighted(got, spread):
    total = None
    for c in range(5):
        term = got[:, c * CAP : (c + 1) * CAP] * spread(c)
        total = term if total is None else total + term
    return jnp.sum(jnp.sum(total.reshape(-1, 8, CAP), 0), 0, keepdims=True)


def sample(planes, pick, spread):
    rows = NY * len(planes)
    return weighted(picked(planes, pick), lambda c: spread[c, :rows, :])


def all_planes(u, last):
    return [u[0], u[1], u[2], u[3], last]


def sample_first_kernel(u0, l0, u1, l1, u2, pick, spread, out):
    out[0:1, :] = sample(all_planes(u0, l0[...]), pick, spread)
    out[1:2, :] = sample(all_planes(u1, l1[...]), pick, spread)
    out[2:3, :] = sample([u2[k] for k in range(4)], pick, spread)


def sample_second_kernel(first, l2, u3, pick, spread, out):
    got = picked(all_planes(u3, l2[...]), pick)
    rest = 4 * NY
    out[0:2, :] = first[0:2, :]
    out[2:3, :] = first[2:3, :] + weighted(got[rest:], lambda c: spread[c, rest:, :])
    out[3:4, :] = weighted(got[:rest], lambda c: spread[c, :rest, :])


def sample_third_kernel(
    par, before, l3, u4, g, sxl, pick, spread, pick_l, pick_2, spread_o, out
):
    odd = par[0] == 1
    got = picked(all_planes(u4, l3[...]), pick)
    rest = 4 * NY
    face = u4[0]
    x = sxl[...] * face
    left = picked([x, face], pick_l)
    second = picked([jnp.where(odd, -g[...], -float(AB[0, 4]) * x)], pick_2)
    out[0:3, :] = before[0:3, :]
    out[3:4, :] = before[3:4, :] + weighted(got[rest:], lambda c: spread[c, rest:, :])
    out[4:5, :] = weighted(got[:rest], lambda c: spread[c, :rest, :])
    out[5:6, :] = weighted(left[:NY], lambda c: spread_o[1, c])
    out[6:7, :] = weighted(second, lambda c: spread_o[2, c])
    out[7:8, :] = jnp.where(odd, 0.0, weighted(left[NY:], lambda c: spread_o[0, c]))


def sample_last_kernel(
    par, before, inner, tent, g, pick, spread, pick_l, spread_o, out, block, sems
):
    odd = par[0] == 1
    own_g = jnp.where(odd, -g[...], 0.0)
    last = jnp.where(odd, 0.0, inner[...])
    got = picked(all_planes(tent, own_g) + [last], pick)
    face = picked([tent[0]], pick_l)
    rest = 4 * NY
    rows = [
        before[0:4, :],
        before[4:5, :] + weighted(got[5 * NY :], lambda c: spread[c, rest:, :]),
        weighted(got[: 5 * NY], lambda c: spread[c]),
        before[5:6, :] + weighted(face, lambda c: spread_o[0, c]),
        before[6:8, :],
    ]
    rows = jnp.concatenate(rows, 0)
    for i in range(8):
        block[ROWS * i : ROWS * (i + 1), :] = rows
    size = 8 * ROWS
    copies = [
        pltpu.make_async_copy(block, out.at[pl.ds(size * i, size), :], sems.at[i])
        for i in range(out.shape[0] // size)
    ]
    for copy in copies:
        copy.start()
    for copy in copies:
        copy.wait()


def stations_kernel(par, blocks, stations, row_ref, lane_ref):
    odd = par[0] == 1
    for j in range(2 * SB):
        wanted = blocks[0, j // SB] * SB + j % SB
        hit = jnp.zeros((8, CAP), FP)
        for r in range(16):
            hit = hit + jnp.where(stations[8 * r : 8 * r + 8, :] == wanted, 1.0, 0.0)
        lane_ref[j : j + 1, :] = jnp.sum(hit, 0, keepdims=True)
    lane = lane_ref[...]
    ids = stations[...].astype(FP)
    at = lax.dot_general(
        lane, ids, (((1,), (1,)), ((), ())), precision=HIGHEST, preferred_element_type=jnp.float32
    )
    j = lax.broadcasted_iota(jnp.int32, (2 * SB, 128), 0)
    wanted = jnp.where(j < SB, blocks[0, 0] * SB + j, blocks[0, 1] * SB + (j - SB))
    place = lax.broadcasted_iota(jnp.int32, (2 * SB, 128), 1)
    hit = jnp.where(jnp.abs(at - wanted.astype(FP)) < 0.5, place.astype(FP), 0.0)
    device = jnp.sum(hit, 1, keepdims=True).astype(jnp.int32)
    first = jnp.where(odd, 1, 0)

    def one_hot(device):
        device = jnp.bitwise_and(device, 127)
        side = jnp.where(jnp.bitwise_and(device, 1) == first, 0, 64)
        return jnp.where(place == side + jnp.right_shift(device, 1), 1.0, 0.0)

    row_ref[0] = one_hot(device)
    row_ref[1] = one_hot(device + 1)
    even = jnp.where(jnp.bitwise_and(device, 1) == 0, 1.0, 0.0)
    row_ref[2] = even * (one_hot(device + 2) + one_hot(device + 127))


def spectra_kernel(near, far, row, lane, table, out):
    slabs = [
        jnp.concatenate([half[pl.ds(t, 64, stride=ROWS), :] for half in (near, far)], 0)
        for t in range(ROWS)
    ]

    def select(which, slabs):
        hot = row[which].astype(jnp.bfloat16)
        parts = jnp.concatenate(parts_of(jnp.concatenate(slabs, 1), 2), 0)
        return jnp.dot(
            jnp.concatenate([hot, hot], 1), parts, preferred_element_type=jnp.float32
        )

    found = select(0, slabs[:6])
    more = select(1, [slabs[8], slabs[6]])
    last = select(2, [slabs[7]])
    found = [found[:, 128 * t : 128 * (t + 1)] for t in range(NT)]
    found[4] = found[4] + more[:, :128]
    found[5] = found[5] + more[:, 128:] + last
    at = lax.broadcasted_iota(jnp.int32, (2 * SB, 128), 1)
    samples = jnp.zeros((2 * SB, 128), FP)
    for t in range(NT):
        one = jnp.sum(found[t] * lane[...], 1, keepdims=True)
        samples = jnp.where(at % 8 == t, one, samples)
    parts = [part.astype(FP) for part in parts_of(samples, 3)]
    mixed = jnp.zeros((2 * SB, 128), FP)
    for group, (part, _) in enumerate(PART_PAIRS):
        mixed = jnp.where(at // 8 == group, parts[part], mixed)
    out[...] = lax.dot_general(
        table[...], mixed.astype(jnp.bfloat16), (((1,), (1,)), ((), ())),
        preferred_element_type=jnp.float32,
    ).astype(jnp.bfloat16)


def cross_kernel(
    par, base, inner, outer, coef, spectra_in, spread_a, spread_b, end, out, held_end, held, sems
):
    odd = par[0] == 1
    pull = coef[4] * jnp.where(odd, outer[...], inner[...])
    for k in range(4):
        value = base[k] - float(AB[k, 4]) * pull
        held_end[k] = value - jnp.where(odd, inner[...], outer[...]) if k == 0 else value
    copies = [pltpu.make_async_copy(held_end, end, sems.at[8])]
    copies[0].start()
    spectra = spectra_in[...]
    second = jnp.dot(spectra, spread_b[...], preferred_element_type=jnp.float32) * (1.0 / NT)
    b_re = second[:F]
    b_im = second[F:]
    for i in range(4):
        first = jnp.dot(
            spectra, spread_a[:, 256 * i : 256 * (i + 1)], preferred_element_type=jnp.float32
        )
        for half in range(2):
            at = 2 * i + half
            cols = slice(128 * at, 128 * (at + 1))
            a_re = first[:F, 128 * half : 128 * (half + 1)]
            a_im = first[F:, 128 * half : 128 * (half + 1)]
            held[0, :, cols] = (a_re * b_re + a_im * b_im).astype(jnp.bfloat16)
            held[1, :, cols] = (a_im * b_re - a_re * b_im).astype(jnp.bfloat16)
            copy = pltpu.make_async_copy(held.at[:, :, cols], out.at[0, :, :, cols], sems.at[at])
            copy.start()
            copies.append(copy)
    for copy in copies:
        copy.wait()


def body(
    now, vel, speed_sq, src, wavelet, slot_elem, slot_station, slot_weight, pair_blocks, devices
):
    inner_route = [(i, i ^ 1) for i in range(devices)]
    outer_route = [(i, (i + 1 if i % 2 else i - 1) % devices) for i in range(devices)]

    def swap_inner(x):
        return lax.ppermute(x, AXES, inner_route)

    def swap_outer(x):
        return lax.ppermute(x, AXES, outer_route)

    mat_z, left, right, over = (jnp.asarray(x) for x in tables())
    table = jnp.asarray(dft_table())
    reps = np.zeros((2 * SB, SB * SB))
    for i in range(SB):
        reps[i, i * SB : (i + 1) * SB] = 1.0
    tiles = np.zeros((2 * SB, 128))
    for i in range(128):
        tiles[SB + i % SB, i] = 1.0
    reps = jnp.asarray(reps, jnp.bfloat16)
    tiles = jnp.asarray(tiles, jnp.bfloat16)
    pads = (pltpu.VMEM((4, NY + 16, NZ), FP),)
    one_pad = (pltpu.VMEM((1, NY + 16, NZ), FP),)

    par = lax.axis_index("core").astype(jnp.int32).reshape(1)

    inputs = (
        now, vel, src, speed_sq, left, right, over, mat_z, slot_elem.reshape(1, CAP), slot_weight,
        wavelet.reshape(1, NT),
    )
    kept = [jax.ShapeDtypeStruct(x.shape, x.dtype) for x in inputs]
    kept[3] = jax.ShapeDtypeStruct((EY, EZ), FP)
    now, vel, src, speed, left, right, over, mat_z, elem, weight, wavelet, msg = call(
        start_kernel,
        [(x.shape, x.dtype) for x in kept] + [((NY + EY + PACK, NZ), FP)],
        (par, *(in_hbm(x) for x in inputs)), "start",
        specs=[SMEM] + [HBM] * len(inputs), scratch=(pltpu.SemaphoreType.DMA((len(inputs),)),),
    )
    inner0 = swap_inner(msg)
    base, coef, g0 = call(
        base_first_kernel, [(FOUR, FP), (FIVE, FP), (PLANE, FP)],
        (wavelet, now, vel, src, speed, left, right, over, mat_z), "base0", scratch=pads,
    )
    tent, msg, cleft = call(
        inner_first_kernel,
        [(FOUR, FP), ((PACK_AT + 6 * PACK, NZ), jnp.bfloat16), (FIVE, FP)],
        (par, base, now, g0, inner0, speed, elem, weight, coef, left, right, over, mat_z), "inner0", 1,
        scratch=one_pad,
    )
    outer0 = swap_outer(msg)
    pick_shape = ((2 * NZ, 5 * CAP), jnp.bfloat16)
    pick, spread = call(slots_kernel, [pick_shape, ((5, 5 * NY, CAP), FP)], (elem, weight), "slots")
    row, lane = call(
        stations_kernel, [((3, 2 * SB, 128), FP), ((2 * SB, CAP), FP)],
        (par, pair_blocks, slot_station.reshape(128, CAP)), "stations", 2,
    )
    outer0, pick, spread, row, lane = lax.optimization_barrier((outer0, pick, spread, row, lane))
    u1, msg, outer, coef0, sxl, last0 = call(
        outer_first_kernel,
        [(FOUR, FP), (PLANE, FP), (PLANE, FP), (FIVE, FP), (PLANE, FP), (PLANE, FP)],
        (par, tent, now, g0, outer0, inner0, coef, cleft, left, right, over, mat_z), "outer0", 1,
        scratch=one_pad,
    )

    def base_of(step, u, before):
        return call(
            functools.partial(base_kernel, step), [(FOUR, FP)],
            (wavelet, u, before, src, coef, coef0, mat_z), "base", scratch=pads,
        )[0]

    def two_steps(step, u_b, u_a, msg, outer, fill=(None, None)):
        inner = swap_inner(msg)
        base = base_of(step, u_b, u_a)
        more = None
        if fill[0]:
            inner, base, more = lax.optimization_barrier((inner, base, fill[0]()))
        u_c, g, msg, last = call(
            both_kernel, [(FOUR, FP), (PLANE, FP), (PLANE, FP), (PLANE, FP)],
            (par, base, inner, outer, coef), "both", 1,
        )
        inner = swap_inner(msg)
        base = base_of(step + 1, u_c, u_b)
        if fill[1]:
            inner, base, more = lax.optimization_barrier((inner, base, fill[1](more, u_c, g, last)))
        tent, msg = call(
            inner_kernel, [(FOUR, FP), ((2 * NY, NZ), jnp.bfloat16)],
            (par, base, u_c, g, inner, coef), "inner", 1,
        )
        return u_c, g, last, inner, tent, msg, more

    def complete(tent, u, g, recv, inner):
        return call(
            outer_kernel, [(FOUR, FP), (PLANE, FP), (PLANE, FP), (PLANE, FP)],
            (par, tent, u, g, recv, inner, coef, sxl), "outer", 1,
        )

    u2, g2, last1, inner2, tent, msg, _ = two_steps(1, u1, now, msg, outer)
    recv = swap_outer(msg)
    (rows,) = call(
        sample_first_kernel, [((3, CAP), FP)], (now, last0, u1, last1, u2, pick, spread), "sample3"
    )
    others = call(
        others_kernel, [pick_shape, pick_shape, ((3, 5, NY, CAP), FP)], (par, inner0, outer0), "others", 1
    )
    recv, rows, *others = lax.optimization_barrier((recv, rows, *others))
    u3, msg, outer, last2 = complete(tent, u2, g2, recv, inner2)

    def second_rows():
        return call(
            sample_second_kernel, [((4, CAP), FP)], (rows, last2, u3, pick, spread), "sample5"
        )[0]

    def third_rows(before, u, g, last):
        return call(
            sample_third_kernel, [((8, CAP), FP)],
            (par, before, last, u, g, sxl, pick, spread, *others), "sample8", 1,
        )[0]

    u4, g4, _, inner4, tent, msg, rows = two_steps(3, u3, u2, msg, outer, (second_rows, third_rows))
    pick_l, _, spread_o = others
    (mine,) = call(
        sample_last_kernel, [((devices // 2 * ROWS, CAP), FP)],
        (par, rows, inner4, tent, g4, pick, spread, pick_l, spread_o), "sample7", 1,
        out_specs=[HBM],
        scratch=(
            pltpu.VMEM((8 * ROWS, CAP), FP), pltpu.SemaphoreType.DMA((devices // 16,)),
        ),
    )
    near = lax.all_to_all(
        mine.reshape(devices // 2, 1, ROWS * CAP), ("pair", "chip"), 0, 0, tiled=True
    ).reshape(devices // 2 * ROWS, CAP)
    recv = swap_outer(msg)
    recv, near = lax.optimization_barrier((recv, near))
    far = swap_inner(near)
    u5, msg, outer = call(
        outer_last_kernel, [(FOUR, FP), (PLANE, FP), (PLANE, FP)],
        (par, tent, u4, g4, recv, inner4, coef, sxl), "outer", 1,
    )
    inner = swap_inner(msg)
    base = base_of(5, u5, u4)
    (spectra,) = call(
        spectra_kernel, [((2 * F, 2 * SB), jnp.bfloat16)],
        (near, far, row, lane, table), "spectra",
    )
    inner, base, spectra = lax.optimization_barrier((inner, base, spectra))
    end, cross = call(
        cross_kernel, [(FOUR, FP), ((1, 2, F, SB * SB), jnp.bfloat16)],
        (par, base, inner, outer, coef, spectra, reps, tiles), "cross", 1,
        out_specs=[HBM, HBM],
        scratch=(
            pltpu.VMEM(FOUR, FP), pltpu.VMEM((2, F, SB * SB), jnp.bfloat16),
            pltpu.SemaphoreType.DMA((9,)),
        ),
    )
    return end, cross


def solution(mesh):
    split = P(AXES)
    in_specs = (
        P(AXES, None, None), P(AXES, None, None), P(AXES, None, None), P(AXES, None, None),
        P(), split, P(), P(None, AXES), P(AXES, None),
    )
    out_specs = (P(AXES, None, None), P(AXES, None, None, None))
    grid = mesh.devices.reshape(mesh.shape["pair"], -1, 2)
    mesh = jax.sharding.Mesh(grid, AXES)
    devices = grid.size
    run = functools.partial(body, devices=devices)
    return jax.shard_map(run, mesh=mesh, in_specs=in_specs, out_specs=out_specs, check_vma=False)
```

```python
import functools
import math

import jax
import jax.numpy as jnp
import numpy as np
from jax import lax
from jax.experimental import pallas as pl
from jax.experimental.pallas import tpu as pltpu
from jax.sharding import PartitionSpec as P

NT = 6
F = 256
SB = 32
STEP_DT = 0.04
NY = 96
NZ = 128
EY = 24
EZ = 32
CAP = 128
AXES = ("pair", "chip", "core")
HIGHEST = lax.Precision.HIGHEST
W1 = np.array([0.1, 49.0 / 90.0, 32.0 / 45.0, 49.0 / 90.0, 0.1])


def stiffness_1d():
    points = np.array([-1.0, -math.sqrt(3.0 / 7.0), 0.0, math.sqrt(3.0 / 7.0), 1.0])
    factor = np.array(
        [np.prod([points[i] - points[j] for j in range(5) if j != i]) for i in range(5)]
    )
    d = np.zeros((5, 5))
    for i in range(5):
        for j in range(5):
            if i != j:
                d[i, j] = factor[i] / (factor[j] * (points[i] - points[j]))
        d[i, i] = -np.sum(d[i])
    return d.T @ np.diag(W1) @ d


A = stiffness_1d()
MX = np.array([0.2, W1[1], W1[2], W1[3], 0.2])
AB = A / MX[:, None]
KAPPA = float(sum(AB[4, k] * AB[k, 4] for k in range(4)))


def f32(x):
    return np.asarray(x, np.float32)


def tables():
    my = np.array([MX[y % 4] for y in range(NY)])
    mz = np.array([0.1 if z == 0 else MX[z % 4] for z in range(NZ)])
    mat_z = np.zeros((NZ, 2 * NZ))
    for z in range(NZ):
        e, c = divmod(z, 4)
        for m in range(5):
            if 4 * e + m < NZ:
                mat_z[4 * e + m, z] += A[c, m]
            if c == 0 and e > 0:
                mat_z[4 * (e - 1) + m, NZ + z] += A[4, m]
    left = np.zeros((3 * NY, EY))
    for y in range(NY):
        e, b = divmod(y, 4)
        left[y, e] += W1[b]
        left[NY + y, e] += 1.0
        if b == 0:
            left[y, (e - 1) % EY] += W1[4]
            left[2 * NY + y, (e - 1) % EY] += 1.0
    left[:NY] /= my[:, None]
    right = np.zeros((EZ, 3 * NZ))
    for z in range(NZ):
        e, c = divmod(z, 4)
        right[e, z] += 1.0
        right[e, 2 * NZ + z] += W1[c]
        if c == 0 and e > 0:
            right[e - 1, NZ + z] += 1.0
            right[e - 1, 2 * NZ + z] += W1[4]
    right[:, 2 * NZ :] /= mz[None, :]
    over_z = np.broadcast_to(1.0 / mz, (8, NZ)) * (STEP_DT * STEP_DT)
    over_y = np.broadcast_to(1.0 / my[:8, None], (8, NZ)) * (STEP_DT * STEP_DT)
    left = np.tile(left, (1, 3)).astype(jnp.bfloat16)
    right = np.tile(right, (3, 1)).astype(jnp.bfloat16)
    high = mat_z.astype(jnp.bfloat16).astype(np.float64)
    low = (mat_z - high).astype(jnp.bfloat16)
    stack = np.concatenate([mat_z, mat_z], 0).astype(jnp.bfloat16)
    return np.concatenate([stack, low], 0), left, right, f32(np.concatenate([over_y, over_z], 0))


PART_PAIRS = ((0, 0), (1, 0), (0, 1), (1, 1), (2, 0), (0, 2))


def parts_of(x, count):
    parts = []
    for _ in range(count):
        part = x.astype(jnp.bfloat16)
        parts.append(part)
        x = x - part.astype(x.dtype)
    return parts


def dft_table():
    angle = np.pi * (np.arange(F) + 0.5) / F
    phase = angle[:, None] * np.arange(NT)[None, :]
    parts = parts_of(f32(np.concatenate([np.cos(phase), -np.sin(phase)], 0)), 3)
    table = np.zeros((2 * F, 128), jnp.bfloat16)
    for group, (_, part) in enumerate(PART_PAIRS):
        table[:, 8 * group : 8 * group + NT] = parts[part]
    return table


def dot(a, b):
    return jnp.dot(a, b, precision=HIGHEST, preferred_element_type=jnp.float32)


VMEM = pl.BlockSpec(memory_space=pltpu.VMEM)
SMEM = pl.BlockSpec(memory_space=pltpu.SMEM)
HBM = pl.BlockSpec(memory_space=pltpu.HBM)


def call(kernel, outs, args, name, smem=0, specs=None, out_specs=None, scratch=(), flops=4_000_000):
    return pl.pallas_call(
        kernel,
        out_shape=[jax.ShapeDtypeStruct(s, d) for s, d in outs],
        in_specs=specs or [SMEM] * smem + [VMEM] * (len(args) - smem),
        out_specs=out_specs or [VMEM] * len(outs),
        scratch_shapes=list(scratch),
        compiler_params=pltpu.CompilerParams(vmem_limit_bytes=24 * 1024 * 1024),
        cost_estimate=pl.CostEstimate(flops=flops, bytes_accessed=1_000_000, transcendentals=0),
        name=name,
    )(*args)


def in_hbm(x):
    return pltpu.with_memory_space_constraint(x, pltpu.HBM)


PACK = 32
ROWS = 9
PACK_AT = 2 * NY + 2 * EY
PLANE = (NY, NZ)
FOUR = (4, NY, NZ)
FIVE = (5, NY, NZ)
FP = jnp.float32


def expand_speed(parts, left, right, over):
    rows = jnp.dot(left, parts, preferred_element_type=jnp.float32)
    parts = jnp.concatenate(parts_of(rows, 3), 1)
    by_z = jnp.dot(parts[:NY], right, preferred_element_type=jnp.float32)
    by_y = jnp.dot(parts[NY:], right[:, 2 * NZ :], preferred_element_type=jnp.float32)
    over_y = jnp.concatenate([over[:8]] * (NY // 8), 0)
    over_z = over[8:9]
    return (
        by_z[:, :NZ] * over_z, by_z[:, NZ : 2 * NZ] * over_z, by_y[:NY] * over_y, by_y[NY:] * over_y,
        by_z[:, 2 * NZ :] * (STEP_DT * STEP_DT),
    )


def speed_parts(speed, count=3):
    return jnp.concatenate(parts_of(speed, count), 0)


def along_z(u, mat_z):
    high, low = parts_of(u, 2)
    return jnp.dot(
        jnp.concatenate([high, low], 1), mat_z[: 2 * NZ], preferred_element_type=jnp.float32
    ) + jnp.dot(high, mat_z[2 * NZ :], preferred_element_type=jnp.float32)


def y_patterns():
    b = lax.broadcasted_iota(jnp.int32, (8, NZ), 0) % 4
    own, before = {}, {}
    for d in range(-4, 5):
        total = jnp.zeros((8, NZ), FP)
        for row in range(4):
            if 0 <= row + d <= 4:
                total = jnp.where(b == row, float(A[row, row + d]), total)
        own[d] = total
        if d <= 0:
            before[d] = jnp.where(b == 0, float(A[4, 4 + d]), 0.0)
    return own, before


def y_coefs(y1, y2, patterns):
    own, before = patterns
    return {d: y1 * own[d] + y2 * before[d] if d in before else y1 * own[d] for d in own}


def wrap_rows(pad, at, plane):
    pad[at, 8 : 8 + NY, :] = plane
    pad[at, 4:8, :] = plane[NY - 4 :]
    pad[at, 8 + NY : 12 + NY, :] = plane[:4]


def along_y(pad, at, row, coefs):
    total = None
    for d, c in coefs.items():
        term = c * pad[at, 8 + row + d : 16 + row + d, :]
        total = term if total is None else total + term
    return total


def to_right(sx, u):
    total = float(AB[4, 0]) * u[0]
    for m in range(1, 4):
        total = total + float(AB[4, m]) * u[m]
    return sx * total


def start_kernel(
    par, now_in, vel_in, src_in, speed_in, left_in, right_in, over_in, mat_in, elem_in, weight_in, wave_in,
    now, vel, src, speed, left, right, over, mat, elem, weight, wave, msg_ref, sems,
):
    pairs = (
        (now_in, now), (speed_in.at[0], speed), (elem_in, elem), (weight_in, weight), (vel_in, vel),
        (src_in, src), (left_in, left), (right_in, right), (over_in, over), (mat_in, mat), (wave_in, wave),
    )
    copies = [pltpu.make_async_copy(a, b, sems.at[i]) for i, (a, b) in enumerate(pairs)]
    for copy in copies:
        copy.start()
    msg_ref[NY:] = jnp.zeros((EY + PACK, NZ), FP)
    copies[0].wait()
    msg_ref[:NY] = jnp.where(par[0] == 1, now[0], to_right(1.0, [now[k] for k in range(4)]))
    for copy in copies[1:4]:
        copy.wait()
    msg_ref[NY : NY + EY, :EZ] = speed[...]
    msg_ref[NY + EY : NY + EY + 25] = weight[100:125]
    msg_ref[NY + EY + PACK - 1 :] = elem[...].astype(FP)
    for copy in copies[4:]:
        copy.wait()


def base_first_kernel(
    wave, now, vel, src, speed, left, right, over, mat_z, out, coef_ref, first_ref, pad
):
    coefs = expand_speed(speed_parts(speed[...]), left[...], right[...], over[...])
    for i in range(5):
        coef_ref[i] = coefs[i]
    first_ref[...] = to_right(coefs[4], [now[k] for k in range(4)])
    base_body(0, wave, now, None, vel, src, coef_ref, None, mat_z, out, pad)


def base_body(step, wave, now, prev, vel, src, coef, coef0, mat_z, out, pad):
    scale = jnp.broadcast_to(wave[:, step : step + 1] * (STEP_DT * STEP_DT), (8, NZ))
    by_z = along_z(now[...].reshape(4 * NY, NZ), mat_z)
    patterns = y_patterns()
    for k in range(4):
        wrap_rows(pad, k, now[k])
    for row in range(0, NY, 8):
        at = slice(row, row + 8)
        u = [now[k, at, :] for k in range(4)]
        sx = coef[4, at, :]
        own = [coef[i, at, :] for i in range(4)]
        first = own if coef0 is None else [coef0[i, at, :] for i in range(4)]
        cy = y_coefs(own[2], own[3], patterns)
        cy0 = cy if coef0 is None else y_coefs(first[2], first[3], patterns)
        for k in range(4):
            c = own if k else first
            z = by_z[NY * k + row : NY * k + row + 8]
            force = c[0] * z[:, :NZ] + c[1] * z[:, NZ:] + along_y(pad, k, row, cy if k else cy0)
            if k == 0:
                force = 0.5 * force if coef0 is None else force + coef0[4, at, :] * u[0]
            mix = float(AB[k, 0]) * u[0]
            for m in range(1, 4):
                mix = mix + float(AB[k, m]) * u[m]
            force = scale * src[k, at, :] - (force + sx * mix)
            if prev is None:
                out[k, at, :] = u[k] + STEP_DT * vel[k, at, :] + force
            else:
                out[k, at, :] = 2.0 * u[k] - prev[k, at, :] + force


def base_kernel(step, wave, now, prev, src, coef, coef0, mat_z, out, pad):
    base_body(step, wave, now, prev, None, src, coef, coef0, mat_z, out, pad)


def half_left(plane, coefs, mat_z, pad):
    by_z = along_z(plane, mat_z)
    wrap_rows(pad, 0, plane)
    patterns = y_patterns()
    tiles = []
    for row in range(0, NY, 8):
        c = [x[row : row + 8] for x in coefs]
        by_y = along_y(pad, 0, row, y_coefs(c[2], c[3], patterns))
        z = by_z[row : row + 8]
        tiles.append(0.5 * (c[0] * z[:, :NZ] + c[1] * z[:, NZ:] + by_y))
    return jnp.concatenate(tiles, 0) + float(AB[4, 4]) * (coefs[4] * plane)


def inner_first_kernel(
    par, base, now, first, recv, speed, elem, weight, coef, left, right, over, mat_z,
    tent_ref, msg_ref, cleft_ref, pad,
):
    odd = par[0] == 1
    their_speed = jnp.where(odd, recv[NY : NY + EY, :EZ], 0.0)
    coefs = expand_speed(speed_parts(their_speed), left[...], right[...], over[...])
    for i in range(5):
        cleft_ref[i] = coefs[i]
    share = half_left(now[0], coefs, mat_z, pad)
    inner = jnp.where(odd, coefs[4] * recv[:NY], recv[:NY])
    inner_finish(odd, base, now, first[...], inner, coef[4], share, tent_ref, msg_ref)
    own_speed = jnp.concatenate([speed[...], jnp.zeros((EY, NZ - EZ), FP)], 1)
    msg_ref[2 * NY : PACK_AT] = speed_parts(own_speed, 2)
    pulled = -float(AB[0, 4]) * weight[:25]
    for k in range(1, 4):
        pulled = pulled - float(AB[k, 4]) * weight[25 * k : 25 * k + 25]
    slots = elem[...].astype(FP)
    theirs = recv[NY + EY :]
    packages = (
        (jnp.where(odd, weight[100:125], weight[:25]), slots),
        (pulled, slots),
        (theirs[:25], theirs[PACK - 1 :]),
    )
    for group, (rows, slots) in enumerate(packages):
        eights = jnp.floor(slots * 0.125)
        package = [rows, jnp.zeros((PACK - 27, CAP), FP), eights, slots - 8.0 * eights]
        at = PACK_AT + 2 * PACK * group
        msg_ref[at : at + 2 * PACK] = jnp.concatenate(parts_of(jnp.concatenate(package, 0), 2), 0)


def inner_finish(odd, base, now, g_now, inner, sx, share, tent_ref, msg_ref):
    even_part = jnp.where(odd, 0.0, sx * inner)
    tent = []
    for k in range(4):
        value = base[k] - float(AB[k, 4]) * even_part
        if k == 0:
            value = value - jnp.where(odd, inner, 0.0)
            if share is not None:
                value = value - share
        tent_ref[k] = value
        tent.append(value)
    msg_ref[:NY] = jnp.where(odd, g_now, now[0]).astype(jnp.bfloat16)
    msg_ref[NY : 2 * NY] = jnp.where(odd, to_right(sx, tent), tent[0]).astype(jnp.bfloat16)


def inner_kernel(par, base, now, g_now, recv, coef, tent_ref, msg_ref):
    odd = par[0] == 1
    inner_finish(odd, base, now, g_now[...], recv[...], coef[4], None, tent_ref, msg_ref)


def outer_finish(odd, tent, sx, sx_left, recv0, recv1, g_own, u0_own, share, refs):
    u_ref, msg_ref, outer_ref = refs
    odd_part = jnp.where(odd, sx * recv0, 0.0)
    values = []
    for k in range(4):
        value = tent[k] - float(AB[k, 4]) * odd_part
        if k == 0:
            lost = recv0 if share is None else recv0 + share
            value = value - jnp.where(odd, 0.0, lost)
        u_ref[k] = value
        values.append(value)
    msg_ref[...] = jnp.where(odd, values[0], to_right(sx, values))
    mine = g_own if share is None else g_own + share
    outer_ref[...] = recv1 - jnp.where(odd, mine, KAPPA * sx_left * sx_left * u0_own)


def outer_first_kernel(
    par, tent, now, first, recv, inner, coef, cleft, left, right, over, mat_z,
    u_ref, msg_ref, outer_ref, coef0_ref, sxl_ref, last_ref, pad,
):
    odd = par[0] == 1
    parts = jnp.concatenate([recv[2 * NY : PACK_AT, :EZ], jnp.zeros((EY, EZ), jnp.bfloat16)], 0)
    theirs = expand_speed(parts, left[...], right[...], over[...])
    coefs = [jnp.where(odd, coef[i], theirs[i]) for i in range(5)]
    recv0 = recv[:NY].astype(FP)
    plane = jnp.where(odd, recv0, now[0])
    share = half_left(plane, coefs, mat_z, pad)
    on_left = [jnp.where(odd, cleft[i], theirs[i]) for i in range(5)]
    for i in range(4):
        coef0_ref[i] = 0.5 * (coef[i] + on_left[i])
    coef0_ref[4] = float(AB[4, 4]) * on_left[4]
    sxl_ref[...] = on_left[4]
    last_ref[...] = jnp.where(odd, recv0, inner[:NY])
    outer_finish(
        odd, tent, coef[4], on_left[4], recv0, recv[NY : 2 * NY].astype(FP), first[...], now[0], share,
        (u_ref, msg_ref, outer_ref),
    )


def outer_kernel(par, tent, now, g_now, recv, inner, coef, sxl, u_ref, msg_ref, outer_ref, last_ref):
    odd = par[0] == 1
    recv0 = recv[:NY].astype(FP)
    last_ref[...] = jnp.where(odd, recv0, inner[...])
    outer_finish(
        odd, tent, coef[4], sxl[...], recv0, recv[NY:].astype(FP), g_now[...], now[0], None,
        (u_ref, msg_ref, outer_ref),
    )


def both_kernel(par, base, inner, outer, coef, u_ref, g_ref, msg_ref, last_ref):
    odd = par[0] == 1
    last = jnp.where(odd, outer[...], inner[...])
    from_left = jnp.where(odd, inner[...], outer[...])
    sx = coef[4]
    pull = sx * last
    values = []
    for k in range(4):
        value = base[k] - float(AB[k, 4]) * pull
        if k == 0:
            value = value - from_left
        u_ref[k] = value
        values.append(value)
    g = to_right(sx, values)
    g_ref[...] = g
    msg_ref[...] = jnp.where(odd, values[0], g)
    last_ref[...] = last


def outer_last_kernel(par, tent, now, g_now, recv, inner, coef, sxl, u_ref, msg_ref, outer_ref):
    outer_finish(
        par[0] == 1, tent, coef[4], sxl[...], recv[:NY].astype(FP), recv[NY:].astype(FP), g_now[...],
        now[0], None,
        (u_ref, msg_ref, outer_ref),
    )


def pick_nodes(ez, pick_ref):
    z = lax.broadcasted_iota(jnp.int32, (NZ, CAP), 0)
    for c in range(5):
        hot = (z == 4 * ez + c).astype(FP).astype(jnp.bfloat16)
        for half in range(2):
            pick_ref[half * NZ : (half + 1) * NZ, c * CAP : (c + 1) * CAP] = hot


def y_masks(ey):
    y = lax.broadcasted_iota(jnp.int32, (NY, CAP), 0)
    masks = []
    for b in range(5):
        row = 4 * ey + b
        masks.append(y == jnp.where(row >= NY, row - NY, row))
    return masks


def spread_nodes(masks, weight, c):
    total = jnp.zeros((NY, CAP), FP)
    for b in range(5):
        total = jnp.where(masks[b], weight[5 * b + c : 5 * b + c + 1, :], total)
    return total


def slots_kernel(elem, weight, pick_ref, spread_ref):
    ey = elem[...] // EZ
    pick_nodes(elem[...] - ey * EZ, pick_ref)
    masks = y_masks(ey)
    for a in range(5):
        plane = weight[25 * a : 25 * a + 25, :]
        for c in range(5):
            spread_ref[c, a * NY : (a + 1) * NY, :] = spread_nodes(masks, plane, c)


def others_kernel(par, inner, outer, pick_l_ref, pick_2_ref, spread_ref):
    odd = par[0] == 1
    from_inner = inner[NY + EY :]
    halves = [
        outer[PACK_AT + PACK * i : PACK_AT + PACK * (i + 1)].astype(FP) for i in range(6)
    ]
    from_outer, pulled, relayed = (halves[2 * i] + halves[2 * i + 1] for i in range(3))
    pulled = jnp.where(odd, 0.0, pulled)

    def number(package):
        return 8.0 * package[PACK - 2 : PACK - 1] + package[PACK - 1 :]

    groups = (
        (
            jnp.where(odd, from_inner[:25], from_outer[:25]),
            jnp.where(odd, from_inner[PACK - 1 :], number(from_outer)),
            pick_l_ref,
        ),
        (
            jnp.where(odd, from_outer[:25], relayed[:25]),
            jnp.where(odd, number(from_outer), number(relayed)),
            pick_2_ref,
        ),
    )
    for group, (rows, elem, pick_ref) in enumerate(groups):
        elem = elem.astype(jnp.int32)
        ey = elem // EZ
        pick_nodes(elem - ey * EZ, pick_ref)
        masks = y_masks(ey)
        for c in range(5):
            spread_ref[2 * group, c] = spread_nodes(masks, rows, c)
            if group == 0:
                spread_ref[1, c] = spread_nodes(masks, pulled, c)


def picked(planes, pick):
    high, low = parts_of(jnp.concatenate(planes, 0), 2)
    return jnp.dot(
        jnp.concatenate([high, low], 1), pick[...], preferred_element_type=jnp.float32
    )


def weighted(got, spread):
    total = None
    for c in range(5):
        term = got[:, c * CAP : (c + 1) * CAP] * spread(c)
        total = term if total is None else total + term
    return jnp.sum(jnp.sum(total.reshape(-1, 8, CAP), 0), 0, keepdims=True)


def sample(planes, pick, spread):
    rows = NY * len(planes)
    return weighted(picked(planes, pick), lambda c: spread[c, :rows, :])


def all_planes(u, last):
    return [u[0], u[1], u[2], u[3], last]


def sample_first_kernel(u0, l0, u1, l1, u2, pick, spread, out):
    out[0:1, :] = sample(all_planes(u0, l0[...]), pick, spread)
    out[1:2, :] = sample(all_planes(u1, l1[...]), pick, spread)
    out[2:3, :] = sample([u2[k] for k in range(4)], pick, spread)


def sample_second_kernel(first, l2, u3, pick, spread, out):
    got = picked(all_planes(u3, l2[...]), pick)
    rest = 4 * NY
    out[0:2, :] = first[0:2, :]
    out[2:3, :] = first[2:3, :] + weighted(got[rest:], lambda c: spread[c, rest:, :])
    out[3:4, :] = weighted(got[:rest], lambda c: spread[c, :rest, :])


def sample_third_kernel(
    par, before, l3, u4, g, sxl, pick, spread, pick_l, pick_2, spread_o, out
):
    odd = par[0] == 1
    got = picked(all_planes(u4, l3[...]), pick)
    rest = 4 * NY
    face = u4[0]
    x = sxl[...] * face
    left = picked([x, face], pick_l)
    second = picked([jnp.where(odd, -g[...], -float(AB[0, 4]) * x)], pick_2)
    out[0:3, :] = before[0:3, :]
    out[3:4, :] = before[3:4, :] + weighted(got[rest:], lambda c: spread[c, rest:, :])
    out[4:5, :] = weighted(got[:rest], lambda c: spread[c, :rest, :])
    out[5:6, :] = weighted(left[:NY], lambda c: spread_o[1, c])
    out[6:7, :] = weighted(second, lambda c: spread_o[2, c])
    out[7:8, :] = jnp.where(odd, 0.0, weighted(left[NY:], lambda c: spread_o[0, c]))


def sample_last_kernel(
    par, before, inner, tent, g, pick, spread, pick_l, spread_o, out, block, sems
):
    odd = par[0] == 1
    own_g = jnp.where(odd, -g[...], 0.0)
    last = jnp.where(odd, 0.0, inner[...])
    got = picked(all_planes(tent, own_g) + [last], pick)
    face = picked([tent[0]], pick_l)
    rest = 4 * NY
    rows = [
        before[0:4, :],
        before[4:5, :] + weighted(got[5 * NY :], lambda c: spread[c, rest:, :]),
        weighted(got[: 5 * NY], lambda c: spread[c]),
        before[5:6, :] + weighted(face, lambda c: spread_o[0, c]),
        before[6:8, :],
    ]
    rows = jnp.concatenate(rows, 0)
    for i in range(8):
        block[ROWS * i : ROWS * (i + 1), :] = rows
    size = 8 * ROWS
    copies = [
        pltpu.make_async_copy(block, out.at[pl.ds(size * i, size), :], sems.at[i])
        for i in range(out.shape[0] // size)
    ]
    for copy in copies:
        copy.start()
    for copy in copies:
        copy.wait()


def stations_kernel(par, blocks, stations, row_ref, lane_ref):
    odd = par[0] == 1
    for j in range(2 * SB):
        wanted = blocks[0, j // SB] * SB + j % SB
        hit = jnp.zeros((8, CAP), FP)
        for r in range(16):
            hit = hit + jnp.where(stations[8 * r : 8 * r + 8, :] == wanted, 1.0, 0.0)
        lane_ref[j : j + 1, :] = jnp.sum(hit, 0, keepdims=True)
    lane = lane_ref[...]
    ids = stations[...].astype(FP)
    at = lax.dot_general(
        lane, ids, (((1,), (1,)), ((), ())), precision=HIGHEST, preferred_element_type=jnp.float32
    )
    j = lax.broadcasted_iota(jnp.int32, (2 * SB, 128), 0)
    wanted = jnp.where(j < SB, blocks[0, 0] * SB + j, blocks[0, 1] * SB + (j - SB))
    place = lax.broadcasted_iota(jnp.int32, (2 * SB, 128), 1)
    hit = jnp.where(jnp.abs(at - wanted.astype(FP)) < 0.5, place.astype(FP), 0.0)
    device = jnp.sum(hit, 1, keepdims=True).astype(jnp.int32)
    first = jnp.where(odd, 1, 0)

    def one_hot(device):
        device = jnp.bitwise_and(device, 127)
        side = jnp.where(jnp.bitwise_and(device, 1) == first, 0, 64)
        return jnp.where(place == side + jnp.right_shift(device, 1), 1.0, 0.0)

    row_ref[0] = one_hot(device)
    row_ref[1] = one_hot(device + 1)
    even = jnp.where(jnp.bitwise_and(device, 1) == 0, 1.0, 0.0)
    row_ref[2] = even * (one_hot(device + 2) + one_hot(device + 127))


def station_spectra(near, far, row, lane, table):
    slabs = [
        jnp.concatenate([half[pl.ds(t, 64, stride=ROWS), :] for half in (near, far)], 0)
        for t in range(ROWS)
    ]

    def select(which, slabs):
        hot = row[which].astype(jnp.bfloat16)
        parts = jnp.concatenate(parts_of(jnp.concatenate(slabs, 1), 2), 0)
        return jnp.dot(
            jnp.concatenate([hot, hot], 1), parts, preferred_element_type=jnp.float32
        )

    found = select(0, slabs[:6])
    more = select(1, [slabs[8], slabs[6]])
    last = select(2, [slabs[7]])
    found = [found[:, 128 * t : 128 * (t + 1)] for t in range(NT)]
    found[4] = found[4] + more[:, :128]
    found[5] = found[5] + more[:, 128:] + last
    at = lax.broadcasted_iota(jnp.int32, (2 * SB, 128), 1)
    samples = jnp.zeros((2 * SB, 128), FP)
    for t in range(NT):
        one = jnp.sum(found[t] * lane[...], 1, keepdims=True)
        samples = jnp.where(at % 8 == t, one, samples)
    parts = [part.astype(FP) for part in parts_of(samples, 3)]
    mixed = jnp.zeros((2 * SB, 128), FP)
    for group, (part, _) in enumerate(PART_PAIRS):
        mixed = jnp.where(at // 8 == group, parts[part], mixed)
    return lax.dot_general(
        table[...], mixed.astype(jnp.bfloat16), (((1,), (1,)), ((), ())),
        preferred_element_type=jnp.float32,
    ).astype(jnp.bfloat16)


def cross_kernel(
    par, base, inner, outer, coef, near, far, row, lane, table, spread_a, spread_b,
    end, out, held_end, held, sems,
):
    odd = par[0] == 1
    pull = coef[4] * jnp.where(odd, outer[...], inner[...])
    for k in range(4):
        value = base[k] - float(AB[k, 4]) * pull
        held_end[k] = value - jnp.where(odd, inner[...], outer[...]) if k == 0 else value
    copies = [pltpu.make_async_copy(held_end, end, sems.at[4])]
    copies[0].start()
    spectra = station_spectra(near, far, row, lane, table)
    second = jnp.dot(spectra, spread_b[...], preferred_element_type=jnp.float32) * (1.0 / NT)
    b_re = second[:F]
    b_im = second[F:]
    size = F // 4
    for i in range(4):
        rows = slice(size * i, size * (i + 1))
        first = jnp.dot(
            jnp.concatenate([spectra[rows], spectra[F + size * i : F + size * (i + 1)]], 0), spread_a[...],
            preferred_element_type=jnp.float32,
        )
        for at in range(0, SB * SB, 128):
            a_re = first[:size, at : at + 128]
            a_im = first[size:, at : at + 128]
            held[0, rows, at : at + 128] = (a_re * b_re[rows] + a_im * b_im[rows]).astype(jnp.bfloat16)
            held[1, rows, at : at + 128] = (a_im * b_re[rows] - a_re * b_im[rows]).astype(jnp.bfloat16)
        copy = pltpu.make_async_copy(held.at[:, rows, :], out.at[0, :, rows, :], sems.at[i])
        copy.start()
        copies.append(copy)
    for copy in copies:
        copy.wait()


def body(
    now, vel, speed_sq, src, wavelet, slot_elem, slot_station, slot_weight, pair_blocks, devices
):
    inner_route = [(i, i ^ 1) for i in range(devices)]
    outer_route = [(i, (i + 1 if i % 2 else i - 1) % devices) for i in range(devices)]

    def swap_inner(x):
        return lax.ppermute(x, AXES, inner_route)

    def swap_outer(x):
        return lax.ppermute(x, AXES, outer_route)

    mat_z, left, right, over = (jnp.asarray(x) for x in tables())
    table = jnp.asarray(dft_table())
    reps = np.zeros((2 * SB, SB * SB))
    for i in range(SB):
        reps[i, i * SB : (i + 1) * SB] = 1.0
    tiles = np.zeros((2 * SB, 128))
    for i in range(128):
        tiles[SB + i % SB, i] = 1.0
    reps = jnp.asarray(reps, jnp.bfloat16)
    tiles = jnp.asarray(tiles, jnp.bfloat16)
    pads = (pltpu.VMEM((4, NY + 16, NZ), FP),)
    one_pad = (pltpu.VMEM((1, NY + 16, NZ), FP),)

    par = lax.axis_index("core").astype(jnp.int32).reshape(1)

    inputs = (
        now, vel, src, speed_sq, left, right, over, mat_z, slot_elem.reshape(1, CAP), slot_weight,
        wavelet.reshape(1, NT),
    )
    kept = [jax.ShapeDtypeStruct(x.shape, x.dtype) for x in inputs]
    kept[3] = jax.ShapeDtypeStruct((EY, EZ), FP)
    now, vel, src, speed, left, right, over, mat_z, elem, weight, wavelet, msg = call(
        start_kernel,
        [(x.shape, x.dtype) for x in kept] + [((NY + EY + PACK, NZ), FP)],
        (par, *(in_hbm(x) for x in inputs)), "start",
        specs=[SMEM] + [HBM] * len(inputs), scratch=(pltpu.SemaphoreType.DMA((len(inputs),)),),
    )
    inner0 = swap_inner(msg)
    base, coef, g0 = call(
        base_first_kernel, [(FOUR, FP), (FIVE, FP), (PLANE, FP)],
        (wavelet, now, vel, src, speed, left, right, over, mat_z), "base0", scratch=pads,
    )
    tent, msg, cleft = call(
        inner_first_kernel,
        [(FOUR, FP), ((PACK_AT + 6 * PACK, NZ), jnp.bfloat16), (FIVE, FP)],
        (par, base, now, g0, inner0, speed, elem, weight, coef, left, right, over, mat_z), "inner0", 1,
        scratch=one_pad,
    )
    outer0 = swap_outer(msg)
    pick_shape = ((2 * NZ, 5 * CAP), jnp.bfloat16)
    pick, spread = call(slots_kernel, [pick_shape, ((5, 5 * NY, CAP), FP)], (elem, weight), "slots")
    row, lane = call(
        stations_kernel, [((3, 2 * SB, 128), FP), ((2 * SB, CAP), FP)],
        (par, pair_blocks, slot_station.reshape(128, CAP)), "stations", 2,
    )
    outer0, pick, spread, row, lane = lax.optimization_barrier((outer0, pick, spread, row, lane))
    u1, msg, outer, coef0, sxl, last0 = call(
        outer_first_kernel,
        [(FOUR, FP), (PLANE, FP), (PLANE, FP), (FIVE, FP), (PLANE, FP), (PLANE, FP)],
        (par, tent, now, g0, outer0, inner0, coef, cleft, left, right, over, mat_z), "outer0", 1,
        scratch=one_pad,
    )

    def base_of(step, u, before):
        return call(
            functools.partial(base_kernel, step), [(FOUR, FP)],
            (wavelet, u, before, src, coef, coef0, mat_z), "base", scratch=pads,
        )[0]

    def two_steps(step, u_b, u_a, msg, outer, fill=(None, None)):
        inner = swap_inner(msg)
        base = base_of(step, u_b, u_a)
        more = None
        if fill[0]:
            inner, base, more = lax.optimization_barrier((inner, base, fill[0]()))
        u_c, g, msg, last = call(
            both_kernel, [(FOUR, FP), (PLANE, FP), (PLANE, FP), (PLANE, FP)],
            (par, base, inner, outer, coef), "both", 1,
        )
        inner = swap_inner(msg)
        base = base_of(step + 1, u_c, u_b)
        if fill[1]:
            inner, base, more = lax.optimization_barrier((inner, base, fill[1](more, u_c, g, last)))
        tent, msg = call(
            inner_kernel, [(FOUR, FP), ((2 * NY, NZ), jnp.bfloat16)],
            (par, base, u_c, g, inner, coef), "inner", 1,
        )
        return u_c, g, last, inner, tent, msg, more

    def complete(tent, u, g, recv, inner):
        return call(
            outer_kernel, [(FOUR, FP), (PLANE, FP), (PLANE, FP), (PLANE, FP)],
            (par, tent, u, g, recv, inner, coef, sxl), "outer", 1,
        )

    u2, g2, last1, inner2, tent, msg, _ = two_steps(1, u1, now, msg, outer)
    recv = swap_outer(msg)
    (rows,) = call(
        sample_first_kernel, [((3, CAP), FP)], (now, last0, u1, last1, u2, pick, spread), "sample3"
    )
    others = call(
        others_kernel, [pick_shape, pick_shape, ((3, 5, NY, CAP), FP)], (par, inner0, outer0), "others", 1
    )
    recv, rows, *others = lax.optimization_barrier((recv, rows, *others))
    u3, msg, outer, last2 = complete(tent, u2, g2, recv, inner2)

    def second_rows():
        return call(
            sample_second_kernel, [((4, CAP), FP)], (rows, last2, u3, pick, spread), "sample5"
        )[0]

    def third_rows(before, u, g, last):
        return call(
            sample_third_kernel, [((8, CAP), FP)],
            (par, before, last, u, g, sxl, pick, spread, *others), "sample8", 1,
        )[0]

    u4, g4, _, inner4, tent, msg, rows = two_steps(3, u3, u2, msg, outer, (second_rows, third_rows))
    pick_l, _, spread_o = others
    (mine,) = call(
        sample_last_kernel, [((devices // 2 * ROWS, CAP), FP)],
        (par, rows, inner4, tent, g4, pick, spread, pick_l, spread_o), "sample7", 1,
        out_specs=[HBM],
        scratch=(
            pltpu.VMEM((8 * ROWS, CAP), FP), pltpu.SemaphoreType.DMA((devices // 16,)),
        ),
    )
    near = lax.all_to_all(
        mine.reshape(devices // 2, 1, ROWS * CAP), ("pair", "chip"), 0, 0, tiled=True
    ).reshape(devices // 2 * ROWS, CAP)
    recv = swap_outer(msg)
    recv, near = lax.optimization_barrier((recv, near))
    far = swap_inner(near)
    u5, msg, outer = call(
        outer_last_kernel, [(FOUR, FP), (PLANE, FP), (PLANE, FP)],
        (par, tent, u4, g4, recv, inner4, coef, sxl), "outer", 1,
    )
    inner = swap_inner(msg)
    base = base_of(5, u5, u4)
    end, cross = call(
        cross_kernel, [(FOUR, FP), ((1, 2, F, SB * SB), jnp.bfloat16)],
        (par, base, inner, outer, coef, near, far, row, lane, table, reps, tiles), "cross", 1,
        out_specs=[HBM, HBM],
        scratch=(
            pltpu.VMEM(FOUR, FP), pltpu.VMEM((2, F, SB * SB), jnp.bfloat16),
            pltpu.SemaphoreType.DMA((5,)),
        ),
    )
    return end, cross


def solution(mesh):
    split = P(AXES)
    in_specs = (
        P(AXES, None, None), P(AXES, None, None), P(AXES, None, None), P(AXES, None, None),
        P(), split, P(), P(None, AXES), P(AXES, None),
    )
    out_specs = (P(AXES, None, None), P(AXES, None, None, None))
    grid = mesh.devices.reshape(mesh.shape["pair"], -1, 2)
    mesh = jax.sharding.Mesh(grid, AXES)
    devices = grid.size
    run = functools.partial(body, devices=devices)
    return jax.shard_map(run, mesh=mesh, in_specs=in_specs, out_specs=out_specs, check_vma=False)
```

```python
import functools
import math

import jax
import jax.numpy as jnp
import numpy as np
from jax import lax
from jax.experimental import pallas as pl
from jax.experimental.pallas import tpu as pltpu
from jax.sharding import PartitionSpec as P

NT = 6
F = 256
SB = 32
STEP_DT = 0.04
NY = 96
NZ = 128
EY = 24
EZ = 32
CAP = 128
AXES = ("pair", "chip", "core")
HIGHEST = lax.Precision.HIGHEST
W1 = np.array([0.1, 49.0 / 90.0, 32.0 / 45.0, 49.0 / 90.0, 0.1])


def stiffness_1d():
    points = np.array([-1.0, -math.sqrt(3.0 / 7.0), 0.0, math.sqrt(3.0 / 7.0), 1.0])
    factor = np.array(
        [np.prod([points[i] - points[j] for j in range(5) if j != i]) for i in range(5)]
    )
    d = np.zeros((5, 5))
    for i in range(5):
        for j in range(5):
            if i != j:
                d[i, j] = factor[i] / (factor[j] * (points[i] - points[j]))
        d[i, i] = -np.sum(d[i])
    return d.T @ np.diag(W1) @ d


A = stiffness_1d()
MX = np.array([0.2, W1[1], W1[2], W1[3], 0.2])
AB = A / MX[:, None]
KAPPA = float(sum(AB[4, k] * AB[k, 4] for k in range(4)))


def f32(x):
    return np.asarray(x, np.float32)


def tables():
    my = np.array([MX[y % 4] for y in range(NY)])
    mz = np.array([0.1 if z == 0 else MX[z % 4] for z in range(NZ)])
    mat_z = np.zeros((NZ, 2 * NZ))
    for z in range(NZ):
        e, c = divmod(z, 4)
        for m in range(5):
            if 4 * e + m < NZ:
                mat_z[4 * e + m, z] += A[c, m]
            if c == 0 and e > 0:
                mat_z[4 * (e - 1) + m, NZ + z] += A[4, m]
    left = np.zeros((3 * NY, EY))
    for y in range(NY):
        e, b = divmod(y, 4)
        left[y, e] += W1[b]
        left[NY + y, e] += 1.0
        if b == 0:
            left[y, (e - 1) % EY] += W1[4]
            left[2 * NY + y, (e - 1) % EY] += 1.0
    left[:NY] /= my[:, None]
    right = np.zeros((EZ, 3 * NZ))
    for z in range(NZ):
        e, c = divmod(z, 4)
        right[e, z] += 1.0
        right[e, 2 * NZ + z] += W1[c]
        if c == 0 and e > 0:
            right[e - 1, NZ + z] += 1.0
            right[e - 1, 2 * NZ + z] += W1[4]
    right[:, 2 * NZ :] /= mz[None, :]
    over_z = np.broadcast_to(1.0 / mz, (8, NZ)) * (STEP_DT * STEP_DT)
    over_y = np.broadcast_to(1.0 / my[:8, None], (8, NZ)) * (STEP_DT * STEP_DT)
    left = np.tile(left, (1, 3)).astype(jnp.bfloat16)
    right = np.tile(right, (3, 1)).astype(jnp.bfloat16)
    high = mat_z.astype(jnp.bfloat16).astype(np.float64)
    low = (mat_z - high).astype(jnp.bfloat16)
    stack = np.concatenate([mat_z, mat_z], 0).astype(jnp.bfloat16)
    return np.concatenate([stack, low], 0), left, right, f32(np.concatenate([over_y, over_z], 0))


PART_PAIRS = ((0, 0), (1, 0), (0, 1), (1, 1), (2, 0), (0, 2))


def parts_of(x, count):
    parts = []
    for _ in range(count):
        part = x.astype(jnp.bfloat16)
        parts.append(part)
        x = x - part.astype(x.dtype)
    return parts


def dft_table():
    angle = np.pi * (np.arange(F) + 0.5) / F
    phase = angle[:, None] * np.arange(NT)[None, :]
    parts = parts_of(f32(np.concatenate([np.cos(phase), -np.sin(phase)], 0)), 3)
    table = np.zeros((2 * F, 128), jnp.bfloat16)
    for group, (_, part) in enumerate(PART_PAIRS):
        table[:, 8 * group : 8 * group + NT] = parts[part]
    return table


def dot(a, b):
    return jnp.dot(a, b, precision=HIGHEST, preferred_element_type=jnp.float32)


VMEM = pl.BlockSpec(memory_space=pltpu.VMEM)
SMEM = pl.BlockSpec(memory_space=pltpu.SMEM)
HBM = pl.BlockSpec(memory_space=pltpu.HBM)


def call(kernel, outs, args, name, smem=0, specs=None, out_specs=None, scratch=(), flops=4_000_000):
    return pl.pallas_call(
        kernel,
        out_shape=[jax.ShapeDtypeStruct(s, d) for s, d in outs],
        in_specs=specs or [SMEM] * smem + [VMEM] * (len(args) - smem),
        out_specs=out_specs or [VMEM] * len(outs),
        scratch_shapes=list(scratch),
        compiler_params=pltpu.CompilerParams(vmem_limit_bytes=24 * 1024 * 1024),
        cost_estimate=pl.CostEstimate(flops=flops, bytes_accessed=1_000_000, transcendentals=0),
        name=name,
    )(*args)


def in_hbm(x):
    return pltpu.with_memory_space_constraint(x, pltpu.HBM)


PACK = 32
ROWS = 9
PACK_AT = 2 * NY + 2 * EY
PLANE = (NY, NZ)
FOUR = (4, NY, NZ)
FIVE = (5, NY, NZ)
FP = jnp.float32


def expand_speed(parts, left, right, over):
    rows = jnp.dot(left, parts, preferred_element_type=jnp.float32)
    parts = jnp.concatenate(parts_of(rows, 3), 1)
    by_z = jnp.dot(parts[:NY], right, preferred_element_type=jnp.float32)
    by_y = jnp.dot(parts[NY:], right[:, 2 * NZ :], preferred_element_type=jnp.float32)
    over_y = jnp.concatenate([over[:8]] * (NY // 8), 0)
    over_z = over[8:9]
    return (
        by_z[:, :NZ] * over_z, by_z[:, NZ : 2 * NZ] * over_z, by_y[:NY] * over_y, by_y[NY:] * over_y,
        by_z[:, 2 * NZ :] * (STEP_DT * STEP_DT),
    )


def speed_parts(speed, count=3):
    return jnp.concatenate(parts_of(speed, count), 0)


def along_z(u, mat_z):
    high, low = parts_of(u, 2)
    return jnp.dot(
        jnp.concatenate([high, low], 1), mat_z[: 2 * NZ], preferred_element_type=jnp.float32
    ) + jnp.dot(high, mat_z[2 * NZ :], preferred_element_type=jnp.float32)


def y_patterns():
    b = lax.broadcasted_iota(jnp.int32, (8, NZ), 0) % 4
    own, before = {}, {}
    for d in range(-4, 5):
        total = jnp.zeros((8, NZ), FP)
        for row in range(4):
            if 0 <= row + d <= 4:
                total = jnp.where(b == row, float(A[row, row + d]), total)
        own[d] = total
        if d <= 0:
            before[d] = jnp.where(b == 0, float(A[4, 4 + d]), 0.0)
    return own, before


def y_coefs(y1, y2, patterns):
    own, before = patterns
    return {d: y1 * own[d] + y2 * before[d] if d in before else y1 * own[d] for d in own}


def wrap_rows(pad, at, plane):
    pad[at, 8 : 8 + NY, :] = plane
    pad[at, 4:8, :] = plane[NY - 4 :]
    pad[at, 8 + NY : 12 + NY, :] = plane[:4]


def along_y(pad, at, row, coefs):
    total = None
    for d, c in coefs.items():
        term = c * pad[at, 8 + row + d : 16 + row + d, :]
        total = term if total is None else total + term
    return total


def to_right(sx, u):
    total = float(AB[4, 0]) * u[0]
    for m in range(1, 4):
        total = total + float(AB[4, m]) * u[m]
    return sx * total


def start_kernel(
    par, now_in, speed_in, left_in, right_in, over_in, mat_in, elem_in, weight_in, wave_in,
    now, speed, left, right, over, mat, elem, weight, wave, msg_ref, sems,
):
    pairs = (
        (now_in, now), (speed_in.at[0], speed), (elem_in, elem), (weight_in, weight), (left_in, left),
        (right_in, right), (over_in, over), (mat_in, mat), (wave_in, wave),
    )
    copies = [pltpu.make_async_copy(a, b, sems.at[i]) for i, (a, b) in enumerate(pairs)]
    for copy in copies:
        copy.start()
    msg_ref[NY:] = jnp.zeros((EY + PACK, NZ), FP)
    copies[0].wait()
    msg_ref[:NY] = jnp.where(par[0] == 1, now[0], to_right(1.0, [now[k] for k in range(4)]))
    for copy in copies[1:4]:
        copy.wait()
    msg_ref[NY : NY + EY, :EZ] = speed[...]
    msg_ref[NY + EY : NY + EY + 25] = weight[100:125]
    msg_ref[NY + EY + PACK - 1 :] = elem[...].astype(FP)
    for copy in copies[4:]:
        copy.wait()


def base_first_kernel(
    wave, now, vel_in, src_in, speed, left, right, over, mat_z,
    out, src, coef_ref, first_ref, vel, pad, sems,
):
    copies = [
        pltpu.make_async_copy(vel_in, vel, sems.at[0]), pltpu.make_async_copy(src_in, src, sems.at[1])
    ]
    for copy in copies:
        copy.start()
    coefs = expand_speed(speed_parts(speed[...]), left[...], right[...], over[...])
    for i in range(5):
        coef_ref[i] = coefs[i]
    first_ref[...] = to_right(coefs[4], [now[k] for k in range(4)])
    base_body(0, wave, now, None, None, coef_ref, None, mat_z, out, pad)
    for copy in copies:
        copy.wait()
    scale = jnp.broadcast_to(wave[:, 0:1] * (STEP_DT * STEP_DT), PLANE)
    for k in range(4):
        out[k] = out[k] + STEP_DT * vel[k] + scale * src[k]


def base_body(step, wave, now, prev, src, coef, coef0, mat_z, out, pad):
    scale = jnp.broadcast_to(wave[:, step : step + 1] * (STEP_DT * STEP_DT), (8, NZ))
    by_z = along_z(now[...].reshape(4 * NY, NZ), mat_z)
    patterns = y_patterns()
    for k in range(4):
        wrap_rows(pad, k, now[k])
    for row in range(0, NY, 8):
        at = slice(row, row + 8)
        u = [now[k, at, :] for k in range(4)]
        sx = coef[4, at, :]
        own = [coef[i, at, :] for i in range(4)]
        first = own if coef0 is None else [coef0[i, at, :] for i in range(4)]
        cy = y_coefs(own[2], own[3], patterns)
        cy0 = cy if coef0 is None else y_coefs(first[2], first[3], patterns)
        for k in range(4):
            c = own if k else first
            z = by_z[NY * k + row : NY * k + row + 8]
            force = c[0] * z[:, :NZ] + c[1] * z[:, NZ:] + along_y(pad, k, row, cy if k else cy0)
            if k == 0:
                force = 0.5 * force if coef0 is None else force + coef0[4, at, :] * u[0]
            mix = float(AB[k, 0]) * u[0]
            for m in range(1, 4):
                mix = mix + float(AB[k, m]) * u[m]
            force = force + sx * mix
            if prev is None:
                out[k, at, :] = u[k] - force
            else:
                out[k, at, :] = 2.0 * u[k] - prev[k, at, :] + (scale * src[k, at, :] - force)


def base_kernel(step, wave, now, prev, src, coef, coef0, mat_z, out, pad):
    base_body(step, wave, now, prev, src, coef, coef0, mat_z, out, pad)


def half_left(plane, coefs, mat_z, pad):
    by_z = along_z(plane, mat_z)
    wrap_rows(pad, 0, plane)
    patterns = y_patterns()
    tiles = []
    for row in range(0, NY, 8):
        c = [x[row : row + 8] for x in coefs]
        by_y = along_y(pad, 0, row, y_coefs(c[2], c[3], patterns))
        z = by_z[row : row + 8]
        tiles.append(0.5 * (c[0] * z[:, :NZ] + c[1] * z[:, NZ:] + by_y))
    return jnp.concatenate(tiles, 0) + float(AB[4, 4]) * (coefs[4] * plane)


def inner_first_kernel(
    par, base, now, first, recv, speed, elem, weight, coef, left, right, over, mat_z,
    tent_ref, msg_ref, cleft_ref, pad,
):
    odd = par[0] == 1
    their_speed = jnp.where(odd, recv[NY : NY + EY, :EZ], 0.0)
    coefs = expand_speed(speed_parts(their_speed), left[...], right[...], over[...])
    for i in range(5):
        cleft_ref[i] = coefs[i]
    share = half_left(now[0], coefs, mat_z, pad)
    inner = jnp.where(odd, coefs[4] * recv[:NY], recv[:NY])
    inner_finish(odd, base, now, first[...], inner, coef[4], share, tent_ref, msg_ref)
    own_speed = jnp.concatenate([speed[...], jnp.zeros((EY, NZ - EZ), FP)], 1)
    msg_ref[2 * NY : PACK_AT] = speed_parts(own_speed, 2)
    pulled = -float(AB[0, 4]) * weight[:25]
    for k in range(1, 4):
        pulled = pulled - float(AB[k, 4]) * weight[25 * k : 25 * k + 25]
    slots = elem[...].astype(FP)
    theirs = recv[NY + EY :]
    packages = (
        (jnp.where(odd, weight[100:125], weight[:25]), slots),
        (pulled, slots),
        (theirs[:25], theirs[PACK - 1 :]),
    )
    for group, (rows, slots) in enumerate(packages):
        eights = jnp.floor(slots * 0.125)
        package = [rows, jnp.zeros((PACK - 27, CAP), FP), eights, slots - 8.0 * eights]
        at = PACK_AT + 2 * PACK * group
        msg_ref[at : at + 2 * PACK] = jnp.concatenate(parts_of(jnp.concatenate(package, 0), 2), 0)


def inner_finish(odd, base, now, g_now, inner, sx, share, tent_ref, msg_ref):
    even_part = jnp.where(odd, 0.0, sx * inner)
    tent = []
    for k in range(4):
        value = base[k] - float(AB[k, 4]) * even_part
        if k == 0:
            value = value - jnp.where(odd, inner, 0.0)
            if share is not None:
                value = value - share
        tent_ref[k] = value
        tent.append(value)
    msg_ref[:NY] = jnp.where(odd, g_now, now[0]).astype(jnp.bfloat16)
    msg_ref[NY : 2 * NY] = jnp.where(odd, to_right(sx, tent), tent[0]).astype(jnp.bfloat16)


def inner_kernel(par, base, now, g_now, recv, coef, tent_ref, msg_ref):
    odd = par[0] == 1
    inner_finish(odd, base, now, g_now[...], recv[...], coef[4], None, tent_ref, msg_ref)


def outer_finish(odd, tent, sx, sx_left, recv0, recv1, g_own, u0_own, share, refs):
    u_ref, msg_ref, outer_ref = refs
    odd_part = jnp.where(odd, sx * recv0, 0.0)
    values = []
    for k in range(4):
        value = tent[k] - float(AB[k, 4]) * odd_part
        if k == 0:
            lost = recv0 if share is None else recv0 + share
            value = value - jnp.where(odd, 0.0, lost)
        u_ref[k] = value
        values.append(value)
    msg_ref[...] = jnp.where(odd, values[0], to_right(sx, values))
    mine = g_own if share is None else g_own + share
    outer_ref[...] = recv1 - jnp.where(odd, mine, KAPPA * sx_left * sx_left * u0_own)


def outer_first_kernel(
    par, tent, now, first, recv, inner, coef, cleft, left, right, over, mat_z,
    u_ref, msg_ref, outer_ref, coef0_ref, sxl_ref, last_ref, pad,
):
    odd = par[0] == 1
    parts = jnp.concatenate([recv[2 * NY : PACK_AT, :EZ], jnp.zeros((EY, EZ), jnp.bfloat16)], 0)
    theirs = expand_speed(parts, left[...], right[...], over[...])
    coefs = [jnp.where(odd, coef[i], theirs[i]) for i in range(5)]
    recv0 = recv[:NY].astype(FP)
    plane = jnp.where(odd, recv0, now[0])
    share = half_left(plane, coefs, mat_z, pad)
    on_left = [jnp.where(odd, cleft[i], theirs[i]) for i in range(5)]
    for i in range(4):
        coef0_ref[i] = 0.5 * (coef[i] + on_left[i])
    coef0_ref[4] = float(AB[4, 4]) * on_left[4]
    sxl_ref[...] = on_left[4]
    last_ref[...] = jnp.where(odd, recv0, inner[:NY])
    outer_finish(
        odd, tent, coef[4], on_left[4], recv0, recv[NY : 2 * NY].astype(FP), first[...], now[0], share,
        (u_ref, msg_ref, outer_ref),
    )


def outer_kernel(par, tent, now, g_now, recv, inner, coef, sxl, u_ref, msg_ref, outer_ref, last_ref):
    odd = par[0] == 1
    recv0 = recv[:NY].astype(FP)
    last_ref[...] = jnp.where(odd, recv0, inner[...])
    outer_finish(
        odd, tent, coef[4], sxl[...], recv0, recv[NY:].astype(FP), g_now[...], now[0], None,
        (u_ref, msg_ref, outer_ref),
    )


def both_kernel(par, base, inner, outer, coef, u_ref, g_ref, msg_ref, last_ref):
    odd = par[0] == 1
    last = jnp.where(odd, outer[...], inner[...])
    from_left = jnp.where(odd, inner[...], outer[...])
    sx = coef[4]
    pull = sx * last
    values = []
    for k in range(4):
        value = base[k] - float(AB[k, 4]) * pull
        if k == 0:
            value = value - from_left
        u_ref[k] = value
        values.append(value)
    g = to_right(sx, values)
    g_ref[...] = g
    msg_ref[...] = jnp.where(odd, values[0], g)
    last_ref[...] = last


def outer_last_kernel(par, tent, now, g_now, recv, near, coef, sxl, u_ref, both_ref, outer_ref):
    gathered = near.shape[0]
    both_ref[:gathered] = near[...]
    outer_finish(
        par[0] == 1, tent, coef[4], sxl[...], recv[:NY].astype(FP), recv[NY:].astype(FP), g_now[...],
        now[0], None,
        (u_ref, both_ref.at[pl.ds(gathered, NY), :], outer_ref),
    )


def pick_nodes(ez, pick_ref):
    z = lax.broadcasted_iota(jnp.int32, (NZ, CAP), 0)
    for c in range(5):
        hot = (z == 4 * ez + c).astype(FP).astype(jnp.bfloat16)
        for half in range(2):
            pick_ref[half * NZ : (half + 1) * NZ, c * CAP : (c + 1) * CAP] = hot


def y_masks(ey):
    y = lax.broadcasted_iota(jnp.int32, (NY, CAP), 0)
    masks = []
    for b in range(5):
        row = 4 * ey + b
        masks.append(y == jnp.where(row >= NY, row - NY, row))
    return masks


def spread_nodes(masks, weight, c):
    total = jnp.zeros((NY, CAP), FP)
    for b in range(5):
        total = jnp.where(masks[b], weight[5 * b + c : 5 * b + c + 1, :], total)
    return total


def slots_kernel(elem, weight, pick_ref, spread_ref):
    ey = elem[...] // EZ
    pick_nodes(elem[...] - ey * EZ, pick_ref)
    masks = y_masks(ey)
    for a in range(5):
        plane = weight[25 * a : 25 * a + 25, :]
        for c in range(5):
            spread_ref[c, a * NY : (a + 1) * NY, :] = spread_nodes(masks, plane, c)


def others_kernel(par, inner, outer, pick_l_ref, pick_2_ref, spread_ref):
    odd = par[0] == 1
    from_inner = inner[NY + EY :]
    halves = [
        outer[PACK_AT + PACK * i : PACK_AT + PACK * (i + 1)].astype(FP) for i in range(6)
    ]
    from_outer, pulled, relayed = (halves[2 * i] + halves[2 * i + 1] for i in range(3))
    pulled = jnp.where(odd, 0.0, pulled)

    def number(package):
        return 8.0 * package[PACK - 2 : PACK - 1] + package[PACK - 1 :]

    groups = (
        (
            jnp.where(odd, from_inner[:25], from_outer[:25]),
            jnp.where(odd, from_inner[PACK - 1 :], number(from_outer)),
            pick_l_ref,
        ),
        (
            jnp.where(odd, from_outer[:25], relayed[:25]),
            jnp.where(odd, number(from_outer), number(relayed)),
            pick_2_ref,
        ),
    )
    for group, (rows, elem, pick_ref) in enumerate(groups):
        elem = elem.astype(jnp.int32)
        ey = elem // EZ
        pick_nodes(elem - ey * EZ, pick_ref)
        masks = y_masks(ey)
        for c in range(5):
            spread_ref[2 * group, c] = spread_nodes(masks, rows, c)
            if group == 0:
                spread_ref[1, c] = spread_nodes(masks, pulled, c)


def picked(planes, pick):
    high, low = parts_of(jnp.concatenate(planes, 0), 2)
    return jnp.dot(
        jnp.concatenate([high, low], 1), pick[...], preferred_element_type=jnp.float32
    )


def weighted(got, spread):
    total = None
    for c in range(5):
        term = got[:, c * CAP : (c + 1) * CAP] * spread(c)
        total = term if total is None else total + term
    return jnp.sum(jnp.sum(total.reshape(-1, 8, CAP), 0), 0, keepdims=True)


def sample(planes, pick, spread):
    rows = NY * len(planes)
    return weighted(picked(planes, pick), lambda c: spread[c, :rows, :])


def all_planes(u, last):
    return [u[0], u[1], u[2], u[3], last]


def sample_first_kernel(u0, l0, u1, l1, u2, pick, spread, out):
    out[0:1, :] = sample(all_planes(u0, l0[...]), pick, spread)
    out[1:2, :] = sample(all_planes(u1, l1[...]), pick, spread)
    out[2:3, :] = sample([u2[k] for k in range(4)], pick, spread)


def sample_second_kernel(first, l2, u3, pick, spread, out):
    got = picked(all_planes(u3, l2[...]), pick)
    rest = 4 * NY
    out[0:2, :] = first[0:2, :]
    out[2:3, :] = first[2:3, :] + weighted(got[rest:], lambda c: spread[c, rest:, :])
    out[3:4, :] = weighted(got[:rest], lambda c: spread[c, :rest, :])


def sample_third_kernel(
    par, before, l3, u4, g, sxl, pick, spread, pick_l, pick_2, spread_o, out
):
    odd = par[0] == 1
    got = picked(all_planes(u4, l3[...]), pick)
    rest = 4 * NY
    face = u4[0]
    x = sxl[...] * face
    left = picked([x, face], pick_l)
    second = picked([jnp.where(odd, -g[...], -float(AB[0, 4]) * x)], pick_2)
    out[0:3, :] = before[0:3, :]
    out[3:4, :] = before[3:4, :] + weighted(got[rest:], lambda c: spread[c, rest:, :])
    out[4:5, :] = weighted(got[:rest], lambda c: spread[c, :rest, :])
    out[5:6, :] = weighted(left[:NY], lambda c: spread_o[1, c])
    out[6:7, :] = weighted(second, lambda c: spread_o[2, c])
    out[7:8, :] = jnp.where(odd, 0.0, weighted(left[NY:], lambda c: spread_o[0, c]))


def sample_last_kernel(
    par, before, inner, tent, g, pick, spread, pick_l, spread_o, out, block, sems
):
    odd = par[0] == 1
    own_g = jnp.where(odd, -g[...], 0.0)
    last = jnp.where(odd, 0.0, inner[...])
    got = picked(all_planes(tent, own_g) + [last], pick)
    face = picked([tent[0]], pick_l)
    rest = 4 * NY
    rows = [
        before[0:4, :],
        before[4:5, :] + weighted(got[5 * NY :], lambda c: spread[c, rest:, :]),
        weighted(got[: 5 * NY], lambda c: spread[c]),
        before[5:6, :] + weighted(face, lambda c: spread_o[0, c]),
        before[6:8, :],
    ]
    rows = jnp.concatenate(rows, 0)
    for i in range(8):
        block[ROWS * i : ROWS * (i + 1), :] = rows
    size = 8 * ROWS
    copies = [
        pltpu.make_async_copy(block, out.at[pl.ds(size * i, size), :], sems.at[i])
        for i in range(out.shape[0] // size)
    ]
    for copy in copies:
        copy.start()
    for copy in copies:
        copy.wait()


def stations_kernel(par, blocks, stations, row_ref, lane_ref):
    odd = par[0] == 1
    for j in range(2 * SB):
        wanted = blocks[0, j // SB] * SB + j % SB
        hit = jnp.zeros((8, CAP), FP)
        for r in range(16):
            hit = hit + jnp.where(stations[8 * r : 8 * r + 8, :] == wanted, 1.0, 0.0)
        lane_ref[j : j + 1, :] = jnp.sum(hit, 0, keepdims=True)
    lane = lane_ref[...]
    ids = stations[...].astype(FP)
    at = lax.dot_general(
        lane, ids, (((1,), (1,)), ((), ())), precision=HIGHEST, preferred_element_type=jnp.float32
    )
    j = lax.broadcasted_iota(jnp.int32, (2 * SB, 128), 0)
    wanted = jnp.where(j < SB, blocks[0, 0] * SB + j, blocks[0, 1] * SB + (j - SB))
    place = lax.broadcasted_iota(jnp.int32, (2 * SB, 128), 1)
    hit = jnp.where(jnp.abs(at - wanted.astype(FP)) < 0.5, place.astype(FP), 0.0)
    device = jnp.sum(hit, 1, keepdims=True).astype(jnp.int32)
    first = jnp.where(odd, 1, 0)

    def one_hot(device):
        device = jnp.bitwise_and(device, 127)
        side = jnp.where(jnp.bitwise_and(device, 1) == first, 0, 64)
        return jnp.where(place == side + jnp.right_shift(device, 1), 1.0, 0.0)

    row_ref[0] = one_hot(device)
    row_ref[1] = one_hot(device + 1)
    even = jnp.where(jnp.bitwise_and(device, 1) == 0, 1.0, 0.0)
    row_ref[2] = even * (one_hot(device + 2) + one_hot(device + 127))


def station_spectra(near, far, row, lane, table):
    slabs = [
        jnp.concatenate([half[pl.ds(t, 64, stride=ROWS), :] for half in (near, far)], 0)
        for t in range(ROWS)
    ]

    def select(which, slabs):
        hot = row[which].astype(jnp.bfloat16)
        parts = jnp.concatenate(parts_of(jnp.concatenate(slabs, 1), 2), 0)
        return jnp.dot(
            jnp.concatenate([hot, hot], 1), parts, preferred_element_type=jnp.float32
        )

    found = select(0, slabs[:6])
    more = select(1, [slabs[8], slabs[6]])
    last = select(2, [slabs[7]])
    found = [found[:, 128 * t : 128 * (t + 1)] for t in range(NT)]
    found[4] = found[4] + more[:, :128]
    found[5] = found[5] + more[:, 128:] + last
    at = lax.broadcasted_iota(jnp.int32, (2 * SB, 128), 1)
    samples = jnp.zeros((2 * SB, 128), FP)
    for t in range(NT):
        one = jnp.sum(found[t] * lane[...], 1, keepdims=True)
        samples = jnp.where(at % 8 == t, one, samples)
    parts = [part.astype(FP) for part in parts_of(samples, 3)]
    mixed = jnp.zeros((2 * SB, 128), FP)
    for group, (part, _) in enumerate(PART_PAIRS):
        mixed = jnp.where(at // 8 == group, parts[part], mixed)
    return lax.dot_general(
        table[...], mixed.astype(jnp.bfloat16), (((1,), (1,)), ((), ())),
        preferred_element_type=jnp.float32,
    ).astype(jnp.bfloat16)


def cross_kernel(
    par, base, outer, coef, near, far, row, lane, table, spread_a, spread_b,
    end, out, held_end, held, sems,
):
    odd = par[0] == 1
    inner = far[near.shape[0] :]
    pull = coef[4] * jnp.where(odd, outer[...], inner)
    for k in range(4):
        value = base[k] - float(AB[k, 4]) * pull
        held_end[k] = value - jnp.where(odd, inner, outer[...]) if k == 0 else value
    copies = [pltpu.make_async_copy(held_end, end, sems.at[4])]
    copies[0].start()
    spectra = station_spectra(near, far, row, lane, table)
    second = jnp.dot(spectra, spread_b[...], preferred_element_type=jnp.float32) * (1.0 / NT)
    b_re = second[:F]
    b_im = second[F:]
    size = F // 4
    for i in range(4):
        rows = slice(size * i, size * (i + 1))
        first = jnp.dot(
            jnp.concatenate([spectra[rows], spectra[F + size * i : F + size * (i + 1)]], 0), spread_a[...],
            preferred_element_type=jnp.float32,
        )
        for at in range(0, SB * SB, 128):
            a_re = first[:size, at : at + 128]
            a_im = first[size:, at : at + 128]
            held[0, rows, at : at + 128] = (a_re * b_re[rows] + a_im * b_im[rows]).astype(jnp.bfloat16)
            held[1, rows, at : at + 128] = (a_im * b_re[rows] - a_re * b_im[rows]).astype(jnp.bfloat16)
        copy = pltpu.make_async_copy(held.at[:, rows, :], out.at[0, :, rows, :], sems.at[i])
        copy.start()
        copies.append(copy)
    for copy in copies:
        copy.wait()


def body(
    now, vel, speed_sq, src, wavelet, slot_elem, slot_station, slot_weight, pair_blocks, devices
):
    inner_route = [(i, i ^ 1) for i in range(devices)]
    outer_route = [(i, (i + 1 if i % 2 else i - 1) % devices) for i in range(devices)]

    def swap_inner(x):
        return lax.ppermute(x, AXES, inner_route)

    def swap_outer(x):
        return lax.ppermute(x, AXES, outer_route)

    mat_z, left, right, over = (jnp.asarray(x) for x in tables())
    table = jnp.asarray(dft_table())
    reps = np.zeros((2 * SB, SB * SB))
    for i in range(SB):
        reps[i, i * SB : (i + 1) * SB] = 1.0
    tiles = np.zeros((2 * SB, 128))
    for i in range(128):
        tiles[SB + i % SB, i] = 1.0
    reps = jnp.asarray(reps, jnp.bfloat16)
    tiles = jnp.asarray(tiles, jnp.bfloat16)
    pads = (pltpu.VMEM((4, NY + 16, NZ), FP),)
    one_pad = (pltpu.VMEM((1, NY + 16, NZ), FP),)

    par = lax.axis_index("core").astype(jnp.int32).reshape(1)

    inputs = (
        now, speed_sq, left, right, over, mat_z, slot_elem.reshape(1, CAP), slot_weight,
        wavelet.reshape(1, NT),
    )
    kept = [jax.ShapeDtypeStruct(x.shape, x.dtype) for x in inputs]
    kept[1] = jax.ShapeDtypeStruct((EY, EZ), FP)
    now, speed, left, right, over, mat_z, elem, weight, wavelet, msg = call(
        start_kernel,
        [(x.shape, x.dtype) for x in kept] + [((NY + EY + PACK, NZ), FP)],
        (par, *(in_hbm(x) for x in inputs)), "start",
        specs=[SMEM] + [HBM] * len(inputs), scratch=(pltpu.SemaphoreType.DMA((len(inputs),)),),
    )
    inner0 = swap_inner(msg)
    base, src, coef, g0 = call(
        base_first_kernel, [(FOUR, FP), (FOUR, FP), (FIVE, FP), (PLANE, FP)],
        (wavelet, now, in_hbm(vel), in_hbm(src), speed, left, right, over, mat_z), "base0",
        specs=[VMEM, VMEM, HBM, HBM] + [VMEM] * 5,
        scratch=(pltpu.VMEM(FOUR, FP), *pads, pltpu.SemaphoreType.DMA((2,))),
    )
    tent, msg, cleft = call(
        inner_first_kernel,
        [(FOUR, FP), ((PACK_AT + 6 * PACK, NZ), jnp.bfloat16), (FIVE, FP)],
        (par, base, now, g0, inner0, speed, elem, weight, coef, left, right, over, mat_z), "inner0", 1,
        scratch=one_pad,
    )
    outer0 = swap_outer(msg)
    pick_shape = ((2 * NZ, 5 * CAP), jnp.bfloat16)
    pick, spread = call(slots_kernel, [pick_shape, ((5, 5 * NY, CAP), FP)], (elem, weight), "slots")
    row, lane = call(
        stations_kernel, [((3, 2 * SB, 128), FP), ((2 * SB, CAP), FP)],
        (par, pair_blocks, slot_station.reshape(128, CAP)), "stations", 2,
    )
    outer0, pick, spread, row, lane = lax.optimization_barrier((outer0, pick, spread, row, lane))
    u1, msg, outer, coef0, sxl, last0 = call(
        outer_first_kernel,
        [(FOUR, FP), (PLANE, FP), (PLANE, FP), (FIVE, FP), (PLANE, FP), (PLANE, FP)],
        (par, tent, now, g0, outer0, inner0, coef, cleft, left, right, over, mat_z), "outer0", 1,
        scratch=one_pad,
    )

    def base_of(step, u, before):
        return call(
            functools.partial(base_kernel, step), [(FOUR, FP)],
            (wavelet, u, before, src, coef, coef0, mat_z), "base", scratch=pads,
        )[0]

    def two_steps(step, u_b, u_a, msg, outer, fill=(None, None)):
        inner = swap_inner(msg)
        base = base_of(step, u_b, u_a)
        more = None
        if fill[0]:
            inner, base, more = lax.optimization_barrier((inner, base, fill[0]()))
        u_c, g, msg, last = call(
            both_kernel, [(FOUR, FP), (PLANE, FP), (PLANE, FP), (PLANE, FP)],
            (par, base, inner, outer, coef), "both", 1,
        )
        inner = swap_inner(msg)
        base = base_of(step + 1, u_c, u_b)
        if fill[1]:
            inner, base, more = lax.optimization_barrier((inner, base, fill[1](more, u_c, g, last)))
        tent, msg = call(
            inner_kernel, [(FOUR, FP), ((2 * NY, NZ), jnp.bfloat16)],
            (par, base, u_c, g, inner, coef), "inner", 1,
        )
        return u_c, g, last, inner, tent, msg, more

    def complete(tent, u, g, recv, inner):
        return call(
            outer_kernel, [(FOUR, FP), (PLANE, FP), (PLANE, FP), (PLANE, FP)],
            (par, tent, u, g, recv, inner, coef, sxl), "outer", 1,
        )

    u2, g2, last1, inner2, tent, msg, _ = two_steps(1, u1, now, msg, outer)
    recv = swap_outer(msg)
    (rows,) = call(
        sample_first_kernel, [((3, CAP), FP)], (now, last0, u1, last1, u2, pick, spread), "sample3"
    )
    others = call(
        others_kernel, [pick_shape, pick_shape, ((3, 5, NY, CAP), FP)], (par, inner0, outer0), "others", 1
    )
    recv, rows, *others = lax.optimization_barrier((recv, rows, *others))
    u3, msg, outer, last2 = complete(tent, u2, g2, recv, inner2)

    def second_rows():
        return call(
            sample_second_kernel, [((4, CAP), FP)], (rows, last2, u3, pick, spread), "sample5"
        )[0]

    def third_rows(before, u, g, last):
        return call(
            sample_third_kernel, [((8, CAP), FP)],
            (par, before, last, u, g, sxl, pick, spread, *others), "sample8", 1,
        )[0]

    u4, g4, _, inner4, tent, msg, rows = two_steps(3, u3, u2, msg, outer, (second_rows, third_rows))
    pick_l, _, spread_o = others
    (mine,) = call(
        sample_last_kernel, [((devices // 2 * ROWS, CAP), FP)],
        (par, rows, inner4, tent, g4, pick, spread, pick_l, spread_o), "sample7", 1,
        out_specs=[HBM],
        scratch=(
            pltpu.VMEM((8 * ROWS, CAP), FP), pltpu.SemaphoreType.DMA((devices // 16,)),
        ),
    )
    near = lax.all_to_all(
        mine.reshape(devices // 2, 1, ROWS * CAP), ("pair", "chip"), 0, 0, tiled=True
    ).reshape(devices // 2 * ROWS, CAP)
    recv = swap_outer(msg)
    recv, near = lax.optimization_barrier((recv, near))
    gathered = devices // 2 * ROWS
    u5, msg, outer = call(
        outer_last_kernel, [(FOUR, FP), ((gathered + NY, NZ), FP), (PLANE, FP)],
        (par, tent, u4, g4, recv, near, coef, sxl), "outer", 1,
    )
    far = swap_inner(msg)
    base = base_of(5, u5, u4)
    end, cross = call(
        cross_kernel, [(FOUR, FP), ((1, 2, F, SB * SB), jnp.bfloat16)],
        (par, base, outer, coef, near, far, row, lane, table, reps, tiles), "cross", 1,
        out_specs=[HBM, HBM],
        scratch=(
            pltpu.VMEM(FOUR, FP), pltpu.VMEM((2, F, SB * SB), jnp.bfloat16),
            pltpu.SemaphoreType.DMA((5,)),
        ),
    )
    return end, cross


def solution(mesh):
    split = P(AXES)
    in_specs = (
        P(AXES, None, None), P(AXES, None, None), P(AXES, None, None), P(AXES, None, None),
        P(), split, P(), P(None, AXES), P(AXES, None),
    )
    out_specs = (P(AXES, None, None), P(AXES, None, None, None))
    grid = mesh.devices.reshape(mesh.shape["pair"], -1, 2)
    mesh = jax.sharding.Mesh(grid, AXES)
    devices = grid.size
    run = functools.partial(body, devices=devices)
    return jax.shard_map(run, mesh=mesh, in_specs=in_specs, out_specs=out_specs, check_vma=False)
```

```python
import functools
import math

import jax
import jax.numpy as jnp
import numpy as np
from jax import lax
from jax.experimental import pallas as pl
from jax.experimental.pallas import tpu as pltpu
from jax.sharding import PartitionSpec as P

NT = 6
F = 256
SB = 32
STEP_DT = 0.04
NY = 96
NZ = 128
EY = 24
EZ = 32
CAP = 128
AXES = ("pair", "chip", "core")
HIGHEST = lax.Precision.HIGHEST
W1 = np.array([0.1, 49.0 / 90.0, 32.0 / 45.0, 49.0 / 90.0, 0.1])


def stiffness_1d():
    points = np.array([-1.0, -math.sqrt(3.0 / 7.0), 0.0, math.sqrt(3.0 / 7.0), 1.0])
    factor = np.array(
        [np.prod([points[i] - points[j] for j in range(5) if j != i]) for i in range(5)]
    )
    d = np.zeros((5, 5))
    for i in range(5):
        for j in range(5):
            if i != j:
                d[i, j] = factor[i] / (factor[j] * (points[i] - points[j]))
        d[i, i] = -np.sum(d[i])
    return d.T @ np.diag(W1) @ d


A = stiffness_1d()
MX = np.array([0.2, W1[1], W1[2], W1[3], 0.2])
AB = A / MX[:, None]
KAPPA = float(sum(AB[4, k] * AB[k, 4] for k in range(4)))


def f32(x):
    return np.asarray(x, np.float32)


def tables():
    my = np.array([MX[y % 4] for y in range(NY)])
    mz = np.array([0.1 if z == 0 else MX[z % 4] for z in range(NZ)])
    mat_z = np.zeros((NZ, 2 * NZ))
    for z in range(NZ):
        e, c = divmod(z, 4)
        for m in range(5):
            if 4 * e + m < NZ:
                mat_z[4 * e + m, z] += A[c, m]
            if c == 0 and e > 0:
                mat_z[4 * (e - 1) + m, NZ + z] += A[4, m]
    left = np.zeros((3 * NY, EY))
    for y in range(NY):
        e, b = divmod(y, 4)
        left[y, e] += W1[b]
        left[NY + y, e] += 1.0
        if b == 0:
            left[y, (e - 1) % EY] += W1[4]
            left[2 * NY + y, (e - 1) % EY] += 1.0
    left[:NY] /= my[:, None]
    right = np.zeros((EZ, 3 * NZ))
    for z in range(NZ):
        e, c = divmod(z, 4)
        right[e, z] += 1.0
        right[e, 2 * NZ + z] += W1[c]
        if c == 0 and e > 0:
            right[e - 1, NZ + z] += 1.0
            right[e - 1, 2 * NZ + z] += W1[4]
    right[:, 2 * NZ :] /= mz[None, :]
    over_z = np.broadcast_to(1.0 / mz, (8, NZ)) * (STEP_DT * STEP_DT)
    over_y = np.broadcast_to(1.0 / my[:8, None], (8, NZ)) * (STEP_DT * STEP_DT)
    left = np.tile(left, (1, 3)).astype(jnp.bfloat16)
    right = np.tile(right, (3, 1)).astype(jnp.bfloat16)
    high = mat_z.astype(jnp.bfloat16).astype(np.float64)
    low = (mat_z - high).astype(jnp.bfloat16)
    stack = np.concatenate([mat_z, mat_z], 0).astype(jnp.bfloat16)
    return np.concatenate([stack, low], 0), left, right, f32(np.concatenate([over_y, over_z], 0))


PART_PAIRS = ((0, 0), (1, 0), (0, 1), (1, 1), (2, 0), (0, 2))


def parts_of(x, count):
    parts = []
    for _ in range(count):
        part = x.astype(jnp.bfloat16)
        parts.append(part)
        x = x - part.astype(x.dtype)
    return parts


def dft_table():
    angle = np.pi * (np.arange(F) + 0.5) / F
    phase = angle[:, None] * np.arange(NT)[None, :]
    parts = parts_of(f32(np.concatenate([np.cos(phase), -np.sin(phase)], 0)), 3)
    table = np.zeros((2 * F, 128), jnp.bfloat16)
    for group, (_, part) in enumerate(PART_PAIRS):
        table[:, 8 * group : 8 * group + NT] = parts[part]
    return table


def dot(a, b):
    return jnp.dot(a, b, precision=HIGHEST, preferred_element_type=jnp.float32)


VMEM = pl.BlockSpec(memory_space=pltpu.VMEM)
SMEM = pl.BlockSpec(memory_space=pltpu.SMEM)
HBM = pl.BlockSpec(memory_space=pltpu.HBM)


def call(kernel, outs, args, name, smem=0, specs=None, out_specs=None, scratch=(), flops=4_000_000):
    return pl.pallas_call(
        kernel,
        out_shape=[jax.ShapeDtypeStruct(s, d) for s, d in outs],
        in_specs=specs or [SMEM] * smem + [VMEM] * (len(args) - smem),
        out_specs=out_specs or [VMEM] * len(outs),
        scratch_shapes=list(scratch),
        compiler_params=pltpu.CompilerParams(vmem_limit_bytes=24 * 1024 * 1024),
        cost_estimate=pl.CostEstimate(flops=flops, bytes_accessed=1_000_000, transcendentals=0),
        name=name,
    )(*args)


def in_hbm(x):
    return pltpu.with_memory_space_constraint(x, pltpu.HBM)


PACK = 32
ROWS = 9
PACK_AT = 2 * NY + 2 * EY
PLANE = (NY, NZ)
FOUR = (4, NY, NZ)
FIVE = (5, NY, NZ)
FP = jnp.float32


def expand_speed(parts, left, right, over):
    rows = jnp.dot(left, parts, preferred_element_type=jnp.float32)
    parts = jnp.concatenate(parts_of(rows, 3), 1)
    by_z = jnp.dot(parts[:NY], right, preferred_element_type=jnp.float32)
    by_y = jnp.dot(parts[NY:], right[:, 2 * NZ :], preferred_element_type=jnp.float32)
    over_y = jnp.concatenate([over[:8]] * (NY // 8), 0)
    over_z = over[8:9]
    return (
        by_z[:, :NZ] * over_z, by_z[:, NZ : 2 * NZ] * over_z, by_y[:NY] * over_y, by_y[NY:] * over_y,
        by_z[:, 2 * NZ :] * (STEP_DT * STEP_DT),
    )


def speed_parts(speed, count=3):
    return jnp.concatenate(parts_of(speed, count), 0)


def along_z(u, mat_z):
    high, low = parts_of(u, 2)
    return jnp.dot(
        jnp.concatenate([high, low], 1), mat_z[: 2 * NZ], preferred_element_type=jnp.float32
    ) + jnp.dot(high, mat_z[2 * NZ :], preferred_element_type=jnp.float32)


def y_patterns():
    b = lax.broadcasted_iota(jnp.int32, (8, NZ), 0) % 4
    own, before = {}, {}
    for d in range(-4, 5):
        total = jnp.zeros((8, NZ), FP)
        for row in range(4):
            if 0 <= row + d <= 4:
                total = jnp.where(b == row, float(A[row, row + d]), total)
        own[d] = total
        if d <= 0:
            before[d] = jnp.where(b == 0, float(A[4, 4 + d]), 0.0)
    return own, before


def y_coefs(y1, y2, patterns):
    own, before = patterns
    return {d: y1 * own[d] + y2 * before[d] if d in before else y1 * own[d] for d in own}


def wrap_rows(pad, at, plane):
    pad[at, 8 : 8 + NY, :] = plane
    pad[at, 4:8, :] = plane[NY - 4 :]
    pad[at, 8 + NY : 12 + NY, :] = plane[:4]


def along_y(pad, at, row, coefs):
    total = None
    for d, c in coefs.items():
        term = c * pad[at, 8 + row + d : 16 + row + d, :]
        total = term if total is None else total + term
    return total


def to_right(sx, u):
    total = float(AB[4, 0]) * u[0]
    for m in range(1, 4):
        total = total + float(AB[4, m]) * u[m]
    return sx * total


def start_kernel(
    par, now_in, speed_in, left_in, right_in, over_in, mat_in, elem_in, weight_in, wave_in,
    now, speed, left, right, over, mat, elem, weight, wave, msg_ref, sems,
):
    pairs = (
        (now_in, now), (speed_in.at[0], speed), (elem_in, elem), (weight_in, weight), (left_in, left),
        (right_in, right), (over_in, over), (mat_in, mat), (wave_in, wave),
    )
    copies = [pltpu.make_async_copy(a, b, sems.at[i]) for i, (a, b) in enumerate(pairs)]
    for copy in copies:
        copy.start()
    msg_ref[NY:] = jnp.zeros((EY + PACK, NZ), FP)
    copies[0].wait()
    msg_ref[:NY] = jnp.where(par[0] == 1, now[0], to_right(1.0, [now[k] for k in range(4)]))
    for copy in copies[1:4]:
        copy.wait()
    msg_ref[NY : NY + EY, :EZ] = speed[...]
    msg_ref[NY + EY : NY + EY + 25] = weight[100:125]
    msg_ref[NY + EY + PACK - 1 :] = elem[...].astype(FP)
    for copy in copies[4:]:
        copy.wait()


def base_first_kernel(
    wave, now, vel_in, src_in, speed, left, right, over, mat_z,
    out, src, coef_ref, first_ref, vel, pad, sems,
):
    copies = [
        pltpu.make_async_copy(vel_in, vel, sems.at[0]), pltpu.make_async_copy(src_in, src, sems.at[1])
    ]
    for copy in copies:
        copy.start()
    coefs = expand_speed(speed_parts(speed[...]), left[...], right[...], over[...])
    for i in range(5):
        coef_ref[i] = coefs[i]
    first_ref[...] = to_right(coefs[4], [now[k] for k in range(4)])
    base_body(0, wave, now, None, None, coef_ref, None, mat_z, out, pad)
    for copy in copies:
        copy.wait()
    scale = jnp.broadcast_to(wave[:, 0:1] * (STEP_DT * STEP_DT), PLANE)
    for k in range(4):
        out[k] = out[k] + STEP_DT * vel[k] + scale * src[k]


def base_body(step, wave, now, prev, src, coef, coef0, mat_z, out, pad):
    scale = jnp.broadcast_to(wave[:, step : step + 1] * (STEP_DT * STEP_DT), (8, NZ))
    by_z = along_z(now[...].reshape(4 * NY, NZ), mat_z)
    patterns = y_patterns()
    for k in range(4):
        wrap_rows(pad, k, now[k])
    for row in range(0, NY, 8):
        at = slice(row, row + 8)
        u = [now[k, at, :] for k in range(4)]
        sx = coef[4, at, :]
        own = [coef[i, at, :] for i in range(4)]
        first = own if coef0 is None else [coef0[i, at, :] for i in range(4)]
        cy = y_coefs(own[2], own[3], patterns)
        cy0 = cy if coef0 is None else y_coefs(first[2], first[3], patterns)
        for k in range(4):
            c = own if k else first
            z = by_z[NY * k + row : NY * k + row + 8]
            force = c[0] * z[:, :NZ] + c[1] * z[:, NZ:] + along_y(pad, k, row, cy if k else cy0)
            if k == 0:
                force = 0.5 * force if coef0 is None else force + coef0[4, at, :] * u[0]
            mix = float(AB[k, 0]) * u[0]
            for m in range(1, 4):
                mix = mix + float(AB[k, m]) * u[m]
            force = force + sx * mix
            if prev is None:
                out[k, at, :] = u[k] - force
            else:
                out[k, at, :] = 2.0 * u[k] - prev[k, at, :] + (scale * src[k, at, :] - force)


def base_kernel(step, wave, now, prev, src, coef, coef0, mat_z, out, pad):
    base_body(step, wave, now, prev, src, coef, coef0, mat_z, out, pad)


def half_left(plane, coefs, mat_z, pad):
    by_z = along_z(plane, mat_z)
    wrap_rows(pad, 0, plane)
    patterns = y_patterns()
    tiles = []
    for row in range(0, NY, 8):
        c = [x[row : row + 8] for x in coefs]
        by_y = along_y(pad, 0, row, y_coefs(c[2], c[3], patterns))
        z = by_z[row : row + 8]
        tiles.append(0.5 * (c[0] * z[:, :NZ] + c[1] * z[:, NZ:] + by_y))
    return jnp.concatenate(tiles, 0) + float(AB[4, 4]) * (coefs[4] * plane)


def inner_first_kernel(
    par, base, now, first, recv, speed, elem, weight, coef, left, right, over, mat_z,
    tent_ref, msg_ref, cleft_ref, pad,
):
    odd = par[0] == 1
    their_speed = jnp.where(odd, recv[NY : NY + EY, :EZ], 0.0)
    coefs = expand_speed(speed_parts(their_speed), left[...], right[...], over[...])
    for i in range(5):
        cleft_ref[i] = coefs[i]
    share = half_left(now[0], coefs, mat_z, pad)
    inner = jnp.where(odd, coefs[4] * recv[:NY], recv[:NY])
    inner_finish(odd, base, now, first[...], inner, coef[4], share, tent_ref, msg_ref)
    own_speed = jnp.concatenate([speed[...], jnp.zeros((EY, NZ - EZ), FP)], 1)
    msg_ref[2 * NY : PACK_AT] = speed_parts(own_speed, 2)
    pulled = -float(AB[0, 4]) * weight[:25]
    for k in range(1, 4):
        pulled = pulled - float(AB[k, 4]) * weight[25 * k : 25 * k + 25]
    slots = elem[...].astype(FP)
    theirs = recv[NY + EY :]
    packages = (
        (jnp.where(odd, weight[100:125], weight[:25]), slots),
        (pulled, slots),
        (theirs[:25], theirs[PACK - 1 :]),
    )
    for group, (rows, slots) in enumerate(packages):
        eights = jnp.floor(slots * 0.125)
        package = [rows, jnp.zeros((PACK - 27, CAP), FP), eights, slots - 8.0 * eights]
        at = PACK_AT + 2 * PACK * group
        msg_ref[at : at + 2 * PACK] = jnp.concatenate(parts_of(jnp.concatenate(package, 0), 2), 0)


def inner_finish(odd, base, now, g_now, inner, sx, share, tent_ref, msg_ref):
    even_part = jnp.where(odd, 0.0, sx * inner)
    tent = []
    for k in range(4):
        value = base[k] - float(AB[k, 4]) * even_part
        if k == 0:
            value = value - jnp.where(odd, inner, 0.0)
            if share is not None:
                value = value - share
        tent_ref[k] = value
        tent.append(value)
    msg_ref[:NY] = jnp.where(odd, g_now, now[0]).astype(jnp.bfloat16)
    msg_ref[NY : 2 * NY] = jnp.where(odd, to_right(sx, tent), tent[0]).astype(jnp.bfloat16)


def inner_kernel(par, base, now, g_now, recv, coef, tent_ref, msg_ref):
    odd = par[0] == 1
    inner_finish(odd, base, now, g_now[...], recv[...], coef[4], None, tent_ref, msg_ref)


def outer_finish(odd, tent, sx, sx_left, recv0, recv1, g_own, u0_own, share, refs):
    u_ref, msg_ref, outer_ref = refs
    odd_part = jnp.where(odd, sx * recv0, 0.0)
    values = []
    for k in range(4):
        value = tent[k] - float(AB[k, 4]) * odd_part
        if k == 0:
            lost = recv0 if share is None else recv0 + share
            value = value - jnp.where(odd, 0.0, lost)
        u_ref[k] = value
        values.append(value)
    msg_ref[...] = jnp.where(odd, values[0], to_right(sx, values))
    mine = g_own if share is None else g_own + share
    outer_ref[...] = recv1 - jnp.where(odd, mine, KAPPA * sx_left * sx_left * u0_own)


def outer_first_kernel(
    par, tent, now, first, recv, inner, coef, cleft, left, right, over, mat_z,
    u_ref, msg_ref, outer_ref, coef0_ref, sxl_ref, last_ref, pad,
):
    odd = par[0] == 1
    parts = jnp.concatenate([recv[2 * NY : PACK_AT, :EZ], jnp.zeros((EY, EZ), jnp.bfloat16)], 0)
    theirs = expand_speed(parts, left[...], right[...], over[...])
    coefs = [jnp.where(odd, coef[i], theirs[i]) for i in range(5)]
    recv0 = recv[:NY].astype(FP)
    plane = jnp.where(odd, recv0, now[0])
    share = half_left(plane, coefs, mat_z, pad)
    on_left = [jnp.where(odd, cleft[i], theirs[i]) for i in range(5)]
    for i in range(4):
        coef0_ref[i] = 0.5 * (coef[i] + on_left[i])
    coef0_ref[4] = float(AB[4, 4]) * on_left[4]
    sxl_ref[...] = on_left[4]
    last_ref[...] = jnp.where(odd, recv0, inner[:NY])
    outer_finish(
        odd, tent, coef[4], on_left[4], recv0, recv[NY : 2 * NY].astype(FP), first[...], now[0], share,
        (u_ref, msg_ref, outer_ref),
    )


def outer_kernel(par, tent, now, g_now, recv, inner, coef, sxl, u_ref, msg_ref, outer_ref, last_ref):
    odd = par[0] == 1
    recv0 = recv[:NY].astype(FP)
    last_ref[...] = jnp.where(odd, recv0, inner[...])
    outer_finish(
        odd, tent, coef[4], sxl[...], recv0, recv[NY:].astype(FP), g_now[...], now[0], None,
        (u_ref, msg_ref, outer_ref),
    )


def both_kernel(par, base, inner, outer, coef, u_ref, g_ref, msg_ref, last_ref):
    odd = par[0] == 1
    last = jnp.where(odd, outer[...], inner[...])
    from_left = jnp.where(odd, inner[...], outer[...])
    sx = coef[4]
    pull = sx * last
    values = []
    for k in range(4):
        value = base[k] - float(AB[k, 4]) * pull
        if k == 0:
            value = value - from_left
        u_ref[k] = value
        values.append(value)
    g = to_right(sx, values)
    g_ref[...] = g
    msg_ref[...] = jnp.where(odd, values[0], g)
    last_ref[...] = last


def outer_last_kernel(par, tent, now, g_now, recv, inner, coef, sxl, u_ref, msg_ref, outer_ref):
    outer_finish(
        par[0] == 1, tent, coef[4], sxl[...], recv[:NY].astype(FP), recv[NY:].astype(FP), g_now[...],
        now[0], None,
        (u_ref, msg_ref, outer_ref),
    )


def pick_nodes(ez, pick_ref):
    z = lax.broadcasted_iota(jnp.int32, (NZ, CAP), 0)
    for c in range(5):
        hot = (z == 4 * ez + c).astype(FP).astype(jnp.bfloat16)
        for half in range(2):
            pick_ref[half * NZ : (half + 1) * NZ, c * CAP : (c + 1) * CAP] = hot


def y_masks(ey):
    y = lax.broadcasted_iota(jnp.int32, (NY, CAP), 0)
    masks = []
    for b in range(5):
        row = 4 * ey + b
        masks.append(y == jnp.where(row >= NY, row - NY, row))
    return masks


def spread_nodes(masks, weight, c):
    total = jnp.zeros((NY, CAP), FP)
    for b in range(5):
        total = jnp.where(masks[b], weight[5 * b + c : 5 * b + c + 1, :], total)
    return total


def slots_kernel(elem, weight, pick_ref, spread_ref):
    ey = elem[...] // EZ
    pick_nodes(elem[...] - ey * EZ, pick_ref)
    masks = y_masks(ey)
    for a in range(5):
        plane = weight[25 * a : 25 * a + 25, :]
        for c in range(5):
            spread_ref[c, a * NY : (a + 1) * NY, :] = spread_nodes(masks, plane, c)


def others_kernel(par, inner, outer, pick_l_ref, pick_2_ref, spread_ref):
    odd = par[0] == 1
    from_inner = inner[NY + EY :]
    halves = [
        outer[PACK_AT + PACK * i : PACK_AT + PACK * (i + 1)].astype(FP) for i in range(6)
    ]
    from_outer, pulled, relayed = (halves[2 * i] + halves[2 * i + 1] for i in range(3))
    pulled = jnp.where(odd, 0.0, pulled)

    def number(package):
        return 8.0 * package[PACK - 2 : PACK - 1] + package[PACK - 1 :]

    groups = (
        (
            jnp.where(odd, from_inner[:25], from_outer[:25]),
            jnp.where(odd, from_inner[PACK - 1 :], number(from_outer)),
            pick_l_ref,
        ),
        (
            jnp.where(odd, from_outer[:25], relayed[:25]),
            jnp.where(odd, number(from_outer), number(relayed)),
            pick_2_ref,
        ),
    )
    for group, (rows, elem, pick_ref) in enumerate(groups):
        elem = elem.astype(jnp.int32)
        ey = elem // EZ
        pick_nodes(elem - ey * EZ, pick_ref)
        masks = y_masks(ey)
        for c in range(5):
            spread_ref[2 * group, c] = spread_nodes(masks, rows, c)
            if group == 0:
                spread_ref[1, c] = spread_nodes(masks, pulled, c)


def picked(planes, pick):
    high, low = parts_of(jnp.concatenate(planes, 0), 2)
    return jnp.dot(
        jnp.concatenate([high, low], 1), pick[...], preferred_element_type=jnp.float32
    )


def weighted(got, spread):
    total = None
    for c in range(5):
        term = got[:, c * CAP : (c + 1) * CAP] * spread(c)
        total = term if total is None else total + term
    return jnp.sum(jnp.sum(total.reshape(-1, 8, CAP), 0), 0, keepdims=True)


def sample(planes, pick, spread):
    rows = NY * len(planes)
    return weighted(picked(planes, pick), lambda c: spread[c, :rows, :])


def all_planes(u, last):
    return [u[0], u[1], u[2], u[3], last]


def sample_first_kernel(u0, l0, u1, l1, u2, pick, spread, out):
    out[0:1, :] = sample(all_planes(u0, l0[...]), pick, spread)
    out[1:2, :] = sample(all_planes(u1, l1[...]), pick, spread)
    out[2:3, :] = sample([u2[k] for k in range(4)], pick, spread)


def sample_second_kernel(first, l2, u3, pick, spread, out):
    got = picked(all_planes(u3, l2[...]), pick)
    rest = 4 * NY
    out[0:2, :] = first[0:2, :]
    out[2:3, :] = first[2:3, :] + weighted(got[rest:], lambda c: spread[c, rest:, :])
    out[3:4, :] = weighted(got[:rest], lambda c: spread[c, :rest, :])


def sample_third_kernel(
    par, before, l3, u4, g, sxl, pick, spread, pick_l, pick_2, spread_o, out
):
    odd = par[0] == 1
    got = picked(all_planes(u4, l3[...]), pick)
    rest = 4 * NY
    face = u4[0]
    x = sxl[...] * face
    left = picked([x, face], pick_l)
    second = picked([jnp.where(odd, -g[...], -float(AB[0, 4]) * x)], pick_2)
    out[0:3, :] = before[0:3, :]
    out[3:4, :] = before[3:4, :] + weighted(got[rest:], lambda c: spread[c, rest:, :])
    out[4:5, :] = weighted(got[:rest], lambda c: spread[c, :rest, :])
    out[5:6, :] = weighted(left[:NY], lambda c: spread_o[1, c])
    out[6:7, :] = weighted(second, lambda c: spread_o[2, c])
    out[7:8, :] = jnp.where(odd, 0.0, weighted(left[NY:], lambda c: spread_o[0, c]))


def sample_last_kernel(
    par, before, inner, tent, g, pick, spread, pick_l, spread_o, out, block, sems
):
    odd = par[0] == 1
    own_g = jnp.where(odd, -g[...], 0.0)
    last = jnp.where(odd, 0.0, inner[...])
    got = picked(all_planes(tent, own_g) + [last], pick)
    face = picked([tent[0]], pick_l)
    rest = 4 * NY
    rows = [
        before[0:4, :],
        before[4:5, :] + weighted(got[5 * NY :], lambda c: spread[c, rest:, :]),
        weighted(got[: 5 * NY], lambda c: spread[c]),
        before[5:6, :] + weighted(face, lambda c: spread_o[0, c]),
        before[6:8, :],
    ]
    rows = jnp.concatenate(rows, 0)
    for i in range(8):
        block[ROWS * i : ROWS * (i + 1), :] = rows
    size = 8 * ROWS
    copies = [
        pltpu.make_async_copy(block, out.at[pl.ds(size * i, size), :], sems.at[i])
        for i in range(out.shape[0] // size)
    ]
    for copy in copies:
        copy.start()
    for copy in copies:
        copy.wait()


def stations_kernel(par, blocks, stations, row_ref, lane_ref):
    odd = par[0] == 1
    for j in range(2 * SB):
        wanted = blocks[0, j // SB] * SB + j % SB
        hit = jnp.zeros((8, CAP), FP)
        for r in range(16):
            hit = hit + jnp.where(stations[8 * r : 8 * r + 8, :] == wanted, 1.0, 0.0)
        lane_ref[j : j + 1, :] = jnp.sum(hit, 0, keepdims=True)
    lane = lane_ref[...]
    ids = stations[...].astype(FP)
    at = lax.dot_general(
        lane, ids, (((1,), (1,)), ((), ())), precision=HIGHEST, preferred_element_type=jnp.float32
    )
    j = lax.broadcasted_iota(jnp.int32, (2 * SB, 128), 0)
    wanted = jnp.where(j < SB, blocks[0, 0] * SB + j, blocks[0, 1] * SB + (j - SB))
    place = lax.broadcasted_iota(jnp.int32, (2 * SB, 128), 1)
    hit = jnp.where(jnp.abs(at - wanted.astype(FP)) < 0.5, place.astype(FP), 0.0)
    device = jnp.sum(hit, 1, keepdims=True).astype(jnp.int32)
    first = jnp.where(odd, 1, 0)

    def one_hot(device):
        device = jnp.bitwise_and(device, 127)
        side = jnp.where(jnp.bitwise_and(device, 1) == first, 0, 64)
        return jnp.where(place == side + jnp.right_shift(device, 1), 1.0, 0.0)

    row_ref[0] = one_hot(device)
    row_ref[1] = one_hot(device + 1)
    even = jnp.where(jnp.bitwise_and(device, 1) == 0, 1.0, 0.0)
    row_ref[2] = even * (one_hot(device + 2) + one_hot(device + 127))


def station_spectra(near, far, row, lane, table):
    slabs = [
        jnp.concatenate([half[pl.ds(t, 64, stride=ROWS), :] for half in (near, far)], 0)
        for t in range(ROWS)
    ]

    def select(which, slabs):
        hot = row[which].astype(jnp.bfloat16)
        parts = jnp.concatenate(parts_of(jnp.concatenate(slabs, 1), 2), 0)
        return jnp.dot(
            jnp.concatenate([hot, hot], 1), parts, preferred_element_type=jnp.float32
        )

    found = select(0, slabs[:6])
    more = select(1, [slabs[8], slabs[6]])
    last = select(2, [slabs[7]])
    found = [found[:, 128 * t : 128 * (t + 1)] for t in range(NT)]
    found[4] = found[4] + more[:, :128]
    found[5] = found[5] + more[:, 128:] + last
    at = lax.broadcasted_iota(jnp.int32, (2 * SB, 128), 1)
    samples = jnp.zeros((2 * SB, 128), FP)
    for t in range(NT):
        one = jnp.sum(found[t] * lane[...], 1, keepdims=True)
        samples = jnp.where(at % 8 == t, one, samples)
    parts = [part.astype(FP) for part in parts_of(samples, 3)]
    mixed = jnp.zeros((2 * SB, 128), FP)
    for group, (part, _) in enumerate(PART_PAIRS):
        mixed = jnp.where(at // 8 == group, parts[part], mixed)
    return lax.dot_general(
        table[...], mixed.astype(jnp.bfloat16), (((1,), (1,)), ((), ())),
        preferred_element_type=jnp.float32,
    ).astype(jnp.bfloat16)


def cross_kernel(
    par, base, inner, outer, coef, near, far, row, lane, table, spread_a, spread_b,
    end, out, held_end, held, sems,
):
    odd = par[0] == 1
    pull = coef[4] * jnp.where(odd, outer[...], inner[...])
    for k in range(4):
        value = base[k] - float(AB[k, 4]) * pull
        held_end[k] = value - jnp.where(odd, inner[...], outer[...]) if k == 0 else value
    copies = [pltpu.make_async_copy(held_end, end, sems.at[4])]
    copies[0].start()
    spectra = station_spectra(near, far, row, lane, table)
    second = jnp.dot(spectra, spread_b[...], preferred_element_type=jnp.float32) * (1.0 / NT)
    b_re = second[:F]
    b_im = second[F:]
    size = F // 4
    for i in range(4):
        rows = slice(size * i, size * (i + 1))
        first = jnp.dot(
            jnp.concatenate([spectra[rows], spectra[F + size * i : F + size * (i + 1)]], 0), spread_a[...],
            preferred_element_type=jnp.float32,
        )
        for at in range(0, SB * SB, 128):
            a_re = first[:size, at : at + 128]
            a_im = first[size:, at : at + 128]
            held[0, rows, at : at + 128] = (a_re * b_re[rows] + a_im * b_im[rows]).astype(jnp.bfloat16)
            held[1, rows, at : at + 128] = (a_im * b_re[rows] - a_re * b_im[rows]).astype(jnp.bfloat16)
        copy = pltpu.make_async_copy(held.at[:, rows, :], out.at[0, :, rows, :], sems.at[i])
        copy.start()
        copies.append(copy)
    for copy in copies:
        copy.wait()


def body(
    now, vel, speed_sq, src, wavelet, slot_elem, slot_station, slot_weight, pair_blocks, devices
):
    inner_route = [(i, i ^ 1) for i in range(devices)]
    outer_route = [(i, (i + 1 if i % 2 else i - 1) % devices) for i in range(devices)]

    def swap_inner(x):
        return lax.ppermute(x, AXES, inner_route)

    def swap_outer(x):
        return lax.ppermute(x, AXES, outer_route)

    mat_z, left, right, over = (jnp.asarray(x) for x in tables())
    table = jnp.asarray(dft_table())
    reps = np.zeros((2 * SB, SB * SB))
    for i in range(SB):
        reps[i, i * SB : (i + 1) * SB] = 1.0
    tiles = np.zeros((2 * SB, 128))
    for i in range(128):
        tiles[SB + i % SB, i] = 1.0
    reps = jnp.asarray(reps, jnp.bfloat16)
    tiles = jnp.asarray(tiles, jnp.bfloat16)
    pads = (pltpu.VMEM((4, NY + 16, NZ), FP),)
    one_pad = (pltpu.VMEM((1, NY + 16, NZ), FP),)

    par = lax.axis_index("core").astype(jnp.int32).reshape(1)

    inputs = (
        now, speed_sq, left, right, over, mat_z, slot_elem.reshape(1, CAP), slot_weight,
        wavelet.reshape(1, NT),
    )
    kept = [jax.ShapeDtypeStruct(x.shape, x.dtype) for x in inputs]
    kept[1] = jax.ShapeDtypeStruct((EY, EZ), FP)
    now, speed, left, right, over, mat_z, elem, weight, wavelet, msg = call(
        start_kernel,
        [(x.shape, x.dtype) for x in kept] + [((NY + EY + PACK, NZ), FP)],
        (par, *(in_hbm(x) for x in inputs)), "start",
        specs=[SMEM] + [HBM] * len(inputs), scratch=(pltpu.SemaphoreType.DMA((len(inputs),)),),
    )
    inner0 = swap_inner(msg)
    base, src, coef, g0 = call(
        base_first_kernel, [(FOUR, FP), (FOUR, FP), (FIVE, FP), (PLANE, FP)],
        (wavelet, now, in_hbm(vel), in_hbm(src), speed, left, right, over, mat_z), "base0",
        specs=[VMEM, VMEM, HBM, HBM] + [VMEM] * 5,
        scratch=(pltpu.VMEM(FOUR, FP), *pads, pltpu.SemaphoreType.DMA((2,))),
    )
    tent, msg, cleft = call(
        inner_first_kernel,
        [(FOUR, FP), ((PACK_AT + 6 * PACK, NZ), jnp.bfloat16), (FIVE, FP)],
        (par, base, now, g0, inner0, speed, elem, weight, coef, left, right, over, mat_z), "inner0", 1,
        scratch=one_pad,
    )
    outer0 = swap_outer(msg)
    pick_shape = ((2 * NZ, 5 * CAP), jnp.bfloat16)
    pick, spread = call(slots_kernel, [pick_shape, ((5, 5 * NY, CAP), FP)], (elem, weight), "slots")
    row, lane = call(
        stations_kernel, [((3, 2 * SB, 128), FP), ((2 * SB, CAP), FP)],
        (par, pair_blocks, slot_station.reshape(128, CAP)), "stations", 2,
    )
    outer0, pick, spread, row, lane = lax.optimization_barrier((outer0, pick, spread, row, lane))
    u1, msg, outer, coef0, sxl, last0 = call(
        outer_first_kernel,
        [(FOUR, FP), (PLANE, FP), (PLANE, FP), (FIVE, FP), (PLANE, FP), (PLANE, FP)],
        (par, tent, now, g0, outer0, inner0, coef, cleft, left, right, over, mat_z), "outer0", 1,
        scratch=one_pad,
    )

    def base_of(step, u, before):
        return call(
            functools.partial(base_kernel, step), [(FOUR, FP)],
            (wavelet, u, before, src, coef, coef0, mat_z), "base", scratch=pads,
        )[0]

    def two_steps(step, u_b, u_a, msg, outer, fill=(None, None)):
        inner = swap_inner(msg)
        base = base_of(step, u_b, u_a)
        more = None
        if fill[0]:
            inner, base, more = lax.optimization_barrier((inner, base, fill[0]()))
        u_c, g, msg, last = call(
            both_kernel, [(FOUR, FP), (PLANE, FP), (PLANE, FP), (PLANE, FP)],
            (par, base, inner, outer, coef), "both", 1,
        )
        inner = swap_inner(msg)
        base = base_of(step + 1, u_c, u_b)
        if fill[1]:
            inner, base, more = lax.optimization_barrier((inner, base, fill[1](more, u_c, g, last)))
        tent, msg = call(
            inner_kernel, [(FOUR, FP), ((2 * NY, NZ), jnp.bfloat16)],
            (par, base, u_c, g, inner, coef), "inner", 1,
        )
        return u_c, g, last, inner, tent, msg, more

    def complete(tent, u, g, recv, inner):
        return call(
            outer_kernel, [(FOUR, FP), (PLANE, FP), (PLANE, FP), (PLANE, FP)],
            (par, tent, u, g, recv, inner, coef, sxl), "outer", 1,
        )

    u2, g2, last1, inner2, tent, msg, _ = two_steps(1, u1, now, msg, outer)
    recv = swap_outer(msg)
    (rows,) = call(
        sample_first_kernel, [((3, CAP), FP)], (now, last0, u1, last1, u2, pick, spread), "sample3"
    )
    others = call(
        others_kernel, [pick_shape, pick_shape, ((3, 5, NY, CAP), FP)], (par, inner0, outer0), "others", 1
    )
    recv, rows, *others = lax.optimization_barrier((recv, rows, *others))
    u3, msg, outer, last2 = complete(tent, u2, g2, recv, inner2)

    def second_rows():
        return call(
            sample_second_kernel, [((4, CAP), FP)], (rows, last2, u3, pick, spread), "sample5"
        )[0]

    def third_rows(before, u, g, last):
        return call(
            sample_third_kernel, [((8, CAP), FP)],
            (par, before, last, u, g, sxl, pick, spread, *others), "sample8", 1,
        )[0]

    u4, g4, _, inner4, tent, msg, rows = two_steps(3, u3, u2, msg, outer, (second_rows, third_rows))
    pick_l, _, spread_o = others
    (mine,) = call(
        sample_last_kernel, [((devices // 2 * ROWS, CAP), FP)],
        (par, rows, inner4, tent, g4, pick, spread, pick_l, spread_o), "sample7", 1,
        out_specs=[HBM],
        scratch=(
            pltpu.VMEM((8 * ROWS, CAP), FP), pltpu.SemaphoreType.DMA((devices // 16,)),
        ),
    )
    near = lax.all_to_all(
        mine.reshape(devices // 2, 1, ROWS * CAP), ("pair", "chip"), 0, 0, tiled=True
    ).reshape(devices // 2 * ROWS, CAP)
    recv = swap_outer(msg)
    recv, near = lax.optimization_barrier((recv, near))
    far = swap_inner(near)
    u5, msg, outer = call(
        outer_last_kernel, [(FOUR, FP), (PLANE, FP), (PLANE, FP)],
        (par, tent, u4, g4, recv, inner4, coef, sxl), "outer", 1,
    )
    inner = swap_inner(msg)
    base = base_of(5, u5, u4)
    end, cross = call(
        cross_kernel, [(FOUR, FP), ((1, 2, F, SB * SB), jnp.bfloat16)],
        (par, base, inner, outer, coef, near, far, row, lane, table, reps, tiles), "cross", 1,
        out_specs=[HBM, HBM],
        scratch=(
            pltpu.VMEM(FOUR, FP), pltpu.VMEM((2, F, SB * SB), jnp.bfloat16),
            pltpu.SemaphoreType.DMA((5,)),
        ),
    )
    return end, cross


def solution(mesh):
    split = P(AXES)
    in_specs = (
        P(AXES, None, None), P(AXES, None, None), P(AXES, None, None), P(AXES, None, None),
        P(), split, P(), P(None, AXES), P(AXES, None),
    )
    out_specs = (P(AXES, None, None), P(AXES, None, None, None))
    grid = mesh.devices.reshape(mesh.shape["pair"], -1, 2)
    mesh = jax.sharding.Mesh(grid, AXES)
    devices = grid.size
    run = functools.partial(body, devices=devices)
    return jax.shard_map(run, mesh=mesh, in_specs=in_specs, out_specs=out_specs, check_vma=False)
```
